32 devices in a mesh: tm: 4 (over y, x), vox: 8 (over z, core).
Axes of the slice: x: 2, y: 2, z: 4, core: 2. Of those that a mesh axis runs over, the one named last changes fastest.
Arguments:
- u_train: bfloat16 [3072, 4096], P('tm'), may hold values from -0.109375 to 0.109375
- y_train: bfloat16 [3072, 3072], P('tm', 'vox'), may hold values from -6 to 6
- sing: float32 [4096], replicated, may hold values from 0.5 to 8
- lambdas: float32 [20], replicated, may hold values from 0.1 to 100
- lam_index: int32 [24], P('vox'), may hold values from 0 to 19
- live: int32 [24], P('vox'), may hold values from 0 to 1, as said below
- v_basis: bfloat16 [4096, 4096], P('tm', 'vox'), may hold values from -0.09375 to 0.09375
- x_test: bfloat16 [1024, 4096], P(None, 'tm'), may hold values from -0.09375 to 0.09375
Outputs:
- weights: bfloat16 [4096, 3072], P('tm', 'vox')
- predictions: bfloat16 [1024, 3072], P('tm', 'vox')
The draws below stay inside these ranges and needn't reach their ends.
Inputs may be any that keep to these rules, and one draw needn't show every extreme that they name: Of the 3 voxel blocks that one device along vox holds, at most 2 are live, and some device holds exactly 2.
All inputs are finite; a program needn't handle non-finite values.
Results may differ from the reference program's by a relative error of at most 0.0058.
Values may be sent and summed in bfloat16 or wider, within the bound.
A program may use at most 128 MiB of HBM per device.

```python
import math
import jax
import jax.numpy as jnp

F = 4096
NLAM = 20
BLK = 128
VD = 384
TEST = 1024
TR = 3072
VOX = 3072
NBLK = 24


def draw_live(key, part):
    block_count = VD // BLK
    device_count = NBLK // block_count
    capacity = block_count - block_count // 3
    first_key = jax.random.fold_in(key, 11)
    second_key = jax.random.fold_in(key, 12)
    third_key = jax.random.fold_in(key, 13)
    counts = jax.random.randint(first_key, (device_count,), 1, capacity + 1)
    fullest = jax.random.randint(second_key, (), 0, device_count)
    counts = jnp.where(jnp.arange(device_count) == fullest, capacity, counts)
    scores = jax.random.randint(third_key, (device_count, block_count), 0, 1 << 20)
    scores = scores * block_count + jnp.arange(block_count)[None, :]
    ranking = jnp.argsort(jnp.argsort(scores, axis=1), axis=1)
    marked = (ranking < counts[:, None]).astype(jnp.int32)
    return marked.reshape(NBLK)


def plant(values, rng, least, top_value):
    extent = values.shape
    place = [jax.random.randint(jax.random.fold_in(rng, axis), (), 0, extent[axis]) for axis in range(len(extent))]
    values = values.at[tuple(place)].set(least)
    longest = extent.index(max(extent))
    place[longest] = (place[longest] + 1) % extent[longest]
    return values.at[tuple(place)].set(top_value)


def block_levels(key, extent, cuts, low, top_value):
    gain = 1.0
    for position, shards_of in cuts:
        steps = jax.random.uniform(jax.random.fold_in(jax.random.fold_in(key, 6), position), (shards_of,), jnp.float32, low / len(cuts), top_value / len(cuts))
        gain = gain * jnp.repeat(jnp.exp(steps), extent[position] // shards_of).reshape((-1,) + (1,) * (len(extent) - 1 - position))
    return gain


def centred(stream_key, dims, deviation, bound, cuts=(), kind=jnp.bfloat16):
    result = deviation * jax.random.normal(stream_key, dims, jnp.float32)
    if cuts:
        result = result * block_levels(stream_key, dims, cuts, -0.22, 0.18)
    return jnp.clip(result, -bound, bound).astype(kind)


def setup_inputs(seed: int = 0) -> dict:
    key_list = jax.random.split(jax.random.key(seed), 9)
    u_train = centred(key_list[0], (TR, F), TR ** -0.5, 0.109375, ((0, 4),))
    y_train = centred(key_list[1], (TR, VOX), 1.0, 6.0, ((0, 4), (1, 8)))
    sing = jnp.clip(jnp.exp(jax.random.uniform(key_list[2], (F,), jnp.float32, math.log(0.5), math.log(8.0))), 0.5, 8.0)
    lambdas = jnp.clip(jnp.exp(jax.random.uniform(key_list[3], (NLAM,), jnp.float32, math.log(0.1), math.log(100.0))), 0.1, 100.0)
    lam_index = plant(jax.random.randint(key_list[4], (NBLK,), 0, NLAM), jax.random.fold_in(key_list[4], 1), 0, NLAM - 1).astype(jnp.int32)
    live = draw_live(jax.random.fold_in(key_list[8], 71), 0)
    v_basis = centred(key_list[6], (F, F), F ** -0.5, 0.09375, ((0, 4), (1, 8)))
    x_test = centred(key_list[7], (TEST, F), F ** -0.5, 0.09375, ((1, 4),))
    return dict(u_train=u_train, y_train=y_train, sing=sing, lambdas=lambdas, lam_index=lam_index, live=live, v_basis=v_basis, x_test=x_test)


def reference(u_train, y_train, sing, lambdas, lam_index, live, v_basis, x_test):
    filters = sing[None, :] / (sing[None, :] * sing[None, :] + lambdas[:, None])
    products = jnp.dot(u_train.T, y_train, preferred_element_type=jnp.float32)
    chosen = filters[lam_index] * live[:, None].astype(jnp.float32)
    blocks = products.reshape(F, NBLK, BLK) * chosen.T[:, :, None]
    filtered = blocks.reshape(F, VOX).astype(jnp.bfloat16)
    weights = jnp.dot(v_basis, filtered, preferred_element_type=jnp.float32).astype(jnp.bfloat16)
    predictions = jnp.dot(x_test, weights, preferred_element_type=jnp.float32).astype(jnp.bfloat16)
    return weights, predictions
```

```python
import functools

import jax
import jax.numpy as jnp
from jax import lax
from jax.experimental import pallas as pl
from jax.experimental.pallas import tpu as pltpu
from jax.sharding import PartitionSpec as P

BLK = 128
CHUNKS = 4
TILE = 256
MESH = pl.DeviceIdType.MESH


def one_hot(live_ref, cap):
    blocks = live_ref.shape[0]
    live = [live_ref[i] for i in range(blocks)]
    before = [sum(live[:i], jnp.int32(0)) for i in range(blocks)]
    return [
        [jnp.where(before[i] == j, live[i], 0).astype(jnp.float32) for i in range(blocks)]
        for j in range(cap)
    ]


def expand(cap, live_ref, w_in, pred_in, w_ref, pred_ref):
    pick = one_hot(live_ref, cap)
    for source, target in ((w_in, w_ref), (pred_in, pred_ref)):
        values = [source[:, j * BLK : (j + 1) * BLK].astype(jnp.float32) for j in range(cap)]
        for i in range(live_ref.shape[0]):
            block = sum(pick[j][i] * values[j] for j in range(cap))
            target[:, i * BLK : (i + 1) * BLK] = block.astype(target.dtype)


def kernel(
    n_t,
    n_v,
    cap,
    live_ref,
    index_ref,
    lambda_ref,
    sing_ref,
    y_ref,
    u_ref,
    v_ref,
    x_ref,
    w_ref,
    pred_ref,
    u_buf,
    x_buf,
    v_all,
    part_out,
    part_in,
    part_own,
    filt,
    acc,
    pred_acc,
    pred_out,
    pred_in,
    u_sem,
    x_sem,
    own_sem,
    right_sem,
    left_sem,
    line_sem,
    pair_send,
    pair_recv,
    rs_send,
    rs_recv,
    ag_send,
    ag_recv,
    q_send,
    q_recv,
    far_filt,
    far_out,
    far_in,
    far_filt_send,
    far_filt_recv,
    far_send,
    far_recv,
    hand_send,
    hand_recv,
):
    t = lax.axis_index("tm")
    v = lax.axis_index("vox")
    n_z = n_v // 2
    z, core = v // 2, v % 2
    mate = z * 2 + 1 - core
    rows_v, depth = v_ref.shape
    blocks = live_ref.shape[0]
    share = part_own.shape[2]
    half = n_z // 2
    span = n_t * share
    first_round = jnp.where(z < half, 1, 0)
    at_low, at_high = z == 0, z == n_z - 1
    is_end = at_low | at_high
    is_helper = (z == 1) | (z == n_z - 2)

    def holds(zz, src):
        return jnp.logical_not(
            ((zz == 0) & (src >= half)) | ((zz == n_z - 1) & (src < half))
        )
    test_rows = pred_out.shape[1]
    rc = rows_v // CHUNKS

    def u_copy(r, owner):
        cols = pl.ds(pl.multiple_of(r * span + owner * share, share), share)
        return pltpu.make_async_copy(u_ref.at[:, cols], u_buf.at[:, cols], u_sem.at[r, owner])

    def own_copy(ch):
        rows = pl.ds(ch * rc, rc)
        return pltpu.make_async_copy(v_ref.at[rows], v_all.at[v, rows], own_sem.at[ch])

    def line_copy(src, ch, step, first=False):
        rows = pl.ds(ch * rc, rc)
        slot = src * 2 + core
        return pltpu.make_async_remote_copy(
            src_ref=v_ref.at[rows] if first else v_all.at[slot, rows],
            dst_ref=v_all.at[slot, rows],
            send_sem=(right_sem if step > 0 else left_sem).at[src, ch],
            recv_sem=line_sem.at[src, ch],
            device_id={"vox": v + 2 * step},
            device_id_type=MESH,
        )

    def pair_copy(src, ch, first=False):
        rows = pl.ds(ch * rc, rc)
        slot = src * 2 + core
        return pltpu.make_async_remote_copy(
            src_ref=v_ref.at[rows] if first else v_all.at[slot, rows],
            dst_ref=v_all.at[slot, rows],
            send_sem=pair_send.at[src, ch],
            recv_sem=pair_recv.at[src, ch],
            device_id={"vox": mate},
            device_id_type=MESH,
        )

    def pair_arrival(src, ch):
        rows = pl.ds(ch * rc, rc)
        slot = src * 2 + 1 - core
        return pltpu.make_async_remote_copy(
            src_ref=v_all.at[slot, rows],
            dst_ref=v_all.at[slot, rows],
            send_sem=pair_send.at[src, ch],
            recv_sem=pair_recv.at[src, ch],
            device_id={"vox": mate},
            device_id_type=MESH,
        )

    def peer(d):
        return lax.rem(t + d, n_t)

    def part_copy(r, to, owner):
        return pltpu.make_async_remote_copy(
            src_ref=part_out.at[r, to],
            dst_ref=part_in.at[r, owner],
            send_sem=rs_send.at[r, to],
            recv_sem=rs_recv.at[r, owner],
            device_id={"tm": to},
            device_id_type=MESH,
        )

    def filt_copy(r, to, owner):
        return pltpu.make_async_remote_copy(
            src_ref=filt.at[r, owner],
            dst_ref=filt.at[r, owner],
            send_sem=ag_send.at[r, to],
            recv_sem=ag_recv.at[r, owner],
            device_id={"tm": to},
            device_id_type=MESH,
        )

    relayed = n_t == 4
    near = [t + 1 - 2 * lax.rem(t, 2), lax.rem(t + 2, n_t)] if relayed else [peer(d) for d in range(1, n_t)]

    def relay_copy(r, k, to, owner):
        rows = pl.ds(k * (filt.shape[2] // 2), filt.shape[2] // 2)
        return pltpu.make_async_remote_copy(
            src_ref=filt.at[r, owner, rows],
            dst_ref=filt.at[r, owner, rows],
            send_sem=hand_send.at[r, k],
            recv_sem=hand_recv.at[r, k],
            device_id={"tm": to},
            device_id_type=MESH,
        )

    def pred_copy(to, owner):
        return pltpu.make_async_remote_copy(
            src_ref=pred_out.at[to],
            dst_ref=pred_in.at[owner],
            send_sem=q_send.at[to],
            recv_sem=q_recv.at[owner],
            device_id={"tm": to},
            device_id_type=MESH,
        )

    inward = jnp.where(z < half, 1, -1)

    def far_filt_copy(j, step):
        rows = pl.ds(j * BLK, BLK)
        return pltpu.make_async_remote_copy(
            src_ref=filt.at[first_round, :, rows, :],
            dst_ref=far_filt.at[:, rows, :],
            send_sem=far_filt_send.at[j],
            recv_sem=far_filt_recv.at[j],
            device_id={"vox": v + 2 * step},
            device_id_type=MESH,
        )

    def far_copy(j, ch, step):
        rows = pl.ds(ch * rc, rc)
        return pltpu.make_async_remote_copy(
            src_ref=far_out.at[j, rows],
            dst_ref=far_in.at[j, rows],
            send_sem=far_send.at[j, ch],
            recv_sem=far_recv.at[j, ch],
            device_id={"vox": v + 2 * step},
            device_id_type=MESH,
        )

    rounds = (first_round, 1 - first_round)
    for r in rounds:
        for d in range(n_t):
            u_copy(r, peer((d + 1) % n_t)).start()

    barrier = pltpu.get_barrier_semaphore()
    for d in range(1, n_t):
        pl.semaphore_signal(barrier, inc=1, device_id={"tm": peer(d)}, device_id_type=MESH)
    pl.semaphore_signal(barrier, inc=1, device_id={"vox": mate}, device_id_type=MESH)

    @pl.when(z > 0)
    def _():
        pl.semaphore_signal(barrier, inc=1, device_id={"vox": v - 2}, device_id_type=MESH)

    @pl.when(z < n_z - 1)
    def _():
        pl.semaphore_signal(barrier, inc=1, device_id={"vox": v + 2}, device_id_type=MESH)

    neighbours = jnp.where(z > 0, 1, 0) + jnp.where(z < n_z - 1, 1, 0)
    pl.semaphore_wait(barrier, n_t + neighbours)

    for ch in range(CHUNKS):

        @pl.when(z > 0)
        def _():
            line_copy(z, ch, -1, True).start()

        @pl.when(z < n_z - 1)
        def _():
            line_copy(z, ch, 1, True).start()

    pick = one_hot(live_ref, cap)
    lam = [lambda_ref[index_ref[i]] for i in range(blocks)]
    slot_lam = [sum(pick[j][i] * lam[i] for i in range(blocks)) for j in range(cap)]
    slot_live = [sum(pick[j][i] for i in range(blocks)) for j in range(cap)]

    y_cols = [y_ref[:, i * BLK : (i + 1) * BLK].astype(jnp.float32) for i in range(blocks)]
    y_t = jnp.concatenate(
        [sum(pick[j][i] * y_cols[i] for i in range(blocks)).T for j in range(cap)], axis=0
    ).astype(jnp.bfloat16)

    def make_parts(r, send):
        for d in range(1, n_t + 1):
            to = peer(d % n_t)
            u_copy(r, to).wait()

            def tile(i, _, to=to, d=d):
                off = pl.multiple_of(i * TILE, TILE)
                cols = pl.ds(pl.multiple_of(r * span + to * share + i * TILE, TILE), TILE)
                value = jnp.dot(y_t, u_buf[:, cols], preferred_element_type=jnp.float32)
                if d < n_t:
                    part_out[r, to, :, pl.ds(off, TILE)] = value.astype(jnp.bfloat16)
                else:
                    part_own[r, :, pl.ds(off, TILE)] = value
                return 0

            lax.fori_loop(0, share // TILE, tile, 0)
            if send and d < n_t:
                part_copy(r, to, t).start()

    def send_parts(r):
        for d in range(1, n_t):
            part_copy(r, peer(d), t).start()

    def filter_parts(r):
        for d in range(1, n_t):
            part_copy(r, peer(d), peer(d)).wait_recv()
        for i in range(share // TILE):
            cols = slice(i * TILE, (i + 1) * TILE)
            place = pl.multiple_of(r * span + t * share + i * TILE, TILE)
            sing = sing_ref[:, pl.ds(place, TILE)]
            for j in range(cap):
                rows = slice(j * BLK, (j + 1) * BLK)
                total = part_own[r, rows, cols]
                for d in range(1, n_t):
                    total = total + part_in[r, peer(d), rows, cols].astype(jnp.float32)
                factor = sing / (sing * sing + slot_lam[j]) * slot_live[j]
                filt[r, t, rows, cols] = (total * factor).astype(jnp.bfloat16)
        for to in near:
            filt_copy(r, to, t).start()

    def forward_filt(r):
        for to in near:
            filt_copy(r, to, to).wait_recv()
        if relayed:
            for k in range(2):
                relay_copy(r, k, near[k], near[1 - k]).start()

    def await_filt(r):
        if relayed:
            for k in range(2):
                relay_copy(r, k, near[k], n_t - 1 - t).wait_recv()

    make_parts(rounds[0], True)

    for ch in range(CHUNKS):
        pair_copy(z, ch, True).start()
        own_copy(ch).start()
    x_copy = pltpu.make_async_copy(x_ref, x_buf, x_sem)
    x_copy.start()

    make_parts(rounds[1], False)

    def relay(s, ch):
        low, high = z - 1 - s, z + 1 + s

        @pl.when((low >= 0) & holds(z, low))
        def _():
            line_copy(low, ch, -1).wait_recv()

            @pl.when((z < n_z - 1) & holds(z + 1, low))
            def _():
                line_copy(low, ch, 1).start()

            pair_copy(low, ch).start()

        @pl.when((high < n_z) & holds(z, high))
        def _():
            line_copy(high, ch, 1).wait_recv()

            @pl.when((z > 0) & holds(z - 1, high))
            def _():
                line_copy(high, ch, -1).start()

            pair_copy(high, ch).start()

    def product(values, slot, rows, factors):
        return lax.dot_general(
            values[slot, rows, :], factors, (((1,), (1,)), ((), ())),
            preferred_element_type=jnp.float32,
        )

    def place_of(slot):
        start = lax.rem(slot * depth, span)
        owner = start // share
        return owner, pl.ds(pl.multiple_of(start - owner * share, depth), depth)

    base = jnp.where(z == 1, half, 0) * 2

    def settle(ch):
        own_copy(ch).wait()

        def step(src, _):
            @pl.when(holds(z, src))
            def _():
                pair_arrival(src, ch).wait_recv()

            return 0

        lax.fori_loop(0, n_z, step, 0)

    def add_round(r, ch):
        rows = pl.ds(ch * rc, rc)

        def step(i, value):
            slot = r * half * 2 + i
            owner, inner = place_of(slot)
            return value + product(v_all, slot, rows, filt[r, owner, :, inner])

        value = jnp.zeros((rc, acc.shape[1]), jnp.float32)
        for i in range(2 * half):
            value = step(i, value)
        return value

    def far_half(ch):
        rows = pl.ds(ch * rc, rc)

        @pl.when(jnp.logical_not(is_end))
        def _():
            acc[rows, :] = add_round(rounds[0], ch)

        @pl.when(is_end)
        def _():
            acc[rows, :] = jnp.zeros((rc, acc.shape[1]), jnp.float32)

    def help_end(j, chunks):
        cols = slice(j * BLK, (j + 1) * BLK)

        @pl.when(is_helper)
        def _():
            if chunks[0] == 0:
                far_filt_copy(j, -inward).wait_recv()
            for ch in chunks:
                rows = pl.ds(ch * rc, rc)
                value = jnp.zeros((rc, BLK), jnp.float32)
                for i in range(2 * half):
                    owner, inner = place_of(base + i)
                    value += product(v_all, base + i, rows, far_filt[owner, cols, inner])
                far_out[j, rows, :] = value.astype(jnp.bfloat16)
                far_copy(j, ch, -inward).start()

    early, last = CHUNKS // 2, CHUNKS - 1
    for ch in range(early):
        relay(0, ch)
    filter_parts(rounds[0])
    for ch in range(early, last):
        relay(0, ch)
    forward_filt(rounds[0])
    send_parts(rounds[1])
    relay(0, last)
    await_filt(rounds[0])

    @pl.when(is_end)
    def _():
        for j in range(cap):
            far_filt_copy(j, inward).start()

    def relay_step(s, _):
        for ch in range(CHUNKS):
            relay(s, ch)
        return 0

    lax.fori_loop(1, n_z - 3, relay_step, 0)
    for ch in range(early):
        relay(n_z - 3, ch)
    filter_parts(rounds[1])
    for ch in range(early, last):
        relay(n_z - 3, ch)
    for ch in range(early):
        settle(ch)
        far_half(ch)
    forward_filt(rounds[1])
    for ch in range(early, last):
        settle(ch)
        far_half(ch)
    help_end(0, list(range(last)))
    relay(n_z - 3, last)
    settle(last)
    help_end(0, [last])
    far_half(last)
    help_end(1, list(range(CHUNKS)))
    for j in range(2, cap):
        help_end(j, list(range(CHUNKS)))
    await_filt(rounds[1])
    x_copy.wait()

    def finish(ch):
        rows = slice(ch * rc, (ch + 1) * rc)
        acc[rows, :] += add_round(rounds[1], ch)

        @pl.when(is_end)
        def _():
            for j in range(cap):
                cols = slice(j * BLK, (j + 1) * BLK)
                far_copy(j, ch, inward).wait_recv()
                acc[rows, cols] += far_in[j, rows, :].astype(jnp.float32)

        weights = acc[rows, :].astype(jnp.bfloat16)
        w_ref[rows, :] = weights
        value = jnp.dot(x_buf[:, rows], weights, preferred_element_type=jnp.float32)
        if ch == 0:
            pred_acc[...] = value
        else:
            pred_acc[...] += value

    for ch in range(CHUNKS):
        finish(ch)

    for d in range(1, n_t):
        to = peer(d)
        mine = pl.ds(pl.multiple_of(to * test_rows, test_rows), test_rows)
        pred_out[to] = pred_acc[mine, :].astype(jnp.bfloat16)
        pred_copy(to, t).start()
    for d in range(1, n_t):
        pred_copy(peer(d), peer(d)).wait_recv()
    total = pred_acc[pl.ds(pl.multiple_of(t * test_rows, test_rows), test_rows), :]
    for d in range(1, n_t):
        total = total + pred_in[peer(d)].astype(jnp.float32)
    pred_ref[...] = total.astype(jnp.bfloat16)

    for d in range(1, n_t):
        for r in rounds:
            part_copy(r, peer(d), t).wait_send()
        pred_copy(peer(d), t).wait_send()
    for r in rounds:
        for to in near:
            filt_copy(r, to, t).wait_send()
        if relayed:
            for k in range(2):
                relay_copy(r, k, near[k], near[1 - k]).wait_send()

    @pl.when(is_end)
    def _():
        for j in range(cap):
            far_filt_copy(j, inward).wait_send()

    @pl.when(is_helper)
    def _():
        for j in range(cap):
            for ch in range(CHUNKS):
                far_copy(j, ch, -inward).wait_send()

    def drain(src, _):
        for ch in range(CHUNKS):

            @pl.when(holds(z, src))
            def _():
                pair_copy(src, ch).wait_send()

            @pl.when((src <= z) & (z < n_z - 1) & holds(z, src) & holds(z + 1, src))
            def _():
                line_copy(src, ch, 1).wait_send()

            @pl.when((src >= z) & (z > 0) & holds(z, src) & holds(z - 1, src))
            def _():
                line_copy(src, ch, -1).wait_send()

        return 0

    lax.fori_loop(0, n_z, drain, 0)


def body(n_t, n_v, u_train, y_train, sing, lambdas, lam_index, live, v_basis, x_test):
    time_rows, features = u_train.shape
    columns = y_train.shape[1]
    blocks = lam_index.shape[0]
    cap = blocks - blocks // 3
    used = cap * BLK
    rows_v, depth = v_basis.shape
    tests = x_test.shape[0]
    share = features // n_t // 2
    n_z = n_v // 2
    low, full = jnp.bfloat16, jnp.float32
    smem = pl.BlockSpec(memory_space=pltpu.SMEM)
    vmem = pl.BlockSpec(memory_space=pltpu.VMEM)
    anywhere = pl.BlockSpec(memory_space=pl.ANY)
    dma = pltpu.SemaphoreType.DMA
    weights, predicted = pl.pallas_call(
        functools.partial(kernel, n_t, n_v, cap),
        out_shape=(
            jax.ShapeDtypeStruct((rows_v, used), low),
            jax.ShapeDtypeStruct((tests // n_t, used), low),
        ),
        in_specs=[smem, smem, smem, vmem, vmem, anywhere, anywhere, anywhere],
        out_specs=(vmem, vmem),
        scratch_shapes=[
            pltpu.VMEM((time_rows, features), low),
            pltpu.VMEM((tests, rows_v), low),
            pltpu.VMEM((n_v, rows_v, depth), low),
            pltpu.VMEM((2, n_t, used, share), low),
            pltpu.VMEM((2, n_t, used, share), low),
            pltpu.VMEM((2, used, share), full),
            pltpu.VMEM((2, n_t, used, share), low),
            pltpu.VMEM((rows_v, used), full),
            pltpu.VMEM((tests, used), full),
            pltpu.VMEM((n_t, tests // n_t, used), low),
            pltpu.VMEM((n_t, tests // n_t, used), low),
            dma((2, n_t)),
            dma,
            dma((CHUNKS,)),
            dma((n_z, CHUNKS)),
            dma((n_z, CHUNKS)),
            dma((n_z, CHUNKS)),
            dma((n_z, CHUNKS)),
            dma((n_z, CHUNKS)),
            dma((2, n_t)),
            dma((2, n_t)),
            dma((2, n_t)),
            dma((2, n_t)),
            dma((n_t,)),
            dma((n_t,)),
            pltpu.VMEM((n_t, used, share), low),
            pltpu.VMEM((cap, rows_v, BLK), low),
            pltpu.VMEM((cap, rows_v, BLK), low),
            dma((cap,)),
            dma((cap,)),
            dma((cap, CHUNKS)),
            dma((cap, CHUNKS)),
            dma((2, 2)),
            dma((2, 2)),
        ],
        compiler_params=pltpu.CompilerParams(collective_id=0, has_side_effects=True),
    )(live, lam_index, lambdas, sing.reshape(1, features), y_train, u_train, v_basis, x_test)
    return pl.pallas_call(
        functools.partial(expand, cap),
        out_shape=(
            jax.ShapeDtypeStruct((rows_v, columns), low),
            jax.ShapeDtypeStruct((tests // n_t, columns), low),
        ),
        in_specs=[smem, vmem, vmem],
        out_specs=(vmem, vmem),
    )(live, weights, predicted)


PARTS = (4, 4, 4, 8, 8)


def row_chunks(rows):
    starts, start = [], 0
    for part in PARTS:
        starts.append((start, rows // part))
        start += rows // part
    return starts


def widen(pick, values):
    wide = [values[:, j * BLK : (j + 1) * BLK] for j in range(len(pick))]
    return [sum(pick[j][i] * wide[j] for j in range(len(pick))) for i in range(len(pick[0]))]


def plane_kernel(
    cap,
    live_ref,
    index_ref,
    lambda_ref,
    sing_hbm,
    y_hbm,
    u_hbm,
    v_hbm,
    x_hbm,
    w_ref,
    pred_ref,
    sing_buf,
    y_buf,
    u_buf,
    x_buf,
    v_all,
    part_out,
    part_in,
    own,
    comb_out,
    comb_in,
    filt,
    far_filt,
    acc,
    pred_acc,
    far_out,
    far_in,
    pred_out,
    pred_in,
    in_sem,
    u_sem,
    own_sem,
    line_send,
    line_recv,
    pair_send,
    pair_recv,
    part_send,
    part_recv,
    comb_send,
    comb_recv,
    ag_send,
    ag_recv,
    relay_send,
    relay_recv,
    half_send,
    half_recv,
    far_filt_send,
    far_filt_recv,
    cross_send,
    cross_recv,
    far_send,
    far_recv,
    q_send,
    q_recv,
):
    t = lax.axis_index("tm")
    v = lax.axis_index("vox")
    z, core = v // 2, v % 2
    mate = z * 2 + 1 - core
    rows_v, depth = v_hbm.shape
    blocks = live_ref.shape[0]
    share = depth
    span = 4 * share
    chunks = row_chunks(rows_v)
    count = len(chunks)
    low_side = z < 2
    inward = jnp.where(low_side, 1, -1)
    is_end = (z == 0) | (z == 3)
    is_mid = jnp.logical_not(is_end)
    partner_z = jnp.where(is_end, z + inward, z - inward)
    partner = partner_z * 2 + core
    near_round = z // 2
    rounds = (1 - z % 2, z % 2)
    near = [t + 1 - 2 * lax.rem(t, 2), lax.rem(t + 2, 4)]
    diag = 3 - t
    scope = jax.named_scope

    def remote(src, dst, send, recv, **place):
        return pltpu.make_async_remote_copy(
            src_ref=src, dst_ref=dst, send_sem=send, recv_sem=recv, device_id=place, device_id_type=MESH
        )

    def rows_of(ch):
        return pl.ds(*chunks[ch])

    def slot_of(zz, cc):
        return zz * 2 + cc

    def block_of(slot, ch):
        return v_all.at[slot // 4, rows_of(ch), pl.ds(pl.multiple_of((slot % 4) * depth, depth), depth)]

    def line_copy(kind, ch):
        src = block_of(slot_of(partner_z, core), ch) if kind == 2 else v_hbm.at[rows_of(ch)]
        slot = slot_of(partner_z, core) if kind == 2 else v
        to = partner if kind == 0 else v + 2 * inward
        return remote(src, block_of(slot, ch), line_send.at[kind, ch], line_recv.at[kind, ch], vox=to)

    def line_source(kind):
        return partner_z if kind == 0 else (3 - z if kind == 1 else 3 - partner_z)

    def line_wait(kind, ch):
        at = block_of(slot_of(line_source(kind), core), ch)
        remote(at, at, line_send.at[kind, ch], line_recv.at[kind, ch], vox=partner).wait_recv()

    def pair_copy(kind, ch):
        slot = v if kind == 3 else slot_of(line_source(kind), core)
        src = v_hbm.at[rows_of(ch)] if kind == 3 else block_of(slot, ch)
        return remote(src, block_of(slot, ch), pair_send.at[kind, ch], pair_recv.at[kind, ch], vox=mate)

    def pair_wait(kind, ch):
        slot = mate if kind == 3 else slot_of(line_source(kind), 1 - core)
        at = block_of(slot, ch)
        remote(at, at, pair_send.at[kind, ch], pair_recv.at[kind, ch], vox=mate).wait_recv()

    def own_copy(ch):
        return pltpu.make_async_copy(v_hbm.at[rows_of(ch)], block_of(v, ch), own_sem.at[ch])

    def u_copy(o, i, owner):
        cols = pl.ds(pl.multiple_of(rounds[o] * span + owner * share, share), share)
        return pltpu.make_async_copy(u_hbm.at[:, cols], u_buf.at[:, cols], u_sem.at[o, i])

    def half(i):
        return pl.ds(i * BLK, BLK)

    def rank(owner):
        return pl.ds(pl.multiple_of(owner * share, share), share)

    def part_copy(o, j):
        return remote(part_out.at[o, j], part_in.at[o, j], part_send.at[o, j], part_recv.at[o, j], tm=near[j])

    def comb_copy(o, j):
        return remote(comb_out.at[o, j], comb_in.at[o, j], comb_send.at[o, j], comb_recv.at[o, j], tm=near[1 - j])

    def ag_copy(o, i, owner):
        at = filt.at[o, rank(owner)]
        return remote(at, at, ag_send.at[o, i], ag_recv.at[o, i], tm=near[i])

    def relay_copy(o, i, owner):
        at = filt.at[o, rank(owner), half(i)]
        return remote(at, at, relay_send.at[o, i], relay_recv.at[o, i], tm=near[i])

    def half_copy(i, owner):
        at = filt.at[0, rank(owner), half(i)]
        return remote(at, at, half_send.at[i], half_recv.at[i], tm=near[i])

    def far_filt_copy(k):
        if k == 0:
            src, dst = filt.at[0, rank(t)], far_filt.at[rank(t)]
        else:
            src, dst = filt.at[0, rank(near[k - 1]), half(k - 1)], far_filt.at[rank(near[k - 1]), half(k - 1)]
        return remote(src, dst, far_filt_send.at[k], far_filt_recv.at[k], vox=partner)

    def far_filt_wait(k):
        at = far_filt.at[rank(t)] if k == 0 else far_filt.at[rank(near[k - 1]), half(k - 1)]
        remote(at, at, far_filt_send.at[k], far_filt_recv.at[k], vox=partner).wait_recv()

    def cross_copy(s, i, owner):
        at = far_filt.at[rank(owner), half(1 - i)]
        return remote(at, at, cross_send.at[s, i], cross_recv.at[s, i], tm=near[i])

    def far_copy(ch):
        return remote(
            far_out.at[rows_of(ch)], far_in.at[rows_of(ch)], far_send.at[ch], far_recv.at[ch], vox=partner
        )

    others = near + [diag]
    test_rows = pred_out.shape[1]

    def pred_copy(i):
        return remote(pred_out.at[i], pred_in.at[i], q_send.at[i], q_recv.at[i], tm=others[i])

    barrier = pltpu.get_barrier_semaphore()
    for to in others:
        pl.semaphore_signal(barrier, inc=1, device_id={"tm": to}, device_id_type=MESH)
    pl.semaphore_signal(barrier, inc=1, device_id={"vox": mate}, device_id_type=MESH)
    pl.semaphore_signal(barrier, inc=1, device_id={"vox": partner}, device_id_type=MESH)

    @pl.when(is_mid)
    def _():
        pl.semaphore_signal(barrier, inc=1, device_id={"vox": v + 2 * inward}, device_id_type=MESH)

    y_copy = pltpu.make_async_copy(y_hbm, y_buf, in_sem.at[0])
    sing_copy = pltpu.make_async_copy(sing_hbm, sing_buf, in_sem.at[1])
    x_copy = pltpu.make_async_copy(x_hbm, x_buf, in_sem.at[2])
    owners = (diag, near[0], near[1], t)
    y_copy.start()
    for i in range(4):
        u_copy(0, i, owners[i]).start()
    sing_copy.start()

    with scope("bar"):
        pl.semaphore_wait(barrier, jnp.where(is_end, 5, 6))

    first_chunks = count - 2

    for ch in range(count):

        @pl.when(is_mid)
        def _():
            line_copy(1, ch).start()

        if ch < first_chunks:
            line_copy(0, ch).start()
        else:

            @pl.when(is_mid)
            def _():
                line_copy(0, ch).start()

    for i in range(4):
        u_copy(1, i, owners[i]).start()

    pick = one_hot(live_ref, cap)
    lam = [lambda_ref[index_ref[i]] for i in range(blocks)]
    slot_lam = [sum(pick[j][i] * lam[i] for i in range(blocks)) for j in range(cap)]
    slot_live = [sum(pick[j][i] for i in range(blocks)) for j in range(cap)]

    with scope("ycp"):
        y_copy.wait()
    y_cols = [y_buf[:, i * BLK : (i + 1) * BLK].astype(jnp.float32) for i in range(blocks)]
    y_t = jnp.concatenate(
        [sum(pick[j][i] * y_cols[i] for i in range(blocks)).T for j in range(cap)], axis=0
    ).astype(jnp.bfloat16)

    def make_parts(o):
        for i in range(4):
            u_copy(o, i, owners[i]).wait()
            for tile in range(share // TILE):
                into = slice(tile * TILE, (tile + 1) * TILE)
                start = rounds[o] * span + owners[i] * share + tile * TILE
                cols = pl.ds(pl.multiple_of(start, TILE), TILE)
                value = jnp.dot(y_t, u_buf[:, cols], preferred_element_type=jnp.float32)
                first, second = value[:BLK], value[BLK:]
                if i == 0:
                    part_out[o, 0, 1, :, into] = first.astype(jnp.bfloat16)
                    part_out[o, 1, 1, :, into] = second.astype(jnp.bfloat16)
                elif i == 1:
                    part_out[o, 0, 0, :, into] = first.astype(jnp.bfloat16)
                    own[o, 1, 1, :, into] = second
                elif i == 2:
                    own[o, 0, 1, :, into] = first
                    part_out[o, 1, 0, :, into] = second.astype(jnp.bfloat16)
                else:
                    own[o, 0, 0, :, into] = first
                    own[o, 1, 0, :, into] = second
            if i in (1, 2):
                part_copy(o, i - 1).start()

    def combine(o):
        for j in range(2):
            part_copy(o, j).wait_recv()
            comb_out[o, j] = (own[o, j, 1] + part_in[o, j, 1].astype(jnp.float32)).astype(jnp.bfloat16)
            comb_copy(o, j).start()

    def filter_parts(o):
        place = pl.multiple_of(rounds[o] * span + t * share, share)
        sing = sing_buf[:, pl.ds(place, share)]
        for j in range(cap):
            comb_copy(o, j).wait_recv()
            total = own[o, j, 0] + part_in[o, j, 0].astype(jnp.float32) + comb_in[o, j].astype(jnp.float32)
            factor = sing / (sing * sing + slot_lam[j]) * slot_live[j]
            filt[o, rank(t), half(j)] = (total * factor).T.astype(jnp.bfloat16)

    def send_filt(o):
        for i in range(2):
            ag_copy(o, i, t).start()

    def forward_filt(o):
        for i in range(2):
            ag_copy(o, i, near[i]).wait_recv()
        for i in range(2):
            relay_copy(o, i, near[1 - i]).start()

    def await_filt(o):
        for i in range(2):
            relay_copy(o, i, diag).wait_recv()

    with scope("mp0"):
        make_parts(0)
    with scope("mp1"):
        make_parts(1)
    for ch in range(count):
        pair_copy(3, ch).start()
        own_copy(ch).start()
    x_copy.start()
    sing_copy.wait()

    def near_product(o, ch):
        return jnp.dot(v_all[near_round, rows_of(ch), :], filt[o], preferred_element_type=jnp.float32)

    def far_product(ch, factors):
        return jnp.dot(v_all[1 - near_round, rows_of(ch), :], factors, preferred_element_type=jnp.float32)

    def settle_near(ch):
        own_copy(ch).wait()
        pair_wait(3, ch)
        pair_wait(0, ch)

    last = count - 1

    def finish(ch, value):
        rows = rows_of(ch)
        weights = value.astype(jnp.bfloat16)
        for i, block in enumerate(widen(pick, weights.astype(jnp.float32))):
            w_ref[rows, i * BLK : (i + 1) * BLK] = block.astype(jnp.bfloat16)
        if ch < last:
            part = jnp.dot(x_buf[:, rows], weights, preferred_element_type=jnp.float32)
            if ch == 0:
                pred_acc[...] = part
            else:
                pred_acc[...] += part
            return
        for i, to in enumerate([diag, near[0], near[1], t]):
            mine = pl.ds(pl.multiple_of(to * test_rows, test_rows), test_rows)
            part = jnp.dot(x_buf[mine, rows], weights, preferred_element_type=jnp.float32)
            if i < 3:
                k = (2, 0, 1)[i]
                pred_out[k] = (pred_acc[mine, :] + part).astype(jnp.bfloat16)
                pred_copy(k).start()
            else:
                pred_acc[mine, :] += part

    @pl.when(is_mid)
    def _():
        def arrive(kind, ch):
            line_wait(kind, ch)
            if kind == 0:
                line_copy(2, ch).start()
            pair_copy(kind, ch).start()

        def help_end(ch):
            far_out[rows_of(ch), :] = far_product(ch, far_filt[...]).astype(jnp.bfloat16)
            far_copy(ch).start()

        with scope("m_ar0"):
            arrive(0, 0)
            arrive(1, 0)
        with scope("m_comb0"):
            combine(0)
        with scope("m_ar1"):
            arrive(0, 1)
            arrive(1, 1)
        with scope("m_comb1"):
            combine(1)
        with scope("m_filt0"):
            filter_parts(0)
            send_filt(0)
        with scope("m_ar2"):
            arrive(0, 2)
            arrive(1, 2)
        with scope("m_filt1"):
            filter_parts(1)
            send_filt(1)
        with scope("m_ar34"):
            arrive(1, 3)
            arrive(1, 4)
        with scope("m_ff0"):
            far_filt_wait(0)
            for i in range(2):
                cross_copy(0, i, t).start()
        with scope("m_fw0"):
            forward_filt(0)
        with scope("m_af0"):
            arrive(2, 0)
        with scope("m_ff1"):
            for k in (1, 2):
                far_filt_wait(k)
            for i in range(2):
                cross_copy(1, i, near[1 - i]).start()
        with scope("m_fw1"):
            forward_filt(1)
        with scope("m_ar03"):
            arrive(0, 3)
        with scope("m_af1"):
            arrive(2, 1)
        with scope("m_ar04"):
            arrive(0, 4)
        with scope("m_aw0"):
            await_filt(0)
        with scope("m_near"):
            for ch in range(count):
                settle_near(ch)
                acc[rows_of(ch), :] = near_product(0, ch)
        with scope("m_cross"):
            for i in range(2):
                cross_copy(0, i, near[i]).wait_recv()
                cross_copy(1, i, diag).wait_recv()
        with scope("m_help"):
            for ch in range(2):
                pair_wait(1, ch)
                pair_wait(2, ch)
                help_end(ch)
        with scope("m_aw1"):
            await_filt(1)
        x_copy.wait()


        def own_rows(ch):
            finish(ch, acc[rows_of(ch), :] + far_product(ch, filt[1]))

        def settle_far(ch):
            with scope(f"m_af{ch}"):
                arrive(2, ch)
                pair_wait(1, ch)
                pair_wait(2, ch)

        own_rows(0)
        settle_far(2)
        help_end(2)
        own_rows(1)
        settle_far(3)
        help_end(3)
        own_rows(2)
        settle_far(4)
        help_end(4)
        own_rows(3)
        own_rows(4)

    @pl.when(is_end)
    def _():
        def arrive(ch):
            line_wait(0, ch)
            pair_copy(0, ch).start()

        with scope("e_ar0"):
            arrive(0)
        with scope("e_comb0"):
            combine(0)
        with scope("e_ar1"):
            arrive(1)
        with scope("e_comb1"):
            combine(1)
        with scope("e_ar2"):
            arrive(2)
        with scope("e_filt0"):
            filter_parts(0)
            far_filt_copy(0).start()
            for i in range(2):
                half_copy(i, t).start()
        with scope("e_ar3"):
            arrive(3)
        with scope("e_filt1"):
            filter_parts(1)
            send_filt(1)
        with scope("e_half"):
            for i in range(2):
                half_copy(i, near[i]).wait_recv()
                far_filt_copy(1 + i).start()
            for ch in range(first_chunks, count):
                line_copy(0, ch).start()
        with scope("e_ar4"):
            arrive(4)
        with scope("e_fw1"):
            forward_filt(1)
        x_copy.wait()
        with scope("e_aw1"):
            await_filt(1)
        with scope("e_near"):
            for ch in range(count):
                settle_near(ch)
                acc[rows_of(ch), :] = near_product(1, ch)
        for ch in range(count):
            with scope(f"e_far{ch}"):
                far_copy(ch).wait_recv()
            finish(ch, acc[rows_of(ch), :] + far_in[rows_of(ch), :].astype(jnp.float32))

    with scope("pwait"):
        for i in range(3):
            pred_copy(i).wait_recv()
    total = pred_acc[pl.ds(pl.multiple_of(t * test_rows, test_rows), test_rows), :]
    for i in range(3):
        total = total + pred_in[i].astype(jnp.float32)
    total = total.astype(jnp.bfloat16).astype(jnp.float32)
    for i, block in enumerate(widen(pick, total)):
        pred_ref[:, i * BLK : (i + 1) * BLK] = block.astype(jnp.bfloat16)

    with scope("drain"):
        for ch in range(count):
            line_copy(0, ch).wait_send()
            pair_copy(3, ch).wait_send()
            pair_copy(0, ch).wait_send()
        for o in range(2):
            for j in range(2):
                part_copy(o, j).wait_send()
                comb_copy(o, j).wait_send()
        for i in range(2):
            ag_copy(1, i, t).wait_send()
            relay_copy(1, i, near[1 - i]).wait_send()
        for i in range(3):
            pred_copy(i).wait_send()

        @pl.when(is_mid)
        def _():
            for ch in range(count):
                line_copy(1, ch).wait_send()
                line_copy(2, ch).wait_send()
                pair_copy(1, ch).wait_send()
                pair_copy(2, ch).wait_send()
                far_copy(ch).wait_send()
            for i in range(2):
                ag_copy(0, i, t).wait_send()
                relay_copy(0, i, near[1 - i]).wait_send()
                cross_copy(0, i, t).wait_send()
                cross_copy(1, i, near[1 - i]).wait_send()

        @pl.when(is_end)
        def _():
            for i in range(2):
                half_copy(i, t).wait_send()
            for k in range(3):
                far_filt_copy(k).wait_send()


def plane_body(u_train, y_train, sing, lambdas, lam_index, live, v_basis, x_test):
    time_rows, features = u_train.shape
    columns = y_train.shape[1]
    blocks = lam_index.shape[0]
    cap = blocks - blocks // 3
    used = cap * BLK
    rows_v, depth = v_basis.shape
    tests = x_test.shape[0]
    share = depth
    count = len(PARTS)
    low, full = jnp.bfloat16, jnp.float32
    smem = pl.BlockSpec(memory_space=pltpu.SMEM)
    vmem = pl.BlockSpec(memory_space=pltpu.VMEM)
    anywhere = pl.BlockSpec(memory_space=pl.ANY)
    dma = pltpu.SemaphoreType.DMA
    weights, predicted = pl.pallas_call(
        functools.partial(plane_kernel, cap),
        out_shape=(pltpu.VMEM((rows_v, columns), low), pltpu.VMEM((tests // 4, columns), low)),
        in_specs=[smem, smem, smem] + [anywhere] * 5,
        out_specs=(vmem, vmem),
        scratch_shapes=[
            pltpu.VMEM((1, features), full),
            pltpu.VMEM((time_rows, columns), low),
            pltpu.VMEM((time_rows, features), low),
            pltpu.VMEM((tests, rows_v), low),
            pltpu.VMEM((2, rows_v, 4 * depth), low),
            pltpu.VMEM((2, 2, 2, BLK, share), low),
            pltpu.VMEM((2, 2, 2, BLK, share), low),
            pltpu.VMEM((2, 2, 2, BLK, share), full),
            pltpu.VMEM((2, 2, BLK, share), low),
            pltpu.VMEM((2, 2, BLK, share), low),
            pltpu.VMEM((2, 4 * share, used), low),
            pltpu.VMEM((4 * share, used), low),
            pltpu.VMEM((rows_v, used), full),
            pltpu.VMEM((tests, used), full),
            pltpu.VMEM((rows_v, used), low),
            pltpu.VMEM((rows_v, used), low),
            pltpu.VMEM((3, tests // 4, used), low),
            pltpu.VMEM((3, tests // 4, used), low),
            dma((3,)),
            dma((2, 4)),
            dma((count,)),
            dma((3, count)),
            dma((3, count)),
            dma((4, count)),
            dma((4, count)),
            dma((2, 2)),
            dma((2, 2)),
            dma((2, 2)),
            dma((2, 2)),
            dma((2, 2)),
            dma((2, 2)),
            dma((2, 2)),
            dma((2, 2)),
            dma((2,)),
            dma((2,)),
            dma((3,)),
            dma((3,)),
            dma((2, 2)),
            dma((2, 2)),
            dma((count,)),
            dma((count,)),
            dma((3,)),
            dma((3,)),
        ],
        compiler_params=pltpu.CompilerParams(
            collective_id=1, has_side_effects=True
        ),
    )(live, lam_index, lambdas, sing.reshape(1, features), y_train, u_train, v_basis, x_test)
    return weights, predicted


def routed(n_t, n_v, *args):
    if (n_t, n_v, args[4].shape[0]) == (4, 8, 3):
        return plane_body(*args)
    return body(n_t, n_v, *args)


def solution(mesh):
    placed = (
        P("tm", None),
        P("tm", "vox"),
        P(),
        P(),
        P("vox"),
        P("vox"),
        P("tm", "vox"),
        P(None, "tm"),
    )
    return jax.shard_map(
        functools.partial(routed, mesh.shape["tm"], mesh.shape["vox"]),
        mesh=mesh,
        in_specs=placed,
        out_specs=(P("tm", "vox"), P("tm", "vox")),
        check_vma=False,
    )
```

```python
import functools

import jax
import jax.numpy as jnp
from jax import lax
from jax.experimental import pallas as pl
from jax.experimental.pallas import tpu as pltpu
from jax.sharding import PartitionSpec as P

BLK = 128
CHUNKS = 4
TILE = 256
MESH = pl.DeviceIdType.MESH


def one_hot(live_ref, cap):
    blocks = live_ref.shape[0]
    live = [live_ref[i] for i in range(blocks)]
    before = [sum(live[:i], jnp.int32(0)) for i in range(blocks)]
    return [
        [jnp.where(before[i] == j, live[i], 0).astype(jnp.float32) for i in range(blocks)]
        for j in range(cap)
    ]


def expand(cap, live_ref, w_in, pred_in, w_ref, pred_ref):
    pick = one_hot(live_ref, cap)
    for source, target in ((w_in, w_ref), (pred_in, pred_ref)):
        values = [source[:, j * BLK : (j + 1) * BLK].astype(jnp.float32) for j in range(cap)]
        for i in range(live_ref.shape[0]):
            block = sum(pick[j][i] * values[j] for j in range(cap))
            target[:, i * BLK : (i + 1) * BLK] = block.astype(target.dtype)


def kernel(
    n_t,
    n_v,
    cap,
    live_ref,
    index_ref,
    lambda_ref,
    sing_ref,
    y_ref,
    u_ref,
    v_ref,
    x_ref,
    w_ref,
    pred_ref,
    u_buf,
    x_buf,
    v_all,
    part_out,
    part_in,
    part_own,
    filt,
    acc,
    pred_acc,
    pred_out,
    pred_in,
    u_sem,
    x_sem,
    own_sem,
    right_sem,
    left_sem,
    line_sem,
    pair_send,
    pair_recv,
    rs_send,
    rs_recv,
    ag_send,
    ag_recv,
    q_send,
    q_recv,
    far_filt,
    far_out,
    far_in,
    far_filt_send,
    far_filt_recv,
    far_send,
    far_recv,
    hand_send,
    hand_recv,
):
    t = lax.axis_index("tm")
    v = lax.axis_index("vox")
    n_z = n_v // 2
    z, core = v // 2, v % 2
    mate = z * 2 + 1 - core
    rows_v, depth = v_ref.shape
    blocks = live_ref.shape[0]
    share = part_own.shape[2]
    half = n_z // 2
    span = n_t * share
    first_round = jnp.where(z < half, 1, 0)
    at_low, at_high = z == 0, z == n_z - 1
    is_end = at_low | at_high
    is_helper = (z == 1) | (z == n_z - 2)

    def holds(zz, src):
        return jnp.logical_not(
            ((zz == 0) & (src >= half)) | ((zz == n_z - 1) & (src < half))
        )
    test_rows = pred_out.shape[1]
    rc = rows_v // CHUNKS

    def u_copy(r, owner):
        cols = pl.ds(pl.multiple_of(r * span + owner * share, share), share)
        return pltpu.make_async_copy(u_ref.at[:, cols], u_buf.at[:, cols], u_sem.at[r, owner])

    def own_copy(ch):
        rows = pl.ds(ch * rc, rc)
        return pltpu.make_async_copy(v_ref.at[rows], v_all.at[v, rows], own_sem.at[ch])

    def line_copy(src, ch, step, first=False):
        rows = pl.ds(ch * rc, rc)
        slot = src * 2 + core
        return pltpu.make_async_remote_copy(
            src_ref=v_ref.at[rows] if first else v_all.at[slot, rows],
            dst_ref=v_all.at[slot, rows],
            send_sem=(right_sem if step > 0 else left_sem).at[src, ch],
            recv_sem=line_sem.at[src, ch],
            device_id={"vox": v + 2 * step},
            device_id_type=MESH,
        )

    def pair_copy(src, ch, first=False):
        rows = pl.ds(ch * rc, rc)
        slot = src * 2 + core
        return pltpu.make_async_remote_copy(
            src_ref=v_ref.at[rows] if first else v_all.at[slot, rows],
            dst_ref=v_all.at[slot, rows],
            send_sem=pair_send.at[src, ch],
            recv_sem=pair_recv.at[src, ch],
            device_id={"vox": mate},
            device_id_type=MESH,
        )

    def pair_arrival(src, ch):
        rows = pl.ds(ch * rc, rc)
        slot = src * 2 + 1 - core
        return pltpu.make_async_remote_copy(
            src_ref=v_all.at[slot, rows],
            dst_ref=v_all.at[slot, rows],
            send_sem=pair_send.at[src, ch],
            recv_sem=pair_recv.at[src, ch],
            device_id={"vox": mate},
            device_id_type=MESH,
        )

    def peer(d):
        return lax.rem(t + d, n_t)

    def part_copy(r, to, owner):
        return pltpu.make_async_remote_copy(
            src_ref=part_out.at[r, to],
            dst_ref=part_in.at[r, owner],
            send_sem=rs_send.at[r, to],
            recv_sem=rs_recv.at[r, owner],
            device_id={"tm": to},
            device_id_type=MESH,
        )

    def filt_copy(r, to, owner):
        return pltpu.make_async_remote_copy(
            src_ref=filt.at[r, owner],
            dst_ref=filt.at[r, owner],
            send_sem=ag_send.at[r, to],
            recv_sem=ag_recv.at[r, owner],
            device_id={"tm": to},
            device_id_type=MESH,
        )

    relayed = n_t == 4
    near = [t + 1 - 2 * lax.rem(t, 2), lax.rem(t + 2, n_t)] if relayed else [peer(d) for d in range(1, n_t)]

    def relay_copy(r, k, to, owner):
        rows = pl.ds(k * (filt.shape[2] // 2), filt.shape[2] // 2)
        return pltpu.make_async_remote_copy(
            src_ref=filt.at[r, owner, rows],
            dst_ref=filt.at[r, owner, rows],
            send_sem=hand_send.at[r, k],
            recv_sem=hand_recv.at[r, k],
            device_id={"tm": to},
            device_id_type=MESH,
        )

    def pred_copy(to, owner):
        return pltpu.make_async_remote_copy(
            src_ref=pred_out.at[to],
            dst_ref=pred_in.at[owner],
            send_sem=q_send.at[to],
            recv_sem=q_recv.at[owner],
            device_id={"tm": to},
            device_id_type=MESH,
        )

    inward = jnp.where(z < half, 1, -1)

    def far_filt_copy(j, step):
        rows = pl.ds(j * BLK, BLK)
        return pltpu.make_async_remote_copy(
            src_ref=filt.at[first_round, :, rows, :],
            dst_ref=far_filt.at[:, rows, :],
            send_sem=far_filt_send.at[j],
            recv_sem=far_filt_recv.at[j],
            device_id={"vox": v + 2 * step},
            device_id_type=MESH,
        )

    def far_copy(j, ch, step):
        rows = pl.ds(ch * rc, rc)
        return pltpu.make_async_remote_copy(
            src_ref=far_out.at[j, rows],
            dst_ref=far_in.at[j, rows],
            send_sem=far_send.at[j, ch],
            recv_sem=far_recv.at[j, ch],
            device_id={"vox": v + 2 * step},
            device_id_type=MESH,
        )

    rounds = (first_round, 1 - first_round)
    for r in rounds:
        for d in range(n_t):
            u_copy(r, peer((d + 1) % n_t)).start()

    barrier = pltpu.get_barrier_semaphore()
    for d in range(1, n_t):
        pl.semaphore_signal(barrier, inc=1, device_id={"tm": peer(d)}, device_id_type=MESH)
    pl.semaphore_signal(barrier, inc=1, device_id={"vox": mate}, device_id_type=MESH)

    @pl.when(z > 0)
    def _():
        pl.semaphore_signal(barrier, inc=1, device_id={"vox": v - 2}, device_id_type=MESH)

    @pl.when(z < n_z - 1)
    def _():
        pl.semaphore_signal(barrier, inc=1, device_id={"vox": v + 2}, device_id_type=MESH)

    neighbours = jnp.where(z > 0, 1, 0) + jnp.where(z < n_z - 1, 1, 0)
    pl.semaphore_wait(barrier, n_t + neighbours)

    for ch in range(CHUNKS):

        @pl.when(z > 0)
        def _():
            line_copy(z, ch, -1, True).start()

        @pl.when(z < n_z - 1)
        def _():
            line_copy(z, ch, 1, True).start()

    pick = one_hot(live_ref, cap)
    lam = [lambda_ref[index_ref[i]] for i in range(blocks)]
    slot_lam = [sum(pick[j][i] * lam[i] for i in range(blocks)) for j in range(cap)]
    slot_live = [sum(pick[j][i] for i in range(blocks)) for j in range(cap)]

    y_cols = [y_ref[:, i * BLK : (i + 1) * BLK].astype(jnp.float32) for i in range(blocks)]
    y_t = jnp.concatenate(
        [sum(pick[j][i] * y_cols[i] for i in range(blocks)).T for j in range(cap)], axis=0
    ).astype(jnp.bfloat16)

    def make_parts(r, send):
        for d in range(1, n_t + 1):
            to = peer(d % n_t)
            u_copy(r, to).wait()

            def tile(i, _, to=to, d=d):
                off = pl.multiple_of(i * TILE, TILE)
                cols = pl.ds(pl.multiple_of(r * span + to * share + i * TILE, TILE), TILE)
                value = jnp.dot(y_t, u_buf[:, cols], preferred_element_type=jnp.float32)
                if d < n_t:
                    part_out[r, to, :, pl.ds(off, TILE)] = value.astype(jnp.bfloat16)
                else:
                    part_own[r, :, pl.ds(off, TILE)] = value
                return 0

            lax.fori_loop(0, share // TILE, tile, 0)
            if send and d < n_t:
                part_copy(r, to, t).start()

    def send_parts(r):
        for d in range(1, n_t):
            part_copy(r, peer(d), t).start()

    def filter_parts(r):
        for d in range(1, n_t):
            part_copy(r, peer(d), peer(d)).wait_recv()
        for i in range(share // TILE):
            cols = slice(i * TILE, (i + 1) * TILE)
            place = pl.multiple_of(r * span + t * share + i * TILE, TILE)
            sing = sing_ref[:, pl.ds(place, TILE)]
            for j in range(cap):
                rows = slice(j * BLK, (j + 1) * BLK)
                total = part_own[r, rows, cols]
                for d in range(1, n_t):
                    total = total + part_in[r, peer(d), rows, cols].astype(jnp.float32)
                factor = sing / (sing * sing + slot_lam[j]) * slot_live[j]
                filt[r, t, rows, cols] = (total * factor).astype(jnp.bfloat16)
        for to in near:
            filt_copy(r, to, t).start()

    def forward_filt(r):
        for to in near:
            filt_copy(r, to, to).wait_recv()
        if relayed:
            for k in range(2):
                relay_copy(r, k, near[k], near[1 - k]).start()

    def await_filt(r):
        if relayed:
            for k in range(2):
                relay_copy(r, k, near[k], n_t - 1 - t).wait_recv()

    make_parts(rounds[0], True)

    for ch in range(CHUNKS):
        pair_copy(z, ch, True).start()
        own_copy(ch).start()
    x_copy = pltpu.make_async_copy(x_ref, x_buf, x_sem)
    x_copy.start()

    make_parts(rounds[1], False)

    def relay(s, ch):
        low, high = z - 1 - s, z + 1 + s

        @pl.when((low >= 0) & holds(z, low))
        def _():
            line_copy(low, ch, -1).wait_recv()

            @pl.when((z < n_z - 1) & holds(z + 1, low))
            def _():
                line_copy(low, ch, 1).start()

            pair_copy(low, ch).start()

        @pl.when((high < n_z) & holds(z, high))
        def _():
            line_copy(high, ch, 1).wait_recv()

            @pl.when((z > 0) & holds(z - 1, high))
            def _():
                line_copy(high, ch, -1).start()

            pair_copy(high, ch).start()

    def product(values, slot, rows, factors):
        return lax.dot_general(
            values[slot, rows, :], factors, (((1,), (1,)), ((), ())),
            preferred_element_type=jnp.float32,
        )

    def place_of(slot):
        start = lax.rem(slot * depth, span)
        owner = start // share
        return owner, pl.ds(pl.multiple_of(start - owner * share, depth), depth)

    base = jnp.where(z == 1, half, 0) * 2

    def settle(ch):
        own_copy(ch).wait()

        def step(src, _):
            @pl.when(holds(z, src))
            def _():
                pair_arrival(src, ch).wait_recv()

            return 0

        lax.fori_loop(0, n_z, step, 0)

    def add_round(r, ch):
        rows = pl.ds(ch * rc, rc)

        def step(i, value):
            slot = r * half * 2 + i
            owner, inner = place_of(slot)
            return value + product(v_all, slot, rows, filt[r, owner, :, inner])

        value = jnp.zeros((rc, acc.shape[1]), jnp.float32)
        for i in range(2 * half):
            value = step(i, value)
        return value

    def far_half(ch):
        rows = pl.ds(ch * rc, rc)

        @pl.when(jnp.logical_not(is_end))
        def _():
            acc[rows, :] = add_round(rounds[0], ch)

        @pl.when(is_end)
        def _():
            acc[rows, :] = jnp.zeros((rc, acc.shape[1]), jnp.float32)

    def help_end(j, chunks):
        cols = slice(j * BLK, (j + 1) * BLK)

        @pl.when(is_helper)
        def _():
            if chunks[0] == 0:
                far_filt_copy(j, -inward).wait_recv()
            for ch in chunks:
                rows = pl.ds(ch * rc, rc)
                value = jnp.zeros((rc, BLK), jnp.float32)
                for i in range(2 * half):
                    owner, inner = place_of(base + i)
                    value += product(v_all, base + i, rows, far_filt[owner, cols, inner])
                far_out[j, rows, :] = value.astype(jnp.bfloat16)
                far_copy(j, ch, -inward).start()

    early, last = CHUNKS // 2, CHUNKS - 1
    for ch in range(early):
        relay(0, ch)
    filter_parts(rounds[0])
    for ch in range(early, last):
        relay(0, ch)
    forward_filt(rounds[0])
    send_parts(rounds[1])
    relay(0, last)
    await_filt(rounds[0])

    @pl.when(is_end)
    def _():
        for j in range(cap):
            far_filt_copy(j, inward).start()

    def relay_step(s, _):
        for ch in range(CHUNKS):
            relay(s, ch)
        return 0

    lax.fori_loop(1, n_z - 3, relay_step, 0)
    for ch in range(early):
        relay(n_z - 3, ch)
    filter_parts(rounds[1])
    for ch in range(early, last):
        relay(n_z - 3, ch)
    for ch in range(early):
        settle(ch)
        far_half(ch)
    forward_filt(rounds[1])
    for ch in range(early, last):
        settle(ch)
        far_half(ch)
    help_end(0, list(range(last)))
    relay(n_z - 3, last)
    settle(last)
    help_end(0, [last])
    far_half(last)
    help_end(1, list(range(CHUNKS)))
    for j in range(2, cap):
        help_end(j, list(range(CHUNKS)))
    await_filt(rounds[1])
    x_copy.wait()

    def finish(ch):
        rows = slice(ch * rc, (ch + 1) * rc)
        acc[rows, :] += add_round(rounds[1], ch)

        @pl.when(is_end)
        def _():
            for j in range(cap):
                cols = slice(j * BLK, (j + 1) * BLK)
                far_copy(j, ch, inward).wait_recv()
                acc[rows, cols] += far_in[j, rows, :].astype(jnp.float32)

        weights = acc[rows, :].astype(jnp.bfloat16)
        w_ref[rows, :] = weights
        value = jnp.dot(x_buf[:, rows], weights, preferred_element_type=jnp.float32)
        if ch == 0:
            pred_acc[...] = value
        else:
            pred_acc[...] += value

    for ch in range(CHUNKS):
        finish(ch)

    for d in range(1, n_t):
        to = peer(d)
        mine = pl.ds(pl.multiple_of(to * test_rows, test_rows), test_rows)
        pred_out[to] = pred_acc[mine, :].astype(jnp.bfloat16)
        pred_copy(to, t).start()
    for d in range(1, n_t):
        pred_copy(peer(d), peer(d)).wait_recv()
    total = pred_acc[pl.ds(pl.multiple_of(t * test_rows, test_rows), test_rows), :]
    for d in range(1, n_t):
        total = total + pred_in[peer(d)].astype(jnp.float32)
    pred_ref[...] = total.astype(jnp.bfloat16)

    for d in range(1, n_t):
        for r in rounds:
            part_copy(r, peer(d), t).wait_send()
        pred_copy(peer(d), t).wait_send()
    for r in rounds:
        for to in near:
            filt_copy(r, to, t).wait_send()
        if relayed:
            for k in range(2):
                relay_copy(r, k, near[k], near[1 - k]).wait_send()

    @pl.when(is_end)
    def _():
        for j in range(cap):
            far_filt_copy(j, inward).wait_send()

    @pl.when(is_helper)
    def _():
        for j in range(cap):
            for ch in range(CHUNKS):
                far_copy(j, ch, -inward).wait_send()

    def drain(src, _):
        for ch in range(CHUNKS):

            @pl.when(holds(z, src))
            def _():
                pair_copy(src, ch).wait_send()

            @pl.when((src <= z) & (z < n_z - 1) & holds(z, src) & holds(z + 1, src))
            def _():
                line_copy(src, ch, 1).wait_send()

            @pl.when((src >= z) & (z > 0) & holds(z, src) & holds(z - 1, src))
            def _():
                line_copy(src, ch, -1).wait_send()

        return 0

    lax.fori_loop(0, n_z, drain, 0)


def body(n_t, n_v, u_train, y_train, sing, lambdas, lam_index, live, v_basis, x_test):
    time_rows, features = u_train.shape
    columns = y_train.shape[1]
    blocks = lam_index.shape[0]
    cap = blocks - blocks // 3
    used = cap * BLK
    rows_v, depth = v_basis.shape
    tests = x_test.shape[0]
    share = features // n_t // 2
    n_z = n_v // 2
    low, full = jnp.bfloat16, jnp.float32
    smem = pl.BlockSpec(memory_space=pltpu.SMEM)
    vmem = pl.BlockSpec(memory_space=pltpu.VMEM)
    anywhere = pl.BlockSpec(memory_space=pl.ANY)
    dma = pltpu.SemaphoreType.DMA
    weights, predicted = pl.pallas_call(
        functools.partial(kernel, n_t, n_v, cap),
        out_shape=(
            jax.ShapeDtypeStruct((rows_v, used), low),
            jax.ShapeDtypeStruct((tests // n_t, used), low),
        ),
        in_specs=[smem, smem, smem, vmem, vmem, anywhere, anywhere, anywhere],
        out_specs=(vmem, vmem),
        scratch_shapes=[
            pltpu.VMEM((time_rows, features), low),
            pltpu.VMEM((tests, rows_v), low),
            pltpu.VMEM((n_v, rows_v, depth), low),
            pltpu.VMEM((2, n_t, used, share), low),
            pltpu.VMEM((2, n_t, used, share), low),
            pltpu.VMEM((2, used, share), full),
            pltpu.VMEM((2, n_t, used, share), low),
            pltpu.VMEM((rows_v, used), full),
            pltpu.VMEM((tests, used), full),
            pltpu.VMEM((n_t, tests // n_t, used), low),
            pltpu.VMEM((n_t, tests // n_t, used), low),
            dma((2, n_t)),
            dma,
            dma((CHUNKS,)),
            dma((n_z, CHUNKS)),
            dma((n_z, CHUNKS)),
            dma((n_z, CHUNKS)),
            dma((n_z, CHUNKS)),
            dma((n_z, CHUNKS)),
            dma((2, n_t)),
            dma((2, n_t)),
            dma((2, n_t)),
            dma((2, n_t)),
            dma((n_t,)),
            dma((n_t,)),
            pltpu.VMEM((n_t, used, share), low),
            pltpu.VMEM((cap, rows_v, BLK), low),
            pltpu.VMEM((cap, rows_v, BLK), low),
            dma((cap,)),
            dma((cap,)),
            dma((cap, CHUNKS)),
            dma((cap, CHUNKS)),
            dma((2, 2)),
            dma((2, 2)),
        ],
        compiler_params=pltpu.CompilerParams(collective_id=0, has_side_effects=True),
    )(live, lam_index, lambdas, sing.reshape(1, features), y_train, u_train, v_basis, x_test)
    return pl.pallas_call(
        functools.partial(expand, cap),
        out_shape=(
            jax.ShapeDtypeStruct((rows_v, columns), low),
            jax.ShapeDtypeStruct((tests // n_t, columns), low),
        ),
        in_specs=[smem, vmem, vmem],
        out_specs=(vmem, vmem),
    )(live, weights, predicted)


FAR_PARTS = (4, 4, 4, 8, 16, 16)
SIDE_PARTS = (2, 4, 4)


def row_pieces(rows, parts):
    pieces, start = [], 0
    for part in parts:
        pieces.append((start, rows // part))
        start += rows // part
    return pieces


def widen(pick, values):
    wide = [values[:, j * BLK : (j + 1) * BLK] for j in range(len(pick))]
    return [sum(pick[j][i] * wide[j] for j in range(len(pick))) for i in range(len(pick[0]))]


def plane_kernel(
    cap,
    live_hbm,
    index_hbm,
    lambda_hbm,
    sing_hbm,
    y_hbm,
    u_hbm,
    v_hbm,
    x_hbm,
    w_ref,
    pred_ref,
    live_ref,
    index_ref,
    lambda_ref,
    sing_buf,
    y_buf,
    u_buf,
    x_buf,
    v_all,
    part_out,
    part_in,
    own,
    comb_out,
    comb_in,
    filt,
    far_filt,
    acc,
    pred_acc,
    far_out,
    far_in,
    pred_out,
    pred_in,
    w_buf,
    in_sem,
    u_sem,
    own_sem,
    line_send,
    side_recv,
    across_recv,
    relay_recv,
    pair_send,
    pair_recv,
    pair_far_recv,
    part_send,
    part_recv,
    comb_send,
    comb_recv,
    ag_send,
    ag_recv,
    hand_send,
    hand_recv,
    plane_send,
    plane_recv,
    help_send,
    help_recv,
    q_send,
    q_recv,
):
    t = lax.axis_index("tm")
    v = lax.axis_index("vox")
    z, core = v // 2, v % 2
    mate = z * 2 + 1 - core
    rows_v, depth = v_hbm.shape
    blocks = live_ref.shape[0]
    share = depth
    span = 4 * share
    far_pieces = row_pieces(rows_v, FAR_PARTS)
    side_pieces = row_pieces(rows_v, SIDE_PARTS)
    whole = (0, rows_v)
    count = len(far_pieces)
    low_side = z < 2
    inward = jnp.where(low_side, 1, -1)
    is_end = (z == 0) | (z == 3)
    is_mid = jnp.logical_not(is_end)
    partner_z = jnp.where(is_end, z + inward, z - inward)
    partner = partner_z * 2 + core
    near_round = z // 2
    rounds = (1 - z % 2, z % 2)
    near = [t + 1 - 2 * lax.rem(t, 2), lax.rem(t + 2, 4)]
    diag = 3 - t
    scope = jax.named_scope

    def remote(src, dst, send, recv, **place):
        return pltpu.make_async_remote_copy(
            src_ref=src, dst_ref=dst, send_sem=send, recv_sem=recv, device_id=place, device_id_type=MESH
        )

    def slot_of(zz, cc):
        return zz * 2 + cc

    def block_of(slot, piece):
        cols = pl.ds(pl.multiple_of((slot % 4) * depth, depth), depth)
        return v_all.at[slot // 4, pl.ds(*piece), cols]

    far_mid, far_end = 3 - z, 3 - partner_z

    def side_copy(piece, recv):
        return remote(v_hbm.at[pl.ds(*piece)], block_of(v, piece), line_send.at[0], recv, vox=partner)

    def side_wait(piece, recv):
        at = block_of(partner, piece)
        remote(at, at, line_send.at[0], recv, vox=partner).wait_recv()

    def across_copy():
        return remote(v_hbm, block_of(v, whole), line_send.at[1], across_recv, vox=v + 2 * inward)

    def across_wait():
        at = block_of(slot_of(far_mid, core), whole)
        remote(at, at, line_send.at[1], across_recv, vox=v + 2 * inward).wait_recv()

    def line_relay(i):
        at = block_of(partner, far_pieces[i])
        return remote(at, at, line_send.at[2], relay_recv.at[i], vox=v + 2 * inward)

    def line_relay_wait(i):
        at = block_of(slot_of(far_end, core), far_pieces[i])
        remote(at, at, line_send.at[2], relay_recv.at[i], vox=v + 2 * inward).wait_recv()

    def pair_copy(k):
        src = v_hbm if k == 0 else block_of(pair_slot(k, core), whole)
        return remote(src, block_of(pair_slot(k, core), whole), pair_send.at[k], pair_recv.at[k], vox=mate)

    def pair_slot(k, cc):
        return slot_of((z, partner_z, far_mid)[k], cc)

    def pair_wait(k):
        at = block_of(pair_slot(k, 1 - core), whole)
        remote(at, at, pair_send.at[k], pair_recv.at[k], vox=mate).wait_recv()

    def pair_far_copy(i):
        at = block_of(slot_of(far_end, core), far_pieces[i])
        return remote(at, at, pair_send.at[3], pair_far_recv.at[i], vox=mate)

    def pair_far_wait(i):
        at = block_of(slot_of(far_end, 1 - core), far_pieces[i])
        remote(at, at, pair_send.at[3], pair_far_recv.at[i], vox=mate).wait_recv()

    def own_copy():
        return pltpu.make_async_copy(v_hbm, block_of(v, whole), own_sem)

    def rows_of(i):
        return pl.ds(*far_pieces[i])

    def u_copy(i):
        first, width = (owners[i] * share, share) if i < 4 else (0, span)
        cols = pl.ds(pl.multiple_of(rounds[i // 4] * span + first, share), width)
        return pltpu.make_async_copy(u_hbm.at[:, cols], u_buf.at[:, cols], u_sem.at[i])

    def half(i):
        return pl.ds(i * BLK, BLK)

    def rank(owner):
        return pl.ds(pl.multiple_of(owner * share, share), share)

    def part_copy(o, j, s):
        return remote(part_out.at[o, j, s], part_in.at[o, j, s], part_send, part_recv.at[o, j, s], tm=near[j])

    def comb_copy(o, j):
        return remote(comb_out.at[o, j], comb_in.at[o, j], comb_send, comb_recv.at[o, j], tm=near[1 - j])

    def ag_copy(o, i, owner):
        at = filt.at[o, rank(owner)]
        return remote(at, at, ag_send, ag_recv.at[o, i], tm=near[i])

    def hand_copy(o, i, owner):
        at = filt.at[o, rank(owner), half(i)]
        return remote(at, at, hand_send, hand_recv.at[o, i], tm=near[i])

    def half_copy(i, owner):
        at = filt.at[0, rank(owner), half(i)]
        return remote(at, at, plane_send, plane_recv.at[0, i], tm=near[i])

    def far_filt_copy(k):
        if k == 0:
            src, dst = filt.at[0, rank(t)], far_filt.at[rank(t)]
        else:
            src, dst = filt.at[0, rank(near[k - 1]), half(k - 1)], far_filt.at[rank(near[k - 1]), half(k - 1)]
        return remote(src, dst, help_send, help_recv.at[k], vox=partner)

    def far_filt_wait(k):
        at = far_filt.at[rank(t)] if k == 0 else far_filt.at[rank(near[k - 1]), half(k - 1)]
        remote(at, at, help_send, help_recv.at[k], vox=partner).wait_recv()

    def cross_copy(s, i, owner):
        at = far_filt.at[rank(owner), half(1 - i)]
        return remote(at, at, plane_send, plane_recv.at[s, i], tm=near[i])

    def far_copy(ch):
        return remote(
            far_out.at[rows_of(ch)], far_in.at[rows_of(ch)], help_send, help_recv.at[ch], vox=partner
        )

    others = near + [diag]
    test_rows = pred_out.shape[1]

    def pred_copy(i):
        return remote(pred_out.at[i], pred_in.at[i], q_send, q_recv, tm=others[i])

    barrier = pltpu.get_barrier_semaphore()
    for to in others:
        pl.semaphore_signal(barrier, inc=1, device_id={"tm": to}, device_id_type=MESH)
    pl.semaphore_signal(barrier, inc=1, device_id={"vox": mate}, device_id_type=MESH)
    pl.semaphore_signal(barrier, inc=1, device_id={"vox": partner}, device_id_type=MESH)

    @pl.when(is_mid)
    def _():
        pl.semaphore_signal(barrier, inc=1, device_id={"vox": v + 2 * inward}, device_id_type=MESH)

    y_copy = pltpu.make_async_copy(y_hbm, y_buf, in_sem.at[0])
    sing_copy = pltpu.make_async_copy(sing_hbm, sing_buf, in_sem.at[1])
    x_copy = pltpu.make_async_copy(x_hbm, x_buf, in_sem.at[2])
    owners = (diag, near[0], near[1], t)
    y_copy.start()
    for i in range(4):
        u_copy(i).start()
    sing_copy.start()
    scalars = [
        pltpu.make_async_copy(live_hbm, live_ref, in_sem.at[3]),
        pltpu.make_async_copy(index_hbm, index_ref, in_sem.at[4]),
        pltpu.make_async_copy(lambda_hbm, lambda_ref, in_sem.at[5]),
    ]
    for copy in scalars:
        copy.start()

    with scope("bar"):
        pl.semaphore_wait(barrier, jnp.where(is_end, 5, 6))

    @pl.when(is_mid)
    def _():
        across_copy().start()
        side_copy(whole, side_recv.at[0]).start()

    @pl.when(is_end)
    def _():
        side_copy(side_pieces[0], side_recv.at[0]).start()

    u_copy(4).start()

    for copy in scalars:
        copy.wait()
    pick = one_hot(live_ref, cap)
    lam = [lambda_ref[index_ref[i]] for i in range(blocks)]
    slot_lam = [sum(pick[j][i] * lam[i] for i in range(blocks)) for j in range(cap)]
    slot_live = [sum(pick[j][i] for i in range(blocks)) for j in range(cap)]

    with scope("ycp"):
        y_copy.wait()
    y_cols = [y_buf[:, i * BLK : (i + 1) * BLK].astype(jnp.float32) for i in range(blocks)]
    y_t = jnp.concatenate(
        [sum(pick[j][i] * y_cols[i] for i in range(blocks)).T for j in range(cap)], axis=0
    ).astype(jnp.bfloat16)

    def make_parts(o):
        if o == 1:
            u_copy(4).wait()
        for i in range(4):
            if o == 0:
                u_copy(i).wait()
            for tile in range(share // TILE):
                into = slice(tile * TILE, (tile + 1) * TILE)
                start = rounds[o] * span + owners[i] * share + tile * TILE
                cols = pl.ds(pl.multiple_of(start, TILE), TILE)
                value = jnp.dot(y_t, u_buf[:, cols], preferred_element_type=jnp.float32)
                first, second = value[:BLK], value[BLK:]
                if i == 0:
                    part_out[o, 0, 1, :, into] = first.astype(jnp.bfloat16)
                    part_out[o, 1, 1, :, into] = second.astype(jnp.bfloat16)
                elif i == 1:
                    part_out[o, 0, 0, :, into] = first.astype(jnp.bfloat16)
                    own[o, 1, 1, :, into] = second
                elif i == 2:
                    own[o, 0, 1, :, into] = first
                    part_out[o, 1, 0, :, into] = second.astype(jnp.bfloat16)
                else:
                    own[o, 0, 0, :, into] = first
                    own[o, 1, 0, :, into] = second
            if o == 0 and i == 0:
                for j in range(2):
                    part_copy(o, j, 1).start()
            if o == 0 and i in (1, 2):
                part_copy(o, i - 1, 0).start()

    def combine(o):
        for j in range(2):
            part_copy(o, j, 1).wait_recv()
            comb_out[o, j] = (own[o, j, 1] + part_in[o, j, 1].astype(jnp.float32)).astype(jnp.bfloat16)
            comb_copy(o, j).start()

    def filter_parts(o):
        place = pl.multiple_of(rounds[o] * span + t * share, share)
        sing = sing_buf[:, pl.ds(place, share)]
        for j in range(cap):
            part_copy(o, j, 0).wait_recv()
            comb_copy(o, j).wait_recv()
            total = own[o, j, 0] + part_in[o, j, 0].astype(jnp.float32) + comb_in[o, j].astype(jnp.float32)
            factor = sing / (sing * sing + slot_lam[j]) * slot_live[j]
            filt[o, rank(t), half(j)] = (total * factor).T.astype(jnp.bfloat16)

    def send_filt(o):
        for i in range(2):
            ag_copy(o, i, t).start()

    def forward_filt(o):
        for i in range(2):
            ag_copy(o, i, near[i]).wait_recv()
        for i in range(2):
            hand_copy(o, i, near[1 - i]).start()

    def await_filt(o):
        for i in range(2):
            hand_copy(o, i, diag).wait_recv()

    with scope("mp0"):
        make_parts(0)
    with scope("mp1"):
        make_parts(1)
    pair_copy(0).start()
    own_copy().start()
    x_copy.start()
    sing_copy.wait()

    def near_product(o, rows):
        return jnp.dot(v_all[near_round, rows, :], filt[o], preferred_element_type=jnp.float32)

    def far_product(rows, factors):
        return jnp.dot(v_all[1 - near_round, rows, :], factors, preferred_element_type=jnp.float32)

    def near_rows(o):
        own_copy().wait()
        pair_wait(0)
        pair_wait(1)
        for i in range(4):
            rows = pl.ds(i * (rows_v // 4), rows_v // 4)
            acc[rows, :] = near_product(o, rows)

    def predict(piece):
        rows = pl.ds(*piece)
        part = jnp.dot(x_buf[:, rows], w_buf[rows, :], preferred_element_type=jnp.float32)
        if piece[0] == 0:
            pred_acc[...] = part
        else:
            pred_acc[...] += part

    def predict_last(piece):
        rows = pl.ds(*piece)
        for i, to in enumerate([diag, near[0], near[1], t]):
            mine = pl.ds(pl.multiple_of(to * test_rows, test_rows), test_rows)
            part = jnp.dot(x_buf[mine, rows], w_buf[rows, :], preferred_element_type=jnp.float32)
            if i < 3:
                k = (2, 0, 1)[i]
                pred_out[k] = (pred_acc[mine, :] + part).astype(jnp.bfloat16)
                pred_copy(k).start()
            else:
                pred_acc[mine, :] += part

    def put_rows(piece):
        rows = pl.ds(*piece)
        for i, block in enumerate(widen(pick, w_buf[rows, :].astype(jnp.float32))):
            w_ref[rows, i * BLK : (i + 1) * BLK] = block.astype(jnp.bfloat16)

    head = (0, far_pieces[3][0])
    rest = (head[1], rows_v - head[1])
    tail = (far_pieces[-2][0], far_pieces[-2][1] + far_pieces[-1][1])

    @pl.when(is_mid)
    def _():
        def arrive(i):
            line_relay_wait(i)
            pair_far_copy(i).start()

        def help_end(i):
            pair_far_wait(i)
            far_out[rows_of(i), :] = far_product(rows_of(i), far_filt[...]).astype(jnp.bfloat16)
            far_copy(i).start()

        def own_rows(piece):
            rows = pl.ds(*piece)
            w_buf[rows, :] = (acc[rows, :] + far_product(rows, filt[1])).astype(jnp.bfloat16)

        with scope("m_comb0"):
            combine(0)
            for s in (1, 0):
                for j in range(2):
                    part_copy(1, j, s).start()
        with scope("m_filt0"):
            filter_parts(0)
            send_filt(0)
        with scope("m_side0"):
            side_wait(side_pieces[0], side_recv.at[0])
            for i in range(2):
                line_relay(i).start()
        with scope("m_comb1"):
            combine(1)
        with scope("m_ff0"):
            far_filt_wait(0)
            for i in range(2):
                cross_copy(0, i, t).start()
        with scope("m_fw0"):
            forward_filt(0)
        with scope("m_across"):
            across_wait()
            pair_copy(2).start()
        with scope("m_ff1"):
            for k in (1, 2):
                far_filt_wait(k)
            for i in range(2):
                cross_copy(1, i, near[1 - i]).start()
        with scope("m_filt1"):
            filter_parts(1)
            send_filt(1)
        with scope("m_far0"):
            arrive(0)
        with scope("m_side1"):
            side_wait(side_pieces[1], side_recv.at[1])
            line_relay(2).start()
        with scope("m_cross"):
            for i in range(2):
                cross_copy(0, i, near[i]).wait_recv()
                cross_copy(1, i, diag).wait_recv()
        pair_wait(2)
        with scope("m_help0"):
            help_end(0)
        with scope("m_side2"):
            side_wait(side_pieces[2], side_recv.at[2])
            for i in range(3, count):
                line_relay(i).start()
            pair_copy(1).start()
        with scope("m_far1"):
            arrive(1)
        with scope("m_help1"):
            help_end(1)
        with scope("m_fw1"):
            forward_filt(1)
        with scope("m_aw0"):
            await_filt(0)
        with scope("m_near"):
            near_rows(0)
        with scope("m_far2"):
            arrive(2)
        with scope("m_help2"):
            help_end(2)
        with scope("m_aw1"):
            await_filt(1)
        x_copy.wait()
        with scope("m_own0"):
            for i in range(3):
                own_rows(far_pieces[i])
        with scope("m_far3"):
            arrive(3)
        with scope("m_far4"):
            arrive(4)
        with scope("m_help3"):
            help_end(3)
        with scope("m_far5"):
            arrive(5)
        with scope("m_pred0"):
            predict(head)
        with scope("m_help4"):
            help_end(4)
        with scope("m_help5"):
            help_end(5)
        with scope("m_last"):
            own_rows(rest)
            predict_last(rest)
        put_rows(whole)

    @pl.when(is_end)
    def _():
        with scope("e_comb0"):
            combine(0)
            for j in range(2):
                part_copy(1, j, 1).start()
        with scope("e_filt0"):
            filter_parts(0)
            far_filt_copy(0).start()
            for i in range(2):
                half_copy(i, t).start()
            for j in range(2):
                part_copy(1, j, 0).start()
        with scope("e_half"):
            for i in range(2):
                half_copy(i, near[i]).wait_recv()
                far_filt_copy(1 + i).start()
            for i in range(1, len(side_pieces)):
                side_copy(side_pieces[i], side_recv.at[i]).start()
        with scope("e_comb1"):
            combine(1)
        with scope("e_filt1"):
            filter_parts(1)
            send_filt(1)
        with scope("e_side"):
            side_wait(whole, side_recv.at[0])
            pair_copy(1).start()
        with scope("e_fw1"):
            forward_filt(1)
        x_copy.wait()
        with scope("e_aw1"):
            await_filt(1)
        with scope("e_near"):
            near_rows(1)
        for i in range(count):
            with scope(f"e_far{i}"):
                far_copy(i).wait_recv()
            rows = rows_of(i)
            w_buf[rows, :] = (acc[rows, :] + far_in[rows, :].astype(jnp.float32)).astype(jnp.bfloat16)
            if i < count - 2:
                predict(far_pieces[i])
                put_rows(far_pieces[i])
        with scope("e_last"):
            predict_last(tail)
            put_rows(tail)

    with scope("pwait"):
        remote(pred_in, pred_in, q_send, q_recv, vox=mate).wait_recv()
    total = pred_acc[pl.ds(pl.multiple_of(t * test_rows, test_rows), test_rows), :]
    for i in range(3):
        total = total + pred_in[i].astype(jnp.float32)
    total = total.astype(jnp.bfloat16).astype(jnp.float32)
    for i, block in enumerate(widen(pick, total)):
        pred_ref[:, i * BLK : (i + 1) * BLK] = block.astype(jnp.bfloat16)

    def sent(ref, sem):
        remote(ref, ref, sem, q_recv, vox=mate).wait_send()

    with scope("drain"):
        sent(part_out, part_send)
        sent(comb_out, comb_send)
        sent(pred_out, q_send)
        sent(v_all.at[0, :, pl.ds(0, depth)], line_send.at[0])
        for k in range(2):
            sent(v_all.at[0, :, pl.ds(0, depth)], pair_send.at[k])

        @pl.when(is_mid)
        def _():
            for k in range(1, 3):
                sent(v_all.at[0, :, pl.ds(0, depth)], line_send.at[k])
                sent(v_all.at[0, :, pl.ds(0, depth)], pair_send.at[k + 1])
            sent(filt.at[0], ag_send)
            sent(filt.at[0, pl.ds(0, 2 * share)], hand_send)
            sent(far_filt.at[pl.ds(0, 2 * share)], plane_send)
            sent(far_out, help_send)

        @pl.when(is_end)
        def _():
            sent(filt.at[0, pl.ds(0, 2 * share)], ag_send)
            sent(filt.at[0, pl.ds(0, share)], hand_send)
            sent(filt.at[0, pl.ds(0, share)], plane_send)
            sent(filt.at[0, pl.ds(0, 2 * share)], help_send)


def put_out(w_in, pred_in, w_ref, pred_ref, sem):
    copies = [
        pltpu.make_async_copy(w_in, w_ref, sem.at[0]),
        pltpu.make_async_copy(pred_in, pred_ref, sem.at[1]),
    ]
    for copy in copies:
        copy.start()
    for copy in copies:
        copy.wait()


def plane_body(u_train, y_train, sing, lambdas, lam_index, live, v_basis, x_test):
    time_rows, features = u_train.shape
    columns = y_train.shape[1]
    blocks = lam_index.shape[0]
    cap = blocks - blocks // 3
    used = cap * BLK
    rows_v, depth = v_basis.shape
    tests = x_test.shape[0]
    share = depth
    count = len(FAR_PARTS)
    low, full = jnp.bfloat16, jnp.float32
    vmem = pl.BlockSpec(memory_space=pltpu.VMEM)
    anywhere = pl.BlockSpec(memory_space=pl.ANY)
    dma = pltpu.SemaphoreType.DMA
    weights, predicted = pl.pallas_call(
        functools.partial(plane_kernel, cap),
        out_shape=(pltpu.VMEM((rows_v, columns), low), pltpu.VMEM((tests // 4, columns), low)),
        in_specs=[anywhere] * 8,
        out_specs=(vmem, vmem),
        scratch_shapes=[
            pltpu.SMEM(live.shape, live.dtype),
            pltpu.SMEM(lam_index.shape, lam_index.dtype),
            pltpu.SMEM(lambdas.shape, lambdas.dtype),
            pltpu.VMEM((1, features), full),
            pltpu.VMEM((time_rows, columns), low),
            pltpu.VMEM((time_rows, features), low),
            pltpu.VMEM((tests, rows_v), low),
            pltpu.VMEM((2, rows_v, 4 * depth), low),
            pltpu.VMEM((2, 2, 2, BLK, share), low),
            pltpu.VMEM((2, 2, 2, BLK, share), low),
            pltpu.VMEM((2, 2, 2, BLK, share), full),
            pltpu.VMEM((2, 2, BLK, share), low),
            pltpu.VMEM((2, 2, BLK, share), low),
            pltpu.VMEM((2, 4 * share, used), low),
            pltpu.VMEM((4 * share, used), low),
            pltpu.VMEM((rows_v, used), full),
            pltpu.VMEM((tests, used), full),
            pltpu.VMEM((rows_v, used), low),
            pltpu.VMEM((rows_v, used), low),
            pltpu.VMEM((3, tests // 4, used), low),
            pltpu.VMEM((3, tests // 4, used), low),
            pltpu.VMEM((rows_v, used), low),
            dma((6,)),
            dma((5,)),
            dma,
            dma((3,)),
            dma((len(SIDE_PARTS),)),
            dma,
            dma((count,)),
            dma((4,)),
            dma((3,)),
            dma((count,)),
            dma,
            dma((2, 2, 2)),
            dma,
            dma((2, 2)),
            dma,
            dma((2, 2)),
            dma,
            dma((2, 2)),
            dma,
            dma((2, 2)),
            dma,
            dma((count,)),
            dma,
            dma,
        ],
        compiler_params=pltpu.CompilerParams(
            collective_id=1, has_side_effects=True
        ),
    )(live, lam_index, lambdas, sing.reshape(1, features), y_train, u_train, v_basis, x_test)
    weights = pltpu.with_memory_space_constraint(weights, pltpu.VMEM)
    predicted = pltpu.with_memory_space_constraint(predicted, pltpu.VMEM)
    return pl.pallas_call(
        put_out,
        out_shape=(
            jax.ShapeDtypeStruct((rows_v, columns), low),
            jax.ShapeDtypeStruct((tests // 4, columns), low),
        ),
        in_specs=[anywhere, anywhere],
        out_specs=(anywhere, anywhere),
        scratch_shapes=[dma((2,))],
    )(weights, predicted)


def routed(n_t, n_v, *args):
    if (n_t, n_v, args[4].shape[0]) == (4, 8, 3):
        return plane_body(*args)
    return body(n_t, n_v, *args)


def solution(mesh):
    placed = (
        P("tm", None),
        P("tm", "vox"),
        P(),
        P(),
        P("vox"),
        P("vox"),
        P("tm", "vox"),
        P(None, "tm"),
    )
    return jax.shard_map(
        functools.partial(routed, mesh.shape["tm"], mesh.shape["vox"]),
        mesh=mesh,
        in_specs=placed,
        out_specs=(P("tm", "vox"), P("tm", "vox")),
        check_vma=False,
    )
```

```python
import functools

import jax
import jax.numpy as jnp
from jax import lax
from jax.experimental import pallas as pl
from jax.experimental.pallas import tpu as pltpu
from jax.sharding import PartitionSpec as P

BLK = 128
CHUNKS = 4
TILE = 256
MESH = pl.DeviceIdType.MESH


def one_hot(live_ref, cap):
    blocks = live_ref.shape[0]
    live = [live_ref[i] for i in range(blocks)]
    before = [sum(live[:i], jnp.int32(0)) for i in range(blocks)]
    return [
        [jnp.where(before[i] == j, live[i], 0).astype(jnp.float32) for i in range(blocks)]
        for j in range(cap)
    ]


def expand(cap, live_ref, w_in, pred_in, w_ref, pred_ref):
    pick = one_hot(live_ref, cap)
    for source, target in ((w_in, w_ref), (pred_in, pred_ref)):
        values = [source[:, j * BLK : (j + 1) * BLK].astype(jnp.float32) for j in range(cap)]
        for i in range(live_ref.shape[0]):
            block = sum(pick[j][i] * values[j] for j in range(cap))
            target[:, i * BLK : (i + 1) * BLK] = block.astype(target.dtype)


def kernel(
    n_t,
    n_v,
    cap,
    live_ref,
    index_ref,
    lambda_ref,
    sing_ref,
    y_ref,
    u_ref,
    v_ref,
    x_ref,
    w_ref,
    pred_ref,
    u_buf,
    x_buf,
    v_all,
    part_out,
    part_in,
    part_own,
    filt,
    acc,
    pred_acc,
    pred_out,
    pred_in,
    u_sem,
    x_sem,
    own_sem,
    right_sem,
    left_sem,
    line_sem,
    pair_send,
    pair_recv,
    rs_send,
    rs_recv,
    ag_send,
    ag_recv,
    q_send,
    q_recv,
    far_filt,
    far_out,
    far_in,
    far_filt_send,
    far_filt_recv,
    far_send,
    far_recv,
    hand_send,
    hand_recv,
):
    t = lax.axis_index("tm")
    v = lax.axis_index("vox")
    n_z = n_v // 2
    z, core = v // 2, v % 2
    mate = z * 2 + 1 - core
    rows_v, depth = v_ref.shape
    blocks = live_ref.shape[0]
    share = part_own.shape[2]
    half = n_z // 2
    span = n_t * share
    first_round = jnp.where(z < half, 1, 0)
    at_low, at_high = z == 0, z == n_z - 1
    is_end = at_low | at_high
    is_helper = (z == 1) | (z == n_z - 2)

    def holds(zz, src):
        return jnp.logical_not(
            ((zz == 0) & (src >= half)) | ((zz == n_z - 1) & (src < half))
        )
    test_rows = pred_out.shape[1]
    rc = rows_v // CHUNKS

    def u_copy(r, owner):
        cols = pl.ds(pl.multiple_of(r * span + owner * share, share), share)
        return pltpu.make_async_copy(u_ref.at[:, cols], u_buf.at[:, cols], u_sem.at[r, owner])

    def own_copy(ch):
        rows = pl.ds(ch * rc, rc)
        return pltpu.make_async_copy(v_ref.at[rows], v_all.at[v, rows], own_sem.at[ch])

    def line_copy(src, ch, step, first=False):
        rows = pl.ds(ch * rc, rc)
        slot = src * 2 + core
        return pltpu.make_async_remote_copy(
            src_ref=v_ref.at[rows] if first else v_all.at[slot, rows],
            dst_ref=v_all.at[slot, rows],
            send_sem=(right_sem if step > 0 else left_sem).at[src, ch],
            recv_sem=line_sem.at[src, ch],
            device_id={"vox": v + 2 * step},
            device_id_type=MESH,
        )

    def pair_copy(src, ch, first=False):
        rows = pl.ds(ch * rc, rc)
        slot = src * 2 + core
        return pltpu.make_async_remote_copy(
            src_ref=v_ref.at[rows] if first else v_all.at[slot, rows],
            dst_ref=v_all.at[slot, rows],
            send_sem=pair_send.at[src, ch],
            recv_sem=pair_recv.at[src, ch],
            device_id={"vox": mate},
            device_id_type=MESH,
        )

    def pair_arrival(src, ch):
        rows = pl.ds(ch * rc, rc)
        slot = src * 2 + 1 - core
        return pltpu.make_async_remote_copy(
            src_ref=v_all.at[slot, rows],
            dst_ref=v_all.at[slot, rows],
            send_sem=pair_send.at[src, ch],
            recv_sem=pair_recv.at[src, ch],
            device_id={"vox": mate},
            device_id_type=MESH,
        )

    def peer(d):
        return lax.rem(t + d, n_t)

    def part_copy(r, to, owner):
        return pltpu.make_async_remote_copy(
            src_ref=part_out.at[r, to],
            dst_ref=part_in.at[r, owner],
            send_sem=rs_send.at[r, to],
            recv_sem=rs_recv.at[r, owner],
            device_id={"tm": to},
            device_id_type=MESH,
        )

    def filt_copy(r, to, owner):
        return pltpu.make_async_remote_copy(
            src_ref=filt.at[r, owner],
            dst_ref=filt.at[r, owner],
            send_sem=ag_send.at[r, to],
            recv_sem=ag_recv.at[r, owner],
            device_id={"tm": to},
            device_id_type=MESH,
        )

    relayed = n_t == 4
    near = [t + 1 - 2 * lax.rem(t, 2), lax.rem(t + 2, n_t)] if relayed else [peer(d) for d in range(1, n_t)]

    def relay_copy(r, k, to, owner):
        rows = pl.ds(k * (filt.shape[2] // 2), filt.shape[2] // 2)
        return pltpu.make_async_remote_copy(
            src_ref=filt.at[r, owner, rows],
            dst_ref=filt.at[r, owner, rows],
            send_sem=hand_send.at[r, k],
            recv_sem=hand_recv.at[r, k],
            device_id={"tm": to},
            device_id_type=MESH,
        )

    def pred_copy(to, owner):
        return pltpu.make_async_remote_copy(
            src_ref=pred_out.at[to],
            dst_ref=pred_in.at[owner],
            send_sem=q_send.at[to],
            recv_sem=q_recv.at[owner],
            device_id={"tm": to},
            device_id_type=MESH,
        )

    inward = jnp.where(z < half, 1, -1)

    def far_filt_copy(j, step):
        rows = pl.ds(j * BLK, BLK)
        return pltpu.make_async_remote_copy(
            src_ref=filt.at[first_round, :, rows, :],
            dst_ref=far_filt.at[:, rows, :],
            send_sem=far_filt_send.at[j],
            recv_sem=far_filt_recv.at[j],
            device_id={"vox": v + 2 * step},
            device_id_type=MESH,
        )

    def far_copy(j, ch, step):
        rows = pl.ds(ch * rc, rc)
        return pltpu.make_async_remote_copy(
            src_ref=far_out.at[j, rows],
            dst_ref=far_in.at[j, rows],
            send_sem=far_send.at[j, ch],
            recv_sem=far_recv.at[j, ch],
            device_id={"vox": v + 2 * step},
            device_id_type=MESH,
        )

    rounds = (first_round, 1 - first_round)
    for r in rounds:
        for d in range(n_t):
            u_copy(r, peer((d + 1) % n_t)).start()

    barrier = pltpu.get_barrier_semaphore()
    for d in range(1, n_t):
        pl.semaphore_signal(barrier, inc=1, device_id={"tm": peer(d)}, device_id_type=MESH)
    pl.semaphore_signal(barrier, inc=1, device_id={"vox": mate}, device_id_type=MESH)

    @pl.when(z > 0)
    def _():
        pl.semaphore_signal(barrier, inc=1, device_id={"vox": v - 2}, device_id_type=MESH)

    @pl.when(z < n_z - 1)
    def _():
        pl.semaphore_signal(barrier, inc=1, device_id={"vox": v + 2}, device_id_type=MESH)

    neighbours = jnp.where(z > 0, 1, 0) + jnp.where(z < n_z - 1, 1, 0)
    pl.semaphore_wait(barrier, n_t + neighbours)

    for ch in range(CHUNKS):

        @pl.when(z > 0)
        def _():
            line_copy(z, ch, -1, True).start()

        @pl.when(z < n_z - 1)
        def _():
            line_copy(z, ch, 1, True).start()

    pick = one_hot(live_ref, cap)
    lam = [lambda_ref[index_ref[i]] for i in range(blocks)]
    slot_lam = [sum(pick[j][i] * lam[i] for i in range(blocks)) for j in range(cap)]
    slot_live = [sum(pick[j][i] for i in range(blocks)) for j in range(cap)]

    y_cols = [y_ref[:, i * BLK : (i + 1) * BLK].astype(jnp.float32) for i in range(blocks)]
    y_t = jnp.concatenate(
        [sum(pick[j][i] * y_cols[i] for i in range(blocks)).T for j in range(cap)], axis=0
    ).astype(jnp.bfloat16)

    def make_parts(r, send):
        for d in range(1, n_t + 1):
            to = peer(d % n_t)
            u_copy(r, to).wait()

            def tile(i, _, to=to, d=d):
                off = pl.multiple_of(i * TILE, TILE)
                cols = pl.ds(pl.multiple_of(r * span + to * share + i * TILE, TILE), TILE)
                value = jnp.dot(y_t, u_buf[:, cols], preferred_element_type=jnp.float32)
                if d < n_t:
                    part_out[r, to, :, pl.ds(off, TILE)] = value.astype(jnp.bfloat16)
                else:
                    part_own[r, :, pl.ds(off, TILE)] = value
                return 0

            lax.fori_loop(0, share // TILE, tile, 0)
            if send and d < n_t:
                part_copy(r, to, t).start()

    def send_parts(r):
        for d in range(1, n_t):
            part_copy(r, peer(d), t).start()

    def filter_parts(r):
        for d in range(1, n_t):
            part_copy(r, peer(d), peer(d)).wait_recv()
        for i in range(share // TILE):
            cols = slice(i * TILE, (i + 1) * TILE)
            place = pl.multiple_of(r * span + t * share + i * TILE, TILE)
            sing = sing_ref[:, pl.ds(place, TILE)]
            for j in range(cap):
                rows = slice(j * BLK, (j + 1) * BLK)
                total = part_own[r, rows, cols]
                for d in range(1, n_t):
                    total = total + part_in[r, peer(d), rows, cols].astype(jnp.float32)
                factor = sing / (sing * sing + slot_lam[j]) * slot_live[j]
                filt[r, t, rows, cols] = (total * factor).astype(jnp.bfloat16)
        for to in near:
            filt_copy(r, to, t).start()

    def forward_filt(r):
        for to in near:
            filt_copy(r, to, to).wait_recv()
        if relayed:
            for k in range(2):
                relay_copy(r, k, near[k], near[1 - k]).start()

    def await_filt(r):
        if relayed:
            for k in range(2):
                relay_copy(r, k, near[k], n_t - 1 - t).wait_recv()

    make_parts(rounds[0], True)

    for ch in range(CHUNKS):
        pair_copy(z, ch, True).start()
        own_copy(ch).start()
    x_copy = pltpu.make_async_copy(x_ref, x_buf, x_sem)
    x_copy.start()

    make_parts(rounds[1], False)

    def relay(s, ch):
        low, high = z - 1 - s, z + 1 + s

        @pl.when((low >= 0) & holds(z, low))
        def _():
            line_copy(low, ch, -1).wait_recv()

            @pl.when((z < n_z - 1) & holds(z + 1, low))
            def _():
                line_copy(low, ch, 1).start()

            pair_copy(low, ch).start()

        @pl.when((high < n_z) & holds(z, high))
        def _():
            line_copy(high, ch, 1).wait_recv()

            @pl.when((z > 0) & holds(z - 1, high))
            def _():
                line_copy(high, ch, -1).start()

            pair_copy(high, ch).start()

    def product(values, slot, rows, factors):
        return lax.dot_general(
            values[slot, rows, :], factors, (((1,), (1,)), ((), ())),
            preferred_element_type=jnp.float32,
        )

    def place_of(slot):
        start = lax.rem(slot * depth, span)
        owner = start // share
        return owner, pl.ds(pl.multiple_of(start - owner * share, depth), depth)

    base = jnp.where(z == 1, half, 0) * 2

    def settle(ch):
        own_copy(ch).wait()

        def step(src, _):
            @pl.when(holds(z, src))
            def _():
                pair_arrival(src, ch).wait_recv()

            return 0

        lax.fori_loop(0, n_z, step, 0)

    def add_round(r, ch):
        rows = pl.ds(ch * rc, rc)

        def step(i, value):
            slot = r * half * 2 + i
            owner, inner = place_of(slot)
            return value + product(v_all, slot, rows, filt[r, owner, :, inner])

        value = jnp.zeros((rc, acc.shape[1]), jnp.float32)
        for i in range(2 * half):
            value = step(i, value)
        return value

    def far_half(ch):
        rows = pl.ds(ch * rc, rc)

        @pl.when(jnp.logical_not(is_end))
        def _():
            acc[rows, :] = add_round(rounds[0], ch)

        @pl.when(is_end)
        def _():
            acc[rows, :] = jnp.zeros((rc, acc.shape[1]), jnp.float32)

    def help_end(j, chunks):
        cols = slice(j * BLK, (j + 1) * BLK)

        @pl.when(is_helper)
        def _():
            if chunks[0] == 0:
                far_filt_copy(j, -inward).wait_recv()
            for ch in chunks:
                rows = pl.ds(ch * rc, rc)
                value = jnp.zeros((rc, BLK), jnp.float32)
                for i in range(2 * half):
                    owner, inner = place_of(base + i)
                    value += product(v_all, base + i, rows, far_filt[owner, cols, inner])
                far_out[j, rows, :] = value.astype(jnp.bfloat16)
                far_copy(j, ch, -inward).start()

    early, last = CHUNKS // 2, CHUNKS - 1
    for ch in range(early):
        relay(0, ch)
    filter_parts(rounds[0])
    for ch in range(early, last):
        relay(0, ch)
    forward_filt(rounds[0])
    send_parts(rounds[1])
    relay(0, last)
    await_filt(rounds[0])

    @pl.when(is_end)
    def _():
        for j in range(cap):
            far_filt_copy(j, inward).start()

    def relay_step(s, _):
        for ch in range(CHUNKS):
            relay(s, ch)
        return 0

    lax.fori_loop(1, n_z - 3, relay_step, 0)
    for ch in range(early):
        relay(n_z - 3, ch)
    filter_parts(rounds[1])
    for ch in range(early, last):
        relay(n_z - 3, ch)
    for ch in range(early):
        settle(ch)
        far_half(ch)
    forward_filt(rounds[1])
    for ch in range(early, last):
        settle(ch)
        far_half(ch)
    help_end(0, list(range(last)))
    relay(n_z - 3, last)
    settle(last)
    help_end(0, [last])
    far_half(last)
    help_end(1, list(range(CHUNKS)))
    for j in range(2, cap):
        help_end(j, list(range(CHUNKS)))
    await_filt(rounds[1])
    x_copy.wait()

    def finish(ch):
        rows = slice(ch * rc, (ch + 1) * rc)
        acc[rows, :] += add_round(rounds[1], ch)

        @pl.when(is_end)
        def _():
            for j in range(cap):
                cols = slice(j * BLK, (j + 1) * BLK)
                far_copy(j, ch, inward).wait_recv()
                acc[rows, cols] += far_in[j, rows, :].astype(jnp.float32)

        weights = acc[rows, :].astype(jnp.bfloat16)
        w_ref[rows, :] = weights
        value = jnp.dot(x_buf[:, rows], weights, preferred_element_type=jnp.float32)
        if ch == 0:
            pred_acc[...] = value
        else:
            pred_acc[...] += value

    for ch in range(CHUNKS):
        finish(ch)

    for d in range(1, n_t):
        to = peer(d)
        mine = pl.ds(pl.multiple_of(to * test_rows, test_rows), test_rows)
        pred_out[to] = pred_acc[mine, :].astype(jnp.bfloat16)
        pred_copy(to, t).start()
    for d in range(1, n_t):
        pred_copy(peer(d), peer(d)).wait_recv()
    total = pred_acc[pl.ds(pl.multiple_of(t * test_rows, test_rows), test_rows), :]
    for d in range(1, n_t):
        total = total + pred_in[peer(d)].astype(jnp.float32)
    pred_ref[...] = total.astype(jnp.bfloat16)

    for d in range(1, n_t):
        for r in rounds:
            part_copy(r, peer(d), t).wait_send()
        pred_copy(peer(d), t).wait_send()
    for r in rounds:
        for to in near:
            filt_copy(r, to, t).wait_send()
        if relayed:
            for k in range(2):
                relay_copy(r, k, near[k], near[1 - k]).wait_send()

    @pl.when(is_end)
    def _():
        for j in range(cap):
            far_filt_copy(j, inward).wait_send()

    @pl.when(is_helper)
    def _():
        for j in range(cap):
            for ch in range(CHUNKS):
                far_copy(j, ch, -inward).wait_send()

    def drain(src, _):
        for ch in range(CHUNKS):

            @pl.when(holds(z, src))
            def _():
                pair_copy(src, ch).wait_send()

            @pl.when((src <= z) & (z < n_z - 1) & holds(z, src) & holds(z + 1, src))
            def _():
                line_copy(src, ch, 1).wait_send()

            @pl.when((src >= z) & (z > 0) & holds(z, src) & holds(z - 1, src))
            def _():
                line_copy(src, ch, -1).wait_send()

        return 0

    lax.fori_loop(0, n_z, drain, 0)


def body(n_t, n_v, u_train, y_train, sing, lambdas, lam_index, live, v_basis, x_test):
    time_rows, features = u_train.shape
    columns = y_train.shape[1]
    blocks = lam_index.shape[0]
    cap = blocks - blocks // 3
    used = cap * BLK
    rows_v, depth = v_basis.shape
    tests = x_test.shape[0]
    share = features // n_t // 2
    n_z = n_v // 2
    low, full = jnp.bfloat16, jnp.float32
    smem = pl.BlockSpec(memory_space=pltpu.SMEM)
    vmem = pl.BlockSpec(memory_space=pltpu.VMEM)
    anywhere = pl.BlockSpec(memory_space=pl.ANY)
    dma = pltpu.SemaphoreType.DMA
    weights, predicted = pl.pallas_call(
        functools.partial(kernel, n_t, n_v, cap),
        out_shape=(
            jax.ShapeDtypeStruct((rows_v, used), low),
            jax.ShapeDtypeStruct((tests // n_t, used), low),
        ),
        in_specs=[smem, smem, smem, vmem, vmem, anywhere, anywhere, anywhere],
        out_specs=(vmem, vmem),
        scratch_shapes=[
            pltpu.VMEM((time_rows, features), low),
            pltpu.VMEM((tests, rows_v), low),
            pltpu.VMEM((n_v, rows_v, depth), low),
            pltpu.VMEM((2, n_t, used, share), low),
            pltpu.VMEM((2, n_t, used, share), low),
            pltpu.VMEM((2, used, share), full),
            pltpu.VMEM((2, n_t, used, share), low),
            pltpu.VMEM((rows_v, used), full),
            pltpu.VMEM((tests, used), full),
            pltpu.VMEM((n_t, tests // n_t, used), low),
            pltpu.VMEM((n_t, tests // n_t, used), low),
            dma((2, n_t)),
            dma,
            dma((CHUNKS,)),
            dma((n_z, CHUNKS)),
            dma((n_z, CHUNKS)),
            dma((n_z, CHUNKS)),
            dma((n_z, CHUNKS)),
            dma((n_z, CHUNKS)),
            dma((2, n_t)),
            dma((2, n_t)),
            dma((2, n_t)),
            dma((2, n_t)),
            dma((n_t,)),
            dma((n_t,)),
            pltpu.VMEM((n_t, used, share), low),
            pltpu.VMEM((cap, rows_v, BLK), low),
            pltpu.VMEM((cap, rows_v, BLK), low),
            dma((cap,)),
            dma((cap,)),
            dma((cap, CHUNKS)),
            dma((cap, CHUNKS)),
            dma((2, 2)),
            dma((2, 2)),
        ],
        compiler_params=pltpu.CompilerParams(collective_id=0, has_side_effects=True),
    )(live, lam_index, lambdas, sing.reshape(1, features), y_train, u_train, v_basis, x_test)
    return pl.pallas_call(
        functools.partial(expand, cap),
        out_shape=(
            jax.ShapeDtypeStruct((rows_v, columns), low),
            jax.ShapeDtypeStruct((tests // n_t, columns), low),
        ),
        in_specs=[smem, vmem, vmem],
        out_specs=(vmem, vmem),
    )(live, weights, predicted)


FAR_PARTS = (4, 4, 4, 8, 16, 32, 32)
SIDE_PARTS = (2, 4, 4)


def row_pieces(rows, parts):
    pieces, start = [], 0
    for part in parts:
        pieces.append((start, rows // part))
        start += rows // part
    return pieces


def widen(pick, values):
    wide = [values[:, j * BLK : (j + 1) * BLK] for j in range(len(pick))]
    return [sum(pick[j][i] * wide[j] for j in range(len(pick))) for i in range(len(pick[0]))]


def plane_kernel(
    cap,
    live_hbm,
    index_hbm,
    lambda_hbm,
    sing_hbm,
    y_hbm,
    u_hbm,
    v_hbm,
    x_hbm,
    w_ref,
    pred_ref,
    live_ref,
    index_ref,
    lambda_ref,
    sing_buf,
    y_buf,
    u_buf,
    x_buf,
    v_all,
    part_out,
    part_in,
    own,
    comb_out,
    comb_in,
    filt,
    far_filt,
    acc,
    pred_acc,
    far_out,
    far_in,
    pred_out,
    pred_in,
    lent,
    w_buf,
    in_sem,
    u_sem,
    own_sem,
    line_send,
    side_recv,
    across_recv,
    relay_recv,
    pair_send,
    pair_recv,
    pair_far_recv,
    part_send,
    part_recv,
    comb_send,
    comb_recv,
    ag_send,
    ag_recv,
    hand_send,
    hand_recv,
    plane_send,
    plane_recv,
    help_send,
    help_recv,
    q_send,
    q_recv,
    lend_recv,
):
    t = lax.axis_index("tm")
    v = lax.axis_index("vox")
    z, core = v // 2, v % 2
    mate = z * 2 + 1 - core
    rows_v, depth = v_hbm.shape
    blocks = live_ref.shape[0]
    share = depth
    span = 4 * share
    far_pieces = row_pieces(rows_v, FAR_PARTS)
    side_pieces = row_pieces(rows_v, SIDE_PARTS)
    whole = (0, rows_v)
    count = len(far_pieces)
    low_side = z < 2
    inward = jnp.where(low_side, 1, -1)
    is_end = (z == 0) | (z == 3)
    is_mid = jnp.logical_not(is_end)
    partner_z = jnp.where(is_end, z + inward, z - inward)
    partner = partner_z * 2 + core
    near_round = z // 2
    rounds = (1 - z % 2, z % 2)
    near = [t + 1 - 2 * lax.rem(t, 2), lax.rem(t + 2, 4)]
    diag = 3 - t
    scope = jax.named_scope

    def remote(src, dst, send, recv, **place):
        return pltpu.make_async_remote_copy(
            src_ref=src, dst_ref=dst, send_sem=send, recv_sem=recv, device_id=place, device_id_type=MESH
        )

    def slot_of(zz, cc):
        return zz * 2 + cc

    def block_of(slot, piece):
        cols = pl.ds(pl.multiple_of((slot % 4) * depth, depth), depth)
        return v_all.at[slot // 4, pl.ds(*piece), cols]

    far_mid, far_end = 3 - z, 3 - partner_z
    across_mate = (z + inward) * 2 + 1 - core

    def side_copy(piece, recv):
        return remote(v_hbm.at[pl.ds(*piece)], block_of(v, piece), line_send.at[0], recv, vox=partner)

    def side_wait(piece, recv):
        at = block_of(partner, piece)
        remote(at, at, line_send.at[0], recv, vox=partner).wait_recv()

    def across_copy():
        return remote(v_hbm, block_of(v, whole), line_send.at[1], across_recv, vox=v + 2 * inward)

    def across_wait():
        at = block_of(slot_of(far_mid, core), whole)
        remote(at, at, line_send.at[1], across_recv, vox=v + 2 * inward).wait_recv()

    def line_relay(i):
        at = block_of(partner, far_pieces[i])
        return remote(at, at, line_send.at[2], relay_recv.at[i], vox=v + 2 * inward)

    direct = (count - 2, count - 1)
    direct_rows = rows_v - far_pieces[direct[0]][0]

    def line_relay_other(i):
        at = block_of(partner, far_pieces[i])
        return remote(at, at, line_send.at[3], pair_far_recv.at[i], vox=across_mate)

    def line_relay_wait(i):
        at = block_of(slot_of(far_end, core), far_pieces[i])
        remote(at, at, line_send.at[2], relay_recv.at[i], vox=v + 2 * inward).wait_recv()

    def pair_copy(k):
        src = v_hbm if k == 0 else block_of(pair_slot(k, core), whole)
        return remote(src, block_of(pair_slot(k, core), whole), pair_send.at[k], pair_recv.at[k], vox=mate)

    def pair_slot(k, cc):
        return slot_of((z, partner_z, far_mid)[k], cc)

    def pair_wait(k):
        at = block_of(pair_slot(k, 1 - core), whole)
        remote(at, at, pair_send.at[k], pair_recv.at[k], vox=mate).wait_recv()

    def pair_far_copy(i):
        at = block_of(slot_of(far_end, core), far_pieces[i])
        return remote(at, at, pair_send.at[3], pair_far_recv.at[i], vox=mate)

    def pair_far_wait(i):
        at = block_of(slot_of(far_end, 1 - core), far_pieces[i])
        remote(at, at, pair_send.at[3], pair_far_recv.at[i], vox=mate).wait_recv()

    def own_copy():
        return pltpu.make_async_copy(v_hbm, block_of(v, whole), own_sem)

    def rows_of(i):
        return pl.ds(*far_pieces[i])

    def u_copy(i):
        first, width = (owners[i] * share, share) if i < 4 else (0, span)
        cols = pl.ds(pl.multiple_of(rounds[i // 4] * span + first, share), width)
        return pltpu.make_async_copy(u_hbm.at[:, cols], u_buf.at[:, cols], u_sem.at[i])

    def half(i):
        return pl.ds(i * BLK, BLK)

    def rank(owner):
        return pl.ds(pl.multiple_of(owner * share, share), share)

    def part_copy(o, j, s):
        return remote(part_out.at[o, j, s], part_in.at[o, j, s], part_send, part_recv.at[o, j, s], tm=near[j])

    def comb_copy(o, j):
        return remote(comb_out.at[o, j], comb_in.at[o, j], comb_send, comb_recv.at[o, j], tm=near[1 - j])

    def ag_copy(o, i, owner):
        at = filt.at[o, rank(owner)]
        return remote(at, at, ag_send, ag_recv.at[o, i], tm=near[i])

    def hand_copy(o, i, owner):
        at = filt.at[o, rank(owner), half(i)]
        return remote(at, at, hand_send, hand_recv.at[o, i], tm=near[i])

    def half_copy(i, owner):
        at = filt.at[0, rank(owner), half(i)]
        return remote(at, at, plane_send, plane_recv.at[0, i], tm=near[i])

    def far_filt_copy(k):
        if k == 0:
            src, dst = filt.at[0, rank(t)], far_filt.at[rank(t)]
        else:
            src, dst = filt.at[0, rank(near[k - 1]), half(k - 1)], far_filt.at[rank(near[k - 1]), half(k - 1)]
        return remote(src, dst, help_send, help_recv.at[k], vox=partner)

    def far_filt_wait(k):
        at = far_filt.at[rank(t)] if k == 0 else far_filt.at[rank(near[k - 1]), half(k - 1)]
        remote(at, at, help_send, help_recv.at[k], vox=partner).wait_recv()

    def cross_copy(s, i, owner):
        at = far_filt.at[rank(owner), half(1 - i)]
        return remote(at, at, plane_send, plane_recv.at[s, i], tm=near[i])

    def far_copy(ch):
        return remote(
            far_out.at[rows_of(ch)], far_in.at[rows_of(ch)], help_send, help_recv.at[ch], vox=partner
        )

    others = near + [diag]
    test_rows = pred_out.shape[1]
    strip = test_rows // 2

    def lend_copy(j, k):
        at = (pl.ds(k * strip, strip), half(j))
        return remote(pred_out.at[(2, *at)], lent.at[at], q_send, lend_recv.at[j, k], tm=near[j])

    def pred_copy(i, j, rows):
        at = (i, rows, half(j))
        return remote(pred_out.at[at], pred_in.at[at], q_send, q_recv, tm=near[i])

    barrier = pltpu.get_barrier_semaphore()
    for to in others:
        pl.semaphore_signal(barrier, inc=1, device_id={"tm": to}, device_id_type=MESH)
    pl.semaphore_signal(barrier, inc=1, device_id={"vox": mate}, device_id_type=MESH)
    pl.semaphore_signal(barrier, inc=1, device_id={"vox": partner}, device_id_type=MESH)

    @pl.when(is_mid)
    def _():
        for to in (v + 2 * inward, across_mate):
            pl.semaphore_signal(barrier, inc=1, device_id={"vox": to}, device_id_type=MESH)

    y_copy = pltpu.make_async_copy(y_hbm, y_buf, in_sem.at[0])
    sing_copy = pltpu.make_async_copy(sing_hbm, sing_buf, in_sem.at[1])
    x_copy = pltpu.make_async_copy(x_hbm, x_buf, in_sem.at[2])
    owners = (diag, near[0], near[1], t)
    y_copy.start()
    for i in range(4):
        u_copy(i).start()
    sing_copy.start()
    scalars = [
        pltpu.make_async_copy(live_hbm, live_ref, in_sem.at[3]),
        pltpu.make_async_copy(index_hbm, index_ref, in_sem.at[4]),
        pltpu.make_async_copy(lambda_hbm, lambda_ref, in_sem.at[5]),
    ]
    for copy in scalars:
        copy.start()

    with scope("bar"):
        pl.semaphore_wait(barrier, jnp.where(is_end, 5, 7))

    @pl.when(is_mid)
    def _():
        across_copy().start()
        side_copy(whole, side_recv.at[0]).start()

    @pl.when(is_end)
    def _():
        side_copy(side_pieces[0], side_recv.at[0]).start()

    u_copy(4).start()

    for copy in scalars:
        copy.wait()
    pick = one_hot(live_ref, cap)
    lam = [lambda_ref[index_ref[i]] for i in range(blocks)]
    slot_lam = [sum(pick[j][i] * lam[i] for i in range(blocks)) for j in range(cap)]
    slot_live = [sum(pick[j][i] for i in range(blocks)) for j in range(cap)]

    with scope("ycp"):
        y_copy.wait()
    y_cols = [y_buf[:, i * BLK : (i + 1) * BLK].astype(jnp.float32) for i in range(blocks)]
    y_t = jnp.concatenate(
        [sum(pick[j][i] * y_cols[i] for i in range(blocks)).T for j in range(cap)], axis=0
    ).astype(jnp.bfloat16)

    def make_parts(o):
        if o == 1:
            u_copy(4).wait()
        for i in range(4):
            if o == 0:
                u_copy(i).wait()
            for tile in range(share // TILE):
                into = slice(tile * TILE, (tile + 1) * TILE)
                start = rounds[o] * span + owners[i] * share + tile * TILE
                cols = pl.ds(pl.multiple_of(start, TILE), TILE)
                value = jnp.dot(y_t, u_buf[:, cols], preferred_element_type=jnp.float32)
                first, second = value[:BLK], value[BLK:]
                if i == 0:
                    part_out[o, 0, 1, :, into] = first.astype(jnp.bfloat16)
                    part_out[o, 1, 1, :, into] = second.astype(jnp.bfloat16)
                elif i == 1:
                    part_out[o, 0, 0, :, into] = first.astype(jnp.bfloat16)
                    own[o, 1, 1, :, into] = second
                elif i == 2:
                    own[o, 0, 1, :, into] = first
                    part_out[o, 1, 0, :, into] = second.astype(jnp.bfloat16)
                else:
                    own[o, 0, 0, :, into] = first
                    own[o, 1, 0, :, into] = second
            if o == 0 and i == 0:
                for j in range(2):
                    part_copy(o, j, 1).start()
            if o == 0 and i in (1, 2):
                part_copy(o, i - 1, 0).start()

    def combine(o):
        for j in range(2):
            part_copy(o, j, 1).wait_recv()
            comb_out[o, j] = (own[o, j, 1] + part_in[o, j, 1].astype(jnp.float32)).astype(jnp.bfloat16)
            comb_copy(o, j).start()

    def filter_parts(o):
        place = pl.multiple_of(rounds[o] * span + t * share, share)
        sing = sing_buf[:, pl.ds(place, share)]
        for j in range(cap):
            part_copy(o, j, 0).wait_recv()
            comb_copy(o, j).wait_recv()
            total = own[o, j, 0] + part_in[o, j, 0].astype(jnp.float32) + comb_in[o, j].astype(jnp.float32)
            factor = sing / (sing * sing + slot_lam[j]) * slot_live[j]
            filt[o, rank(t), half(j)] = (total * factor).T.astype(jnp.bfloat16)

    def send_filt(o):
        for i in range(2):
            ag_copy(o, i, t).start()

    def forward_filt(o):
        for i in range(2):
            ag_copy(o, i, near[i]).wait_recv()
        for i in range(2):
            hand_copy(o, i, near[1 - i]).start()

    def await_filt(o):
        for i in range(2):
            hand_copy(o, i, diag).wait_recv()

    with scope("mp0"):
        make_parts(0)
    with scope("mp1"):
        make_parts(1)
    pair_copy(0).start()
    own_copy().start()
    x_copy.start()
    sing_copy.wait()

    def near_product(o, rows):
        return jnp.dot(v_all[near_round, rows, :], filt[o], preferred_element_type=jnp.float32)

    def far_product(rows, factors):
        return jnp.dot(v_all[1 - near_round, rows, :], factors, preferred_element_type=jnp.float32)

    def near_rows(o):
        own_copy().wait()
        pair_wait(0)
        pair_wait(1)
        for i in range(4):
            rows = pl.ds(i * (rows_v // 4), rows_v // 4)
            acc[rows, :] = near_product(o, rows)

    def predict(piece):
        rows = pl.ds(*piece)
        part = jnp.dot(x_buf[:, rows], w_buf[rows, :], preferred_element_type=jnp.float32)
        if piece[0] == 0:
            pred_acc[...] = part
        else:
            pred_acc[...] += part

    def predict_last(piece):
        rows = pl.ds(*piece)
        for i, to in ((2, diag), (3, t), (0, near[0]), (1, near[1])):
            mine = pl.ds(pl.multiple_of(to * test_rows, test_rows), test_rows)
            value = pred_acc[mine, :] + jnp.dot(x_buf[mine, rows], w_buf[rows, :], preferred_element_type=jnp.float32)
            if i == 2:
                pred_out[2] = value.astype(jnp.bfloat16)
                for k in range(2):
                    for j in range(2):
                        lend_copy(j, k).start()
                continue
            pred_acc[mine, :] = value
            if i < 2:
                pred_out[i, :, i * BLK : (i + 1) * BLK] = value[:, i * BLK : (i + 1) * BLK].astype(jnp.bfloat16)

                @pl.when(core == 0)
                def _():
                    pred_copy(i, i, pl.ds(0, test_rows)).start()

    def direct_lead():
        @pl.when(core == 1)
        def _():
            for i in range(2):
                pred_copy(i, i, pl.ds(0, test_rows)).start()

    def hand_on():
        for k in range(2):
            if k == 1:
                direct_lead()
            for j in range(2):
                to = near[1 - j]
                lend_copy(j, k).wait_recv()
                mine = pl.ds(pl.multiple_of(to * test_rows + k * strip, strip), strip)
                here = pl.ds(k * strip, strip)
                value = pred_acc[mine, half(j)] + lent[here, half(j)].astype(jnp.float32)
                pred_out[1 - j, here, half(j)] = value.astype(jnp.bfloat16)
                pred_copy(1 - j, j, here).start()

    def put_rows(piece):
        rows = pl.ds(*piece)
        for i, block in enumerate(widen(pick, w_buf[rows, :].astype(jnp.float32))):
            w_ref[rows, i * BLK : (i + 1) * BLK] = block.astype(jnp.bfloat16)

    head = (0, far_pieces[3][0])
    rest = (head[1], rows_v - head[1])

    @pl.when(is_mid)
    def _():
        def arrive(i, lead=False):
            line_relay_wait(i)
            if lead or i not in direct:
                pair_far_copy(i).start()

        def help_end(*which):
            for i in which:
                pair_far_wait(i)
            first = far_pieces[which[0]][0]
            rows = pl.ds(first, sum(far_pieces[i][1] for i in which))
            far_out[rows, :] = far_product(rows, far_filt[...]).astype(jnp.bfloat16)
            for i in which:
                far_copy(i).start()

        def own_rows(piece):
            rows = pl.ds(*piece)
            w_buf[rows, :] = (acc[rows, :] + far_product(rows, filt[1])).astype(jnp.bfloat16)

        with scope("m_comb0"):
            combine(0)
            for s in (1, 0):
                for j in range(2):
                    part_copy(1, j, s).start()
        with scope("m_filt0"):
            filter_parts(0)
            send_filt(0)
        with scope("m_side0"):
            side_wait(side_pieces[0], side_recv.at[0])
            for i in range(2):
                line_relay(i).start()
        with scope("m_comb1"):
            combine(1)
        with scope("m_ff0"):
            far_filt_wait(0)
            for i in range(2):
                cross_copy(0, i, t).start()
        with scope("m_fw0"):
            forward_filt(0)
        with scope("m_across"):
            across_wait()
            pair_copy(2).start()
        with scope("m_ff1"):
            for k in (1, 2):
                far_filt_wait(k)
            for i in range(2):
                cross_copy(1, i, near[1 - i]).start()
        with scope("m_filt1"):
            filter_parts(1)
            send_filt(1)
        def tail_lead():
            with scope("m_far0"):
                arrive(0, True)
            side_last(1)
            with scope("m_cross"):
                await_cross()
            with scope("m_help0"):
                help_end(0)
            side_last(2)
            with scope("m_far1"):
                arrive(1, True)
            with scope("m_fw1"):
                forward_filt(1)
            with scope("m_help1"):
                help_end(1)
            with scope("m_aw0"):
                await_filt(0)
            with scope("m_near"):
                near_rows(0)
            for i in (2, 3):
                with scope(f"m_far{i}"):
                    arrive(i, True)
            with scope("m_aw1"):
                await_filt(1)
            with scope("m_own0"):
                for i in range(2):
                    own_rows(far_pieces[i])
            with scope("m_far4"):
                arrive(4, True)
            with scope("m_help2"):
                help_end(2)
            with scope("m_far5"):
                arrive(5, True)
            x_copy.wait()
            with scope("m_pred0"):
                own_rows(far_pieces[2])
                predict(head)
            with scope("m_far6"):
                arrive(6, True)
            with scope("m_help3"):
                help_end(3)
            with scope("m_help4"):
                help_end(4, 5, 6)

        def tail_late():
            with scope("m_far0"):
                arrive(0)
            side_last(1)
            with scope("m_cross"):
                await_cross()
            with scope("m_help0"):
                help_end(0)
            side_last(2)
            with scope("m_far1"):
                arrive(1)
            with scope("m_help1"):
                help_end(1)
            with scope("m_fw1"):
                forward_filt(1)
            with scope("m_aw0"):
                await_filt(0)
            with scope("m_near"):
                near_rows(0)
            with scope("m_far2"):
                arrive(2)
            with scope("m_help2"):
                help_end(2)
            with scope("m_aw1"):
                await_filt(1)
            x_copy.wait()
            with scope("m_own0"):
                for i in range(3):
                    own_rows(far_pieces[i])
            with scope("m_far3"):
                arrive(3)
            with scope("m_help3"):
                help_end(3)
            with scope("m_far4"):
                arrive(4)
            with scope("m_help4"):
                help_end(4)
            with scope("m_far6"):
                arrive(5)
                arrive(6)
            with scope("m_help5"):
                help_end(5, 6)
            with scope("m_pred0"):
                predict(head)

        def side_last(k):
            with scope(f"m_side{k}"):
                side_wait(side_pieces[k], side_recv.at[k])
                if k == 1:
                    line_relay(2).start()
                    return
                for i in range(3, count):
                    line_relay(i).start()
                pair_copy(1).start()

            @pl.when(core == 0)
            def _():
                for i in direct:
                    line_relay_other(i).start()

        def await_cross():
            for i in range(2):
                cross_copy(0, i, near[i]).wait_recv()
                cross_copy(1, i, diag).wait_recv()
            pair_wait(2)

        pl.when(core == 1)(tail_lead)
        pl.when(core == 0)(tail_late)
        with scope("m_last"):
            own_rows(rest)
            predict_last(rest)
        put_rows(whole)

    @pl.when(is_end)
    def _():
        with scope("e_comb0"):
            combine(0)
            for j in range(2):
                part_copy(1, j, 1).start()
        with scope("e_filt0"):
            filter_parts(0)
            far_filt_copy(0).start()
            for i in range(2):
                half_copy(i, t).start()
            for j in range(2):
                part_copy(1, j, 0).start()
        with scope("e_half"):
            for i in range(2):
                half_copy(i, near[i]).wait_recv()
                far_filt_copy(1 + i).start()
            for i in range(1, len(side_pieces)):
                side_copy(side_pieces[i], side_recv.at[i]).start()
        with scope("e_comb1"):
            combine(1)
        with scope("e_filt1"):
            filter_parts(1)
            send_filt(1)
        with scope("e_side"):
            side_wait(whole, side_recv.at[0])
            pair_copy(1).start()
        with scope("e_fw1"):
            forward_filt(1)
        x_copy.wait()
        with scope("e_aw1"):
            await_filt(1)
        with scope("e_near"):
            near_rows(1)

        def add_far(piece):
            rows = pl.ds(*piece)
            w_buf[rows, :] = (acc[rows, :] + far_in[rows, :].astype(jnp.float32)).astype(jnp.bfloat16)

        for i in range(3):
            with scope(f"e_far{i}"):
                far_copy(i).wait_recv()
            add_far(far_pieces[i])
            predict(far_pieces[i])
            put_rows(far_pieces[i])
        with scope("e_far3"):
            far_copy(3).wait_recv()
        with scope("e_far4"):
            for i in range(4, count):
                far_copy(i).wait_recv()
        with scope("e_last"):
            add_far(rest)
            predict_last(rest)
        put_rows(rest)

    with scope("hand"):
        hand_on()
    with scope("pwait"):
        remote(pred_in, pred_in, q_send, q_recv, vox=mate).wait_recv()
    total = pred_acc[pl.ds(pl.multiple_of(t * test_rows, test_rows), test_rows), :]
    for i in range(2):
        total = total + pred_in[i].astype(jnp.float32)
    total = total.astype(jnp.bfloat16).astype(jnp.float32)
    for i, block in enumerate(widen(pick, total)):
        pred_ref[:, i * BLK : (i + 1) * BLK] = block.astype(jnp.bfloat16)

    def sent(ref, sem):
        remote(ref, ref, sem, q_recv, vox=mate).wait_send()

    with scope("drain"):
        sent(part_out, part_send)
        sent(comb_out, comb_send)
        sent(pred_out, q_send)
        sent(v_all.at[0, :, pl.ds(0, depth)], line_send.at[0])
        for k in range(2):
            sent(v_all.at[0, :, pl.ds(0, depth)], pair_send.at[k])

        @pl.when(is_mid)
        def _():
            for k in range(1, 3):
                sent(v_all.at[0, :, pl.ds(0, depth)], line_send.at[k])
            sent(v_all.at[0, :, pl.ds(0, depth)], pair_send.at[2])

            @pl.when(core == 0)
            def _():
                sent(v_all.at[0, pl.ds(0, direct_rows), pl.ds(0, depth)], line_send.at[3])
                sent(v_all.at[0, pl.ds(0, rows_v - direct_rows), pl.ds(0, depth)], pair_send.at[3])

            @pl.when(core == 1)
            def _():
                sent(v_all.at[0, :, pl.ds(0, depth)], pair_send.at[3])

            sent(filt.at[0], ag_send)
            sent(filt.at[0, pl.ds(0, 2 * share)], hand_send)
            sent(far_filt.at[pl.ds(0, 2 * share)], plane_send)
            sent(far_out, help_send)

        @pl.when(is_end)
        def _():
            sent(filt.at[0, pl.ds(0, 2 * share)], ag_send)
            sent(filt.at[0, pl.ds(0, share)], hand_send)
            sent(filt.at[0, pl.ds(0, share)], plane_send)
            sent(filt.at[0, pl.ds(0, 2 * share)], help_send)


def put_out(w_in, pred_in, w_ref, pred_ref, sem):
    copies = [
        pltpu.make_async_copy(w_in, w_ref, sem.at[0]),
        pltpu.make_async_copy(pred_in, pred_ref, sem.at[1]),
    ]
    for copy in copies:
        copy.start()
    for copy in copies:
        copy.wait()


def plane_body(u_train, y_train, sing, lambdas, lam_index, live, v_basis, x_test):
    time_rows, features = u_train.shape
    columns = y_train.shape[1]
    blocks = lam_index.shape[0]
    cap = blocks - blocks // 3
    used = cap * BLK
    rows_v, depth = v_basis.shape
    tests = x_test.shape[0]
    share = depth
    count = len(FAR_PARTS)
    low, full = jnp.bfloat16, jnp.float32
    vmem = pl.BlockSpec(memory_space=pltpu.VMEM)
    anywhere = pl.BlockSpec(memory_space=pl.ANY)
    dma = pltpu.SemaphoreType.DMA
    weights, predicted = pl.pallas_call(
        functools.partial(plane_kernel, cap),
        out_shape=(pltpu.VMEM((rows_v, columns), low), pltpu.VMEM((tests // 4, columns), low)),
        in_specs=[anywhere] * 8,
        out_specs=(vmem, vmem),
        scratch_shapes=[
            pltpu.SMEM(live.shape, live.dtype),
            pltpu.SMEM(lam_index.shape, lam_index.dtype),
            pltpu.SMEM(lambdas.shape, lambdas.dtype),
            pltpu.VMEM((1, features), full),
            pltpu.VMEM((time_rows, columns), low),
            pltpu.VMEM((time_rows, features), low),
            pltpu.VMEM((tests, rows_v), low),
            pltpu.VMEM((2, rows_v, 4 * depth), low),
            pltpu.VMEM((2, 2, 2, BLK, share), low),
            pltpu.VMEM((2, 2, 2, BLK, share), low),
            pltpu.VMEM((2, 2, 2, BLK, share), full),
            pltpu.VMEM((2, 2, BLK, share), low),
            pltpu.VMEM((2, 2, BLK, share), low),
            pltpu.VMEM((2, 4 * share, used), low),
            pltpu.VMEM((4 * share, used), low),
            pltpu.VMEM((rows_v, used), full),
            pltpu.VMEM((tests, used), full),
            pltpu.VMEM((rows_v, used), low),
            pltpu.VMEM((rows_v, used), low),
            pltpu.VMEM((3, tests // 4, used), low),
            pltpu.VMEM((2, tests // 4, used), low),
            pltpu.VMEM((tests // 4, used), low),
            pltpu.VMEM((rows_v, used), low),
            dma((6,)),
            dma((5,)),
            dma,
            dma((4,)),
            dma((len(SIDE_PARTS),)),
            dma,
            dma((count,)),
            dma((4,)),
            dma((3,)),
            dma((count,)),
            dma,
            dma((2, 2, 2)),
            dma,
            dma((2, 2)),
            dma,
            dma((2, 2)),
            dma,
            dma((2, 2)),
            dma,
            dma((2, 2)),
            dma,
            dma((count,)),
            dma,
            dma,
            dma((2, 2)),
        ],
        compiler_params=pltpu.CompilerParams(
            collective_id=1, has_side_effects=True
        ),
    )(live, lam_index, lambdas, sing.reshape(1, features), y_train, u_train, v_basis, x_test)
    weights = pltpu.with_memory_space_constraint(weights, pltpu.VMEM)
    predicted = pltpu.with_memory_space_constraint(predicted, pltpu.VMEM)
    return pl.pallas_call(
        put_out,
        out_shape=(
            jax.ShapeDtypeStruct((rows_v, columns), low),
            jax.ShapeDtypeStruct((tests // 4, columns), low),
        ),
        in_specs=[anywhere, anywhere],
        out_specs=(anywhere, anywhere),
        scratch_shapes=[dma((2,))],
    )(weights, predicted)


def routed(n_t, n_v, *args):
    if (n_t, n_v, args[4].shape[0]) == (4, 8, 3):
        return plane_body(*args)
    return body(n_t, n_v, *args)


def solution(mesh):
    placed = (
        P("tm", None),
        P("tm", "vox"),
        P(),
        P(),
        P("vox"),
        P("vox"),
        P("tm", "vox"),
        P(None, "tm"),
    )
    return jax.shard_map(
        functools.partial(routed, mesh.shape["tm"], mesh.shape["vox"]),
        mesh=mesh,
        in_specs=placed,
        out_specs=(P("tm", "vox"), P("tm", "vox")),
        check_vma=False,
    )
```

```python
import functools

import jax
import jax.numpy as jnp
from jax import lax
from jax.experimental import pallas as pl
from jax.experimental.pallas import tpu as pltpu
from jax.sharding import PartitionSpec as P

BLK = 128
CHUNKS = 4
TILE = 256
MESH = pl.DeviceIdType.MESH


def one_hot(live_ref, cap):
    blocks = live_ref.shape[0]
    live = [live_ref[i] for i in range(blocks)]
    before = [sum(live[:i], jnp.int32(0)) for i in range(blocks)]
    return [
        [jnp.where(before[i] == j, live[i], 0).astype(jnp.float32) for i in range(blocks)]
        for j in range(cap)
    ]


def expand(cap, live_ref, w_in, pred_in, w_ref, pred_ref):
    pick = one_hot(live_ref, cap)
    for source, target in ((w_in, w_ref), (pred_in, pred_ref)):
        values = [source[:, j * BLK : (j + 1) * BLK].astype(jnp.float32) for j in range(cap)]
        for i in range(live_ref.shape[0]):
            block = sum(pick[j][i] * values[j] for j in range(cap))
            target[:, i * BLK : (i + 1) * BLK] = block.astype(target.dtype)


def kernel(
    n_t,
    n_v,
    cap,
    live_ref,
    index_ref,
    lambda_ref,
    sing_ref,
    y_ref,
    u_ref,
    v_ref,
    x_ref,
    w_ref,
    pred_ref,
    u_buf,
    x_buf,
    v_all,
    part_out,
    part_in,
    part_own,
    filt,
    acc,
    pred_acc,
    pred_out,
    pred_in,
    u_sem,
    x_sem,
    own_sem,
    right_sem,
    left_sem,
    line_sem,
    pair_send,
    pair_recv,
    rs_send,
    rs_recv,
    ag_send,
    ag_recv,
    q_send,
    q_recv,
    far_filt,
    far_out,
    far_in,
    far_filt_send,
    far_filt_recv,
    far_send,
    far_recv,
    hand_send,
    hand_recv,
):
    t = lax.axis_index("tm")
    v = lax.axis_index("vox")
    n_z = n_v // 2
    z, core = v // 2, v % 2
    mate = z * 2 + 1 - core
    rows_v, depth = v_ref.shape
    blocks = live_ref.shape[0]
    share = part_own.shape[2]
    half = n_z // 2
    span = n_t * share
    first_round = jnp.where(z < half, 1, 0)
    at_low, at_high = z == 0, z == n_z - 1
    is_end = at_low | at_high
    is_helper = (z == 1) | (z == n_z - 2)

    def holds(zz, src):
        return jnp.logical_not(
            ((zz == 0) & (src >= half)) | ((zz == n_z - 1) & (src < half))
        )
    test_rows = pred_out.shape[1]
    rc = rows_v // CHUNKS

    def u_copy(r, owner):
        cols = pl.ds(pl.multiple_of(r * span + owner * share, share), share)
        return pltpu.make_async_copy(u_ref.at[:, cols], u_buf.at[:, cols], u_sem.at[r, owner])

    def own_copy(ch):
        rows = pl.ds(ch * rc, rc)
        return pltpu.make_async_copy(v_ref.at[rows], v_all.at[v, rows], own_sem.at[ch])

    def line_copy(src, ch, step, first=False):
        rows = pl.ds(ch * rc, rc)
        slot = src * 2 + core
        return pltpu.make_async_remote_copy(
            src_ref=v_ref.at[rows] if first else v_all.at[slot, rows],
            dst_ref=v_all.at[slot, rows],
            send_sem=(right_sem if step > 0 else left_sem).at[src, ch],
            recv_sem=line_sem.at[src, ch],
            device_id={"vox": v + 2 * step},
            device_id_type=MESH,
        )

    def pair_copy(src, ch, first=False):
        rows = pl.ds(ch * rc, rc)
        slot = src * 2 + core
        return pltpu.make_async_remote_copy(
            src_ref=v_ref.at[rows] if first else v_all.at[slot, rows],
            dst_ref=v_all.at[slot, rows],
            send_sem=pair_send.at[src, ch],
            recv_sem=pair_recv.at[src, ch],
            device_id={"vox": mate},
            device_id_type=MESH,
        )

    def pair_arrival(src, ch):
        rows = pl.ds(ch * rc, rc)
        slot = src * 2 + 1 - core
        return pltpu.make_async_remote_copy(
            src_ref=v_all.at[slot, rows],
            dst_ref=v_all.at[slot, rows],
            send_sem=pair_send.at[src, ch],
            recv_sem=pair_recv.at[src, ch],
            device_id={"vox": mate},
            device_id_type=MESH,
        )

    def peer(d):
        return lax.rem(t + d, n_t)

    def part_copy(r, to, owner):
        return pltpu.make_async_remote_copy(
            src_ref=part_out.at[r, to],
            dst_ref=part_in.at[r, owner],
            send_sem=rs_send.at[r, to],
            recv_sem=rs_recv.at[r, owner],
            device_id={"tm": to},
            device_id_type=MESH,
        )

    def filt_copy(r, to, owner):
        return pltpu.make_async_remote_copy(
            src_ref=filt.at[r, owner],
            dst_ref=filt.at[r, owner],
            send_sem=ag_send.at[r, to],
            recv_sem=ag_recv.at[r, owner],
            device_id={"tm": to},
            device_id_type=MESH,
        )

    relayed = n_t == 4
    near = [t + 1 - 2 * lax.rem(t, 2), lax.rem(t + 2, n_t)] if relayed else [peer(d) for d in range(1, n_t)]

    def relay_copy(r, k, to, owner):
        rows = pl.ds(k * (filt.shape[2] // 2), filt.shape[2] // 2)
        return pltpu.make_async_remote_copy(
            src_ref=filt.at[r, owner, rows],
            dst_ref=filt.at[r, owner, rows],
            send_sem=hand_send.at[r, k],
            recv_sem=hand_recv.at[r, k],
            device_id={"tm": to},
            device_id_type=MESH,
        )

    def pred_copy(to, owner):
        return pltpu.make_async_remote_copy(
            src_ref=pred_out.at[to],
            dst_ref=pred_in.at[owner],
            send_sem=q_send.at[to],
            recv_sem=q_recv.at[owner],
            device_id={"tm": to},
            device_id_type=MESH,
        )

    inward = jnp.where(z < half, 1, -1)

    def far_filt_copy(j, step):
        rows = pl.ds(j * BLK, BLK)
        return pltpu.make_async_remote_copy(
            src_ref=filt.at[first_round, :, rows, :],
            dst_ref=far_filt.at[:, rows, :],
            send_sem=far_filt_send.at[j],
            recv_sem=far_filt_recv.at[j],
            device_id={"vox": v + 2 * step},
            device_id_type=MESH,
        )

    def far_copy(j, ch, step):
        rows = pl.ds(ch * rc, rc)
        return pltpu.make_async_remote_copy(
            src_ref=far_out.at[j, rows],
            dst_ref=far_in.at[j, rows],
            send_sem=far_send.at[j, ch],
            recv_sem=far_recv.at[j, ch],
            device_id={"vox": v + 2 * step},
            device_id_type=MESH,
        )

    rounds = (first_round, 1 - first_round)
    for r in rounds:
        for d in range(n_t):
            u_copy(r, peer((d + 1) % n_t)).start()

    barrier = pltpu.get_barrier_semaphore()
    for d in range(1, n_t):
        pl.semaphore_signal(barrier, inc=1, device_id={"tm": peer(d)}, device_id_type=MESH)
    pl.semaphore_signal(barrier, inc=1, device_id={"vox": mate}, device_id_type=MESH)

    @pl.when(z > 0)
    def _():
        pl.semaphore_signal(barrier, inc=1, device_id={"vox": v - 2}, device_id_type=MESH)

    @pl.when(z < n_z - 1)
    def _():
        pl.semaphore_signal(barrier, inc=1, device_id={"vox": v + 2}, device_id_type=MESH)

    neighbours = jnp.where(z > 0, 1, 0) + jnp.where(z < n_z - 1, 1, 0)
    pl.semaphore_wait(barrier, n_t + neighbours)

    for ch in range(CHUNKS):

        @pl.when(z > 0)
        def _():
            line_copy(z, ch, -1, True).start()

        @pl.when(z < n_z - 1)
        def _():
            line_copy(z, ch, 1, True).start()

    pick = one_hot(live_ref, cap)
    lam = [lambda_ref[index_ref[i]] for i in range(blocks)]
    slot_lam = [sum(pick[j][i] * lam[i] for i in range(blocks)) for j in range(cap)]
    slot_live = [sum(pick[j][i] for i in range(blocks)) for j in range(cap)]

    y_cols = [y_ref[:, i * BLK : (i + 1) * BLK].astype(jnp.float32) for i in range(blocks)]
    y_t = jnp.concatenate(
        [sum(pick[j][i] * y_cols[i] for i in range(blocks)).T for j in range(cap)], axis=0
    ).astype(jnp.bfloat16)

    def make_parts(r, send):
        for d in range(1, n_t + 1):
            to = peer(d % n_t)
            u_copy(r, to).wait()

            def tile(i, _, to=to, d=d):
                off = pl.multiple_of(i * TILE, TILE)
                cols = pl.ds(pl.multiple_of(r * span + to * share + i * TILE, TILE), TILE)
                value = jnp.dot(y_t, u_buf[:, cols], preferred_element_type=jnp.float32)
                if d < n_t:
                    part_out[r, to, :, pl.ds(off, TILE)] = value.astype(jnp.bfloat16)
                else:
                    part_own[r, :, pl.ds(off, TILE)] = value
                return 0

            lax.fori_loop(0, share // TILE, tile, 0)
            if send and d < n_t:
                part_copy(r, to, t).start()

    def send_parts(r):
        for d in range(1, n_t):
            part_copy(r, peer(d), t).start()

    def filter_parts(r):
        for d in range(1, n_t):
            part_copy(r, peer(d), peer(d)).wait_recv()
        for i in range(share // TILE):
            cols = slice(i * TILE, (i + 1) * TILE)
            place = pl.multiple_of(r * span + t * share + i * TILE, TILE)
            sing = sing_ref[:, pl.ds(place, TILE)]
            for j in range(cap):
                rows = slice(j * BLK, (j + 1) * BLK)
                total = part_own[r, rows, cols]
                for d in range(1, n_t):
                    total = total + part_in[r, peer(d), rows, cols].astype(jnp.float32)
                factor = sing / (sing * sing + slot_lam[j]) * slot_live[j]
                filt[r, t, rows, cols] = (total * factor).astype(jnp.bfloat16)
        for to in near:
            filt_copy(r, to, t).start()

    def forward_filt(r):
        for to in near:
            filt_copy(r, to, to).wait_recv()
        if relayed:
            for k in range(2):
                relay_copy(r, k, near[k], near[1 - k]).start()

    def await_filt(r):
        if relayed:
            for k in range(2):
                relay_copy(r, k, near[k], n_t - 1 - t).wait_recv()

    make_parts(rounds[0], True)

    for ch in range(CHUNKS):
        pair_copy(z, ch, True).start()
        own_copy(ch).start()
    x_copy = pltpu.make_async_copy(x_ref, x_buf, x_sem)
    x_copy.start()

    make_parts(rounds[1], False)

    def relay(s, ch):
        low, high = z - 1 - s, z + 1 + s

        @pl.when((low >= 0) & holds(z, low))
        def _():
            line_copy(low, ch, -1).wait_recv()

            @pl.when((z < n_z - 1) & holds(z + 1, low))
            def _():
                line_copy(low, ch, 1).start()

            pair_copy(low, ch).start()

        @pl.when((high < n_z) & holds(z, high))
        def _():
            line_copy(high, ch, 1).wait_recv()

            @pl.when((z > 0) & holds(z - 1, high))
            def _():
                line_copy(high, ch, -1).start()

            pair_copy(high, ch).start()

    def product(values, slot, rows, factors):
        return lax.dot_general(
            values[slot, rows, :], factors, (((1,), (1,)), ((), ())),
            preferred_element_type=jnp.float32,
        )

    def place_of(slot):
        start = lax.rem(slot * depth, span)
        owner = start // share
        return owner, pl.ds(pl.multiple_of(start - owner * share, depth), depth)

    base = jnp.where(z == 1, half, 0) * 2

    def settle(ch):
        own_copy(ch).wait()

        def step(src, _):
            @pl.when(holds(z, src))
            def _():
                pair_arrival(src, ch).wait_recv()

            return 0

        lax.fori_loop(0, n_z, step, 0)

    def add_round(r, ch):
        rows = pl.ds(ch * rc, rc)

        def step(i, value):
            slot = r * half * 2 + i
            owner, inner = place_of(slot)
            return value + product(v_all, slot, rows, filt[r, owner, :, inner])

        value = jnp.zeros((rc, acc.shape[1]), jnp.float32)
        for i in range(2 * half):
            value = step(i, value)
        return value

    def far_half(ch):
        rows = pl.ds(ch * rc, rc)

        @pl.when(jnp.logical_not(is_end))
        def _():
            acc[rows, :] = add_round(rounds[0], ch)

        @pl.when(is_end)
        def _():
            acc[rows, :] = jnp.zeros((rc, acc.shape[1]), jnp.float32)

    def help_end(j, chunks):
        cols = slice(j * BLK, (j + 1) * BLK)

        @pl.when(is_helper)
        def _():
            if chunks[0] == 0:
                far_filt_copy(j, -inward).wait_recv()
            for ch in chunks:
                rows = pl.ds(ch * rc, rc)
                value = jnp.zeros((rc, BLK), jnp.float32)
                for i in range(2 * half):
                    owner, inner = place_of(base + i)
                    value += product(v_all, base + i, rows, far_filt[owner, cols, inner])
                far_out[j, rows, :] = value.astype(jnp.bfloat16)
                far_copy(j, ch, -inward).start()

    early, last = CHUNKS // 2, CHUNKS - 1
    for ch in range(early):
        relay(0, ch)
    filter_parts(rounds[0])
    for ch in range(early, last):
        relay(0, ch)
    forward_filt(rounds[0])
    send_parts(rounds[1])
    relay(0, last)
    await_filt(rounds[0])

    @pl.when(is_end)
    def _():
        for j in range(cap):
            far_filt_copy(j, inward).start()

    def relay_step(s, _):
        for ch in range(CHUNKS):
            relay(s, ch)
        return 0

    lax.fori_loop(1, n_z - 3, relay_step, 0)
    for ch in range(early):
        relay(n_z - 3, ch)
    filter_parts(rounds[1])
    for ch in range(early, last):
        relay(n_z - 3, ch)
    for ch in range(early):
        settle(ch)
        far_half(ch)
    forward_filt(rounds[1])
    for ch in range(early, last):
        settle(ch)
        far_half(ch)
    help_end(0, list(range(last)))
    relay(n_z - 3, last)
    settle(last)
    help_end(0, [last])
    far_half(last)
    help_end(1, list(range(CHUNKS)))
    for j in range(2, cap):
        help_end(j, list(range(CHUNKS)))
    await_filt(rounds[1])
    x_copy.wait()

    def finish(ch):
        rows = slice(ch * rc, (ch + 1) * rc)
        acc[rows, :] += add_round(rounds[1], ch)

        @pl.when(is_end)
        def _():
            for j in range(cap):
                cols = slice(j * BLK, (j + 1) * BLK)
                far_copy(j, ch, inward).wait_recv()
                acc[rows, cols] += far_in[j, rows, :].astype(jnp.float32)

        weights = acc[rows, :].astype(jnp.bfloat16)
        w_ref[rows, :] = weights
        value = jnp.dot(x_buf[:, rows], weights, preferred_element_type=jnp.float32)
        if ch == 0:
            pred_acc[...] = value
        else:
            pred_acc[...] += value

    for ch in range(CHUNKS):
        finish(ch)

    for d in range(1, n_t):
        to = peer(d)
        mine = pl.ds(pl.multiple_of(to * test_rows, test_rows), test_rows)
        pred_out[to] = pred_acc[mine, :].astype(jnp.bfloat16)
        pred_copy(to, t).start()
    for d in range(1, n_t):
        pred_copy(peer(d), peer(d)).wait_recv()
    total = pred_acc[pl.ds(pl.multiple_of(t * test_rows, test_rows), test_rows), :]
    for d in range(1, n_t):
        total = total + pred_in[peer(d)].astype(jnp.float32)
    pred_ref[...] = total.astype(jnp.bfloat16)

    for d in range(1, n_t):
        for r in rounds:
            part_copy(r, peer(d), t).wait_send()
        pred_copy(peer(d), t).wait_send()
    for r in rounds:
        for to in near:
            filt_copy(r, to, t).wait_send()
        if relayed:
            for k in range(2):
                relay_copy(r, k, near[k], near[1 - k]).wait_send()

    @pl.when(is_end)
    def _():
        for j in range(cap):
            far_filt_copy(j, inward).wait_send()

    @pl.when(is_helper)
    def _():
        for j in range(cap):
            for ch in range(CHUNKS):
                far_copy(j, ch, -inward).wait_send()

    def drain(src, _):
        for ch in range(CHUNKS):

            @pl.when(holds(z, src))
            def _():
                pair_copy(src, ch).wait_send()

            @pl.when((src <= z) & (z < n_z - 1) & holds(z, src) & holds(z + 1, src))
            def _():
                line_copy(src, ch, 1).wait_send()

            @pl.when((src >= z) & (z > 0) & holds(z, src) & holds(z - 1, src))
            def _():
                line_copy(src, ch, -1).wait_send()

        return 0

    lax.fori_loop(0, n_z, drain, 0)


def body(n_t, n_v, u_train, y_train, sing, lambdas, lam_index, live, v_basis, x_test):
    time_rows, features = u_train.shape
    columns = y_train.shape[1]
    blocks = lam_index.shape[0]
    cap = blocks - blocks // 3
    used = cap * BLK
    rows_v, depth = v_basis.shape
    tests = x_test.shape[0]
    share = features // n_t // 2
    n_z = n_v // 2
    low, full = jnp.bfloat16, jnp.float32
    smem = pl.BlockSpec(memory_space=pltpu.SMEM)
    vmem = pl.BlockSpec(memory_space=pltpu.VMEM)
    anywhere = pl.BlockSpec(memory_space=pl.ANY)
    dma = pltpu.SemaphoreType.DMA
    weights, predicted = pl.pallas_call(
        functools.partial(kernel, n_t, n_v, cap),
        out_shape=(
            jax.ShapeDtypeStruct((rows_v, used), low),
            jax.ShapeDtypeStruct((tests // n_t, used), low),
        ),
        in_specs=[smem, smem, smem, vmem, vmem, anywhere, anywhere, anywhere],
        out_specs=(vmem, vmem),
        scratch_shapes=[
            pltpu.VMEM((time_rows, features), low),
            pltpu.VMEM((tests, rows_v), low),
            pltpu.VMEM((n_v, rows_v, depth), low),
            pltpu.VMEM((2, n_t, used, share), low),
            pltpu.VMEM((2, n_t, used, share), low),
            pltpu.VMEM((2, used, share), full),
            pltpu.VMEM((2, n_t, used, share), low),
            pltpu.VMEM((rows_v, used), full),
            pltpu.VMEM((tests, used), full),
            pltpu.VMEM((n_t, tests // n_t, used), low),
            pltpu.VMEM((n_t, tests // n_t, used), low),
            dma((2, n_t)),
            dma,
            dma((CHUNKS,)),
            dma((n_z, CHUNKS)),
            dma((n_z, CHUNKS)),
            dma((n_z, CHUNKS)),
            dma((n_z, CHUNKS)),
            dma((n_z, CHUNKS)),
            dma((2, n_t)),
            dma((2, n_t)),
            dma((2, n_t)),
            dma((2, n_t)),
            dma((n_t,)),
            dma((n_t,)),
            pltpu.VMEM((n_t, used, share), low),
            pltpu.VMEM((cap, rows_v, BLK), low),
            pltpu.VMEM((cap, rows_v, BLK), low),
            dma((cap,)),
            dma((cap,)),
            dma((cap, CHUNKS)),
            dma((cap, CHUNKS)),
            dma((2, 2)),
            dma((2, 2)),
        ],
        compiler_params=pltpu.CompilerParams(collective_id=0, has_side_effects=True),
    )(live, lam_index, lambdas, sing.reshape(1, features), y_train, u_train, v_basis, x_test)
    return pl.pallas_call(
        functools.partial(expand, cap),
        out_shape=(
            jax.ShapeDtypeStruct((rows_v, columns), low),
            jax.ShapeDtypeStruct((tests // n_t, columns), low),
        ),
        in_specs=[smem, vmem, vmem],
        out_specs=(vmem, vmem),
    )(live, weights, predicted)


FAR_PARTS = (4, 4, 4, 8, 16, 32, 32)
SIDE_PARTS = (2, 4, 4)


def row_pieces(rows, parts):
    pieces, start = [], 0
    for part in parts:
        pieces.append((start, rows // part))
        start += rows // part
    return pieces


def widen(pick, values):
    wide = [values[:, j * BLK : (j + 1) * BLK] for j in range(len(pick))]
    return [sum(pick[j][i] * wide[j] for j in range(len(pick))) for i in range(len(pick[0]))]


def plane_kernel(
    cap,
    live_hbm,
    index_hbm,
    lambda_hbm,
    sing_hbm,
    y_hbm,
    u_hbm,
    v_hbm,
    x_hbm,
    w_ref,
    pred_ref,
    live_ref,
    index_ref,
    lambda_ref,
    sing_buf,
    y_buf,
    u_buf,
    x_buf,
    v_all,
    part_out,
    part_in,
    own,
    comb_out,
    comb_in,
    filt,
    far_filt,
    acc,
    pred_acc,
    far_out,
    far_in,
    pred_out,
    pred_in,
    lent,
    w_buf,
    in_sem,
    u_sem,
    own_sem,
    line_send,
    side_recv,
    across_recv,
    rows_recv,
    pair_send,
    pair_recv,
    pair_far_recv,
    part_send,
    part_recv,
    comb_send,
    comb_recv,
    ag_send,
    ag_recv,
    hand_send,
    hand_recv,
    plane_send,
    plane_recv,
    help_send,
    help_recv,
    q_send,
    q_recv,
    lend_recv,
    ready,
    reached,
):
    t = lax.axis_index("tm")
    v = lax.axis_index("vox")
    z, core = v // 2, v % 2
    mate = z * 2 + 1 - core
    rows_v, depth = v_hbm.shape
    blocks = live_ref.shape[0]
    share = depth
    span = 4 * share
    far_pieces = row_pieces(rows_v, FAR_PARTS)
    side_pieces = row_pieces(rows_v, SIDE_PARTS)
    whole = (0, rows_v)
    count = len(far_pieces)
    low_side = z < 2
    inward = jnp.where(low_side, 1, -1)
    is_end = (z == 0) | (z == 3)
    is_mid = jnp.logical_not(is_end)
    partner_z = jnp.where(is_end, z + inward, z - inward)
    partner = partner_z * 2 + core
    near_round = z // 2
    rounds = (1 - z % 2, z % 2)
    near = [t + 1 - 2 * lax.rem(t, 2), lax.rem(t + 2, 4)]
    diag = 3 - t
    scope = jax.named_scope

    def remote(src, dst, send, recv, **place):
        return pltpu.make_async_remote_copy(
            src_ref=src, dst_ref=dst, send_sem=send, recv_sem=recv, device_id=place, device_id_type=MESH
        )

    def slot_of(zz, cc):
        return zz * 2 + cc

    def block_of(slot, piece):
        cols = pl.ds(pl.multiple_of((slot % 4) * depth, depth), depth)
        return v_all.at[slot // 4, pl.ds(*piece), cols]

    far_mid, far_end = 3 - z, 3 - partner_z
    across_mate = (z + inward) * 2 + 1 - core

    def side_copy(piece, recv):
        return remote(v_hbm.at[pl.ds(*piece)], block_of(v, piece), line_send.at[0], recv, vox=partner)

    def side_wait(piece, recv):
        at = block_of(partner, piece)
        remote(at, at, line_send.at[0], recv, vox=partner).wait_recv()

    def across_copy():
        return remote(v_hbm, block_of(v, whole), line_send.at[1], across_recv, vox=v + 2 * inward)

    def across_wait():
        at = block_of(slot_of(far_mid, core), whole)
        remote(at, at, line_send.at[1], across_recv, vox=v + 2 * inward).wait_recv()

    def line_relay(i):
        at = block_of(partner, far_pieces[i])
        return remote(at, at, line_send.at[2], rows_recv.at[i], vox=v + 2 * inward)

    direct = (count - 2, count - 1)
    direct_rows = rows_v - far_pieces[direct[0]][0]

    def line_relay_other(i):
        at = block_of(partner, far_pieces[i])
        return remote(at, at, line_send.at[3], pair_far_recv.at[i], vox=across_mate)

    def line_relay_wait(i):
        at = block_of(slot_of(far_end, core), far_pieces[i])
        remote(at, at, line_send.at[2], rows_recv.at[i], vox=v + 2 * inward).wait_recv()

    def pair_copy(k):
        src = v_hbm if k == 0 else block_of(pair_slot(k, core), whole)
        return remote(src, block_of(pair_slot(k, core), whole), pair_send.at[k], pair_recv.at[k], vox=mate)

    def pair_slot(k, cc):
        return slot_of((z, partner_z, far_mid)[k], cc)

    def pair_wait(k):
        at = block_of(pair_slot(k, 1 - core), whole)
        remote(at, at, pair_send.at[k], pair_recv.at[k], vox=mate).wait_recv()

    def pair_far_copy(i):
        at = block_of(slot_of(far_end, core), far_pieces[i])
        return remote(at, at, pair_send.at[3], pair_far_recv.at[i], vox=mate)

    def pair_far_wait(i):
        at = block_of(slot_of(far_end, 1 - core), far_pieces[i])
        remote(at, at, pair_send.at[3], pair_far_recv.at[i], vox=mate).wait_recv()

    def own_copy():
        return pltpu.make_async_copy(v_hbm, block_of(v, whole), own_sem)

    def rows_of(i):
        return pl.ds(*far_pieces[i])

    def u_copy(i):
        first, width = (owners[i] * share, share) if i < 4 else (0, span)
        cols = pl.ds(pl.multiple_of(rounds[i // 4] * span + first, share), width)
        return pltpu.make_async_copy(u_hbm.at[:, cols], u_buf.at[:, cols], u_sem.at[i])

    def half(i):
        return pl.ds(i * BLK, BLK)

    def rank(owner):
        return pl.ds(pl.multiple_of(owner * share, share), share)

    def part_copy(o, j, s):
        return remote(part_out.at[o, j, s], part_in.at[o, j, s], part_send, part_recv.at[o, s], tm=near[j])

    def comb_copy(o, j):
        return remote(comb_out.at[o, j], comb_in.at[o, j], comb_send, comb_recv.at[o], tm=near[1 - j])

    def ag_copy(o, i, owner):
        at = filt.at[o, rank(owner)]
        return remote(at, at, ag_send, ag_recv.at[o], tm=near[i])

    def hand_copy(o, i, owner):
        at = filt.at[o, rank(owner), half(i)]
        return remote(at, at, hand_send, hand_recv.at[o], tm=near[i])

    def half_copy(i, owner):
        at = filt.at[0, rank(owner), half(i)]
        return remote(at, at, plane_send, plane_recv, tm=near[i])

    def far_filt_copy(k):
        if k == 0:
            src, dst = filt.at[0, rank(t)], far_filt.at[rank(t)]
        else:
            src, dst = filt.at[0, rank(near[k - 1]), half(k - 1)], far_filt.at[rank(near[k - 1]), half(k - 1)]
        return remote(src, dst, help_send, help_recv.at[k], vox=partner)

    def far_filt_wait(k):
        at = far_filt.at[rank(t)] if k == 0 else far_filt.at[rank(near[k - 1]), half(k - 1)]
        remote(at, at, help_send, help_recv.at[k], vox=partner).wait_recv()

    def cross_copy(s, i, owner):
        at = far_filt.at[rank(owner), half(1 - i)]
        return remote(at, at, plane_send, plane_recv, tm=near[i])

    def far_copy(ch):
        return remote(
            far_out.at[rows_of(ch)], far_in.at[rows_of(ch)], help_send, rows_recv.at[ch], vox=partner
        )

    test_rows = pred_out.shape[1]
    strip = test_rows // 2

    def lend_copy(j, k):
        at = (pl.ds(k * strip, strip), half(j))
        return remote(pred_out.at[(2, *at)], lent.at[at], q_send, lend_recv.at[k], tm=near[j])

    def pred_copy(i, j, rows):
        at = (i, rows, half(j))
        return remote(pred_out.at[at], pred_in.at[at], q_send, q_recv, tm=near[i])

    barrier = pltpu.get_barrier_semaphore()

    bits = (lax.rem(t, 2), t // 2, core)
    pairs = ({"tm": near[0]}, {"tm": near[1]}, {"vox": mate})

    def signal(sem, place):
        pl.semaphore_signal(sem, inc=1, device_id=place, device_id_type=MESH)

    for bit, place in zip(bits, pairs):

        @pl.when(bit == 0)
        def _():
            signal(barrier, place)

    @pl.when(z < 3)
    def _():
        signal(barrier, {"vox": v + 2})

    @pl.when(z == 2)
    def _():
        signal(barrier, {"vox": v - 2})

    y_copy = pltpu.make_async_copy(y_hbm, y_buf, in_sem.at[0])
    sing_copy = pltpu.make_async_copy(sing_hbm, sing_buf, in_sem.at[1])
    x_copy = pltpu.make_async_copy(x_hbm, x_buf, in_sem.at[2])
    owners = (diag, near[0], near[1], t)
    y_copy.start()
    for i in range(4):
        u_copy(i).start()
    sing_copy.start()
    scalars = [
        pltpu.make_async_copy(live_hbm, live_ref, in_sem.at[3]),
        pltpu.make_async_copy(index_hbm, index_ref, in_sem.at[4]),
        pltpu.make_async_copy(lambda_hbm, lambda_ref, in_sem.at[5]),
    ]
    for copy in scalars:
        copy.start()

    with scope("bar"):
        callers = sum(bits) + jnp.where(z == 0, 0, jnp.where(z == 1, 2, 1))

        @pl.when(callers > 0)
        def _():
            pl.semaphore_wait(barrier, callers)


    @pl.when(is_mid)
    def _():
        across_copy().start()

    for bit, place in zip(bits, pairs):

        @pl.when(bit == 1)
        def _():
            signal(ready, place)

    @pl.when((z == 1) | (z == 3))
    def _():
        signal(ready, {"vox": v - 2})

    u_copy(4).start()

    for copy in scalars:
        copy.wait()
    pick = one_hot(live_ref, cap)
    lam = [lambda_ref[index_ref[i]] for i in range(blocks)]
    slot_lam = [sum(pick[j][i] * lam[i] for i in range(blocks)) for j in range(cap)]
    slot_live = [sum(pick[j][i] for i in range(blocks)) for j in range(cap)]

    with scope("ycp"):
        y_copy.wait()
    y_cols = [y_buf[:, i * BLK : (i + 1) * BLK].astype(jnp.float32) for i in range(blocks)]
    y_t = jnp.concatenate(
        [sum(pick[j][i] * y_cols[i] for i in range(blocks)).T for j in range(cap)], axis=0
    ).astype(jnp.bfloat16)

    def greet():
        with scope("ready"):
            answers = 3 - sum(bits) + jnp.where((z == 0) | (z == 2), 1, 0)

            @pl.when(answers > 0)
            def _():
                pl.semaphore_wait(ready, answers)


        @pl.when(is_mid)
        def _():
            side_copy(whole, side_recv.at[0]).start()

        @pl.when(is_end)
        def _():
            side_copy(side_pieces[0], side_recv.at[0]).start()

    def make_parts(o):
        if o == 1:
            u_copy(4).wait()
        for i in range(4):
            if o == 0:
                u_copy(i).wait()
            for tile in range(share // TILE):
                into = slice(tile * TILE, (tile + 1) * TILE)
                start = rounds[o] * span + owners[i] * share + tile * TILE
                cols = pl.ds(pl.multiple_of(start, TILE), TILE)
                value = jnp.dot(y_t, u_buf[:, cols], preferred_element_type=jnp.float32)
                first, second = value[:BLK], value[BLK:]
                if i == 0:
                    part_out[o, 0, 1, :, into] = first.astype(jnp.bfloat16)
                    part_out[o, 1, 1, :, into] = second.astype(jnp.bfloat16)
                elif i == 1:
                    part_out[o, 0, 0, :, into] = first.astype(jnp.bfloat16)
                    own[o, 1, 1, :, into] = second
                elif i == 2:
                    own[o, 0, 1, :, into] = first
                    part_out[o, 1, 0, :, into] = second.astype(jnp.bfloat16)
                else:
                    own[o, 0, 0, :, into] = first
                    own[o, 1, 0, :, into] = second
            if o == 0 and i == 0:
                greet()
                for j in range(2):
                    part_copy(o, j, 1).start()
            if o == 0 and i in (1, 2):
                part_copy(o, i - 1, 0).start()

    def received(ref, sem):
        remote(ref, ref, q_send, sem, vox=mate).wait_recv()

    def combine(o):
        received(part_in.at[o, :, 1], part_recv.at[o, 1])
        for j in range(2):
            comb_out[o, j] = (own[o, j, 1] + part_in[o, j, 1].astype(jnp.float32)).astype(jnp.bfloat16)
            comb_copy(o, j).start()

    def filter_parts(o):
        place = pl.multiple_of(rounds[o] * span + t * share, share)
        sing = sing_buf[:, pl.ds(place, share)]
        received(part_in.at[o, :, 0], part_recv.at[o, 0])
        received(comb_in.at[o], comb_recv.at[o])
        for j in range(cap):
            total = own[o, j, 0] + part_in[o, j, 0].astype(jnp.float32) + comb_in[o, j].astype(jnp.float32)
            factor = sing / (sing * sing + slot_lam[j]) * slot_live[j]
            filt[o, rank(t), half(j)] = (total * factor).T.astype(jnp.bfloat16)

    def send_filt(o):
        for i in range(2):
            ag_copy(o, i, t).start()

    def forward_filt(o):
        received(filt.at[o, pl.ds(0, 2 * share)], ag_recv.at[o])
        for i in range(2):
            hand_copy(o, i, near[1 - i]).start()

    def await_filt(o):
        received(filt.at[o, pl.ds(0, share)], hand_recv.at[o])

    with scope("mp0"):
        make_parts(0)
    with scope("mp1"):
        make_parts(1)
    pair_copy(0).start()
    own_copy().start()
    x_copy.start()
    sing_copy.wait()

    def near_product(o, rows):
        return jnp.dot(v_all[near_round, rows, :], filt[o], preferred_element_type=jnp.float32)

    def far_product(rows, factors):
        return jnp.dot(v_all[1 - near_round, rows, :], factors, preferred_element_type=jnp.float32)

    def near_rows(o):
        own_copy().wait()
        pair_wait(0)
        pair_wait(1)
        for i in range(4):
            rows = pl.ds(i * (rows_v // 4), rows_v // 4)
            acc[rows, :] = near_product(o, rows)

    def predict(piece):
        rows = pl.ds(*piece)
        part = jnp.dot(x_buf[:, rows], w_buf[rows, :], preferred_element_type=jnp.float32)
        if piece[0] == 0:
            pred_acc[...] = part
        else:
            pred_acc[...] += part

    def predict_last(piece):
        rows = pl.ds(*piece)
        for i, to in ((2, diag), (3, t), (0, near[0]), (1, near[1])):
            mine = pl.ds(pl.multiple_of(to * test_rows, test_rows), test_rows)
            value = pred_acc[mine, :] + jnp.dot(x_buf[mine, rows], w_buf[rows, :], preferred_element_type=jnp.float32)
            if i == 2:
                pred_out[2] = value.astype(jnp.bfloat16)
                for k in range(2):
                    for j in range(2):
                        lend_copy(j, k).start()
                continue
            pred_acc[mine, :] = value
            if i < 2:
                pred_out[i, :, i * BLK : (i + 1) * BLK] = value[:, i * BLK : (i + 1) * BLK].astype(jnp.bfloat16)

                @pl.when(core == 0)
                def _():
                    pred_copy(i, i, pl.ds(0, test_rows)).start()

    def direct_lead():
        @pl.when(core == 1)
        def _():
            for i in range(2):
                pred_copy(i, i, pl.ds(0, test_rows)).start()

    def hand_on():
        for k in range(2):
            if k == 1:
                direct_lead()
            received(lent.at[pl.ds(k * strip, strip)], lend_recv.at[k])
            for j in range(2):
                to = near[1 - j]
                mine = pl.ds(pl.multiple_of(to * test_rows + k * strip, strip), strip)
                here = pl.ds(k * strip, strip)
                value = pred_acc[mine, half(j)] + lent[here, half(j)].astype(jnp.float32)
                pred_out[1 - j, here, half(j)] = value.astype(jnp.bfloat16)
                pred_copy(1 - j, j, here).start()

    def put_rows(piece):
        rows = pl.ds(*piece)
        for i, block in enumerate(widen(pick, w_buf[rows, :].astype(jnp.float32))):
            w_ref[rows, i * BLK : (i + 1) * BLK] = block.astype(jnp.bfloat16)

    head = (0, far_pieces[3][0])
    rest = (head[1], rows_v - head[1])

    @pl.when(is_mid)
    def _():
        def arrive(i, lead=False):
            line_relay_wait(i)
            if lead or i not in direct:
                pair_far_copy(i).start()

        def help_end(*which):
            for i in which:
                pair_far_wait(i)
            first = far_pieces[which[0]][0]
            rows = pl.ds(first, sum(far_pieces[i][1] for i in which))
            far_out[rows, :] = far_product(rows, far_filt[...]).astype(jnp.bfloat16)
            for i in which:
                far_copy(i).start()

        def own_rows(piece):
            rows = pl.ds(*piece)
            w_buf[rows, :] = (acc[rows, :] + far_product(rows, filt[1])).astype(jnp.bfloat16)

        with scope("m_comb0"):
            combine(0)
            for s in (1, 0):
                for j in range(2):
                    part_copy(1, j, s).start()
        with scope("m_filt0"):
            filter_parts(0)
            send_filt(0)
        with scope("m_side0"):
            side_wait(side_pieces[0], side_recv.at[0])
            for i in range(2):
                line_relay(i).start()
        with scope("m_comb1"):
            combine(1)
        with scope("m_ff0"):
            far_filt_wait(0)
            for i in range(2):
                cross_copy(0, i, t).start()
        with scope("m_fw0"):
            forward_filt(0)
        with scope("m_across"):
            across_wait()
            pair_copy(2).start()
        with scope("m_ff1"):
            for k in (1, 2):
                far_filt_wait(k)
            for i in range(2):
                cross_copy(1, i, near[1 - i]).start()
        with scope("m_filt1"):
            filter_parts(1)
            send_filt(1)
        def tail_lead():
            with scope("m_far0"):
                arrive(0, True)
            side_last(1)
            with scope("m_cross"):
                await_cross()
            with scope("m_help0"):
                help_end(0)
            side_last(2)
            with scope("m_far1"):
                arrive(1, True)
            with scope("m_fw1"):
                forward_filt(1)
            with scope("m_help1"):
                help_end(1)
            with scope("m_aw0"):
                await_filt(0)
            with scope("m_near"):
                near_rows(0)
            for i in (2, 3):
                with scope(f"m_far{i}"):
                    arrive(i, True)
            with scope("m_aw1"):
                await_filt(1)
            with scope("m_own0"):
                for i in range(2):
                    own_rows(far_pieces[i])
            with scope("m_help2"):
                help_end(2)
            with scope("m_far4"):
                arrive(4, True)
            with scope("m_own1"):
                own_rows(far_pieces[2])
            for i in (5, 6):
                with scope(f"m_far{i}"):
                    arrive(i, True)
            with scope("m_help3"):
                help_end(3)
            with scope("m_help4"):
                help_end(4, 5, 6)
            x_copy.wait()
            with scope("m_pred0"):
                predict(head)

        def tail_late():
            with scope("m_far0"):
                arrive(0)
            side_last(1)
            with scope("m_cross"):
                await_cross()
            with scope("m_help0"):
                help_end(0)
            side_last(2)
            with scope("m_far1"):
                arrive(1)
            with scope("m_help1"):
                help_end(1)
            with scope("m_fw1"):
                forward_filt(1)
            with scope("m_aw0"):
                await_filt(0)
            with scope("m_near"):
                near_rows(0)
            with scope("m_far2"):
                arrive(2)
            with scope("m_help2"):
                help_end(2)
            with scope("m_aw1"):
                await_filt(1)
            x_copy.wait()
            with scope("m_own0"):
                own_rows(far_pieces[0])
            with scope("m_far3"):
                arrive(3)
            with scope("m_help3"):
                help_end(3)
            with scope("m_own1"):
                for i in (1, 2):
                    own_rows(far_pieces[i])
            with scope("m_far4"):
                arrive(4)
            with scope("m_help4"):
                help_end(4)
            with scope("m_far6"):
                arrive(5)
                arrive(6)
            with scope("m_help5"):
                help_end(5, 6)
            with scope("m_pred0"):
                predict(head)

        def side_last(k):
            with scope(f"m_side{k}"):
                side_wait(side_pieces[k], side_recv.at[k])
                if k == 1:
                    line_relay(2).start()
                    return
                for i in range(3, count):
                    line_relay(i).start()
                pair_copy(1).start()

            @pl.when(core == 0)
            def _():
                pl.semaphore_wait(reached, 1)
                for i in direct:
                    line_relay_other(i).start()

        def await_cross():
            received(far_filt.at[pl.ds(0, 2 * share)], plane_recv)
            pair_wait(2)

            @pl.when(core == 1)
            def _():
                signal(reached, {"vox": across_mate})


        pl.when(core == 1)(tail_lead)
        pl.when(core == 0)(tail_late)
        with scope("m_last"):
            own_rows(rest)
            predict_last(rest)
        put_rows(whole)

    @pl.when(is_end)
    def _():
        with scope("e_comb0"):
            combine(0)
            for j in range(2):
                part_copy(1, j, 1).start()
        with scope("e_filt0"):
            filter_parts(0)
            far_filt_copy(0).start()
            for i in range(2):
                half_copy(i, t).start()
            for j in range(2):
                part_copy(1, j, 0).start()
        with scope("e_half"):
            received(filt.at[0, pl.ds(0, share)], plane_recv)
            for i in range(2):
                far_filt_copy(1 + i).start()
            for i in range(1, len(side_pieces)):
                side_copy(side_pieces[i], side_recv.at[i]).start()
        with scope("e_comb1"):
            combine(1)
        with scope("e_filt1"):
            filter_parts(1)
            send_filt(1)
        with scope("e_side"):
            side_wait(whole, side_recv.at[0])
            pair_copy(1).start()
        with scope("e_fw1"):
            forward_filt(1)
        x_copy.wait()
        with scope("e_aw1"):
            await_filt(1)
        with scope("e_near"):
            near_rows(1)

        def add_far(piece):
            rows = pl.ds(*piece)
            w_buf[rows, :] = (acc[rows, :] + far_in[rows, :].astype(jnp.float32)).astype(jnp.bfloat16)

        for i in range(3):
            with scope(f"e_far{i}"):
                far_copy(i).wait_recv()
            add_far(far_pieces[i])
            predict(far_pieces[i])
            put_rows(far_pieces[i])
        with scope("e_far3"):
            far_copy(3).wait_recv()
        with scope("e_far4"):
            for i in range(4, count):
                far_copy(i).wait_recv()
        with scope("e_last"):
            add_far(rest)
            predict_last(rest)
        put_rows(rest)

    with scope("hand"):
        hand_on()
    with scope("pwait"):
        remote(pred_in, pred_in, q_send, q_recv, vox=mate).wait_recv()
    total = pred_acc[pl.ds(pl.multiple_of(t * test_rows, test_rows), test_rows), :]
    for i in range(2):
        total = total + pred_in[i].astype(jnp.float32)
    total = total.astype(jnp.bfloat16).astype(jnp.float32)
    for i, block in enumerate(widen(pick, total)):
        pred_ref[:, i * BLK : (i + 1) * BLK] = block.astype(jnp.bfloat16)

    def sent(ref, sem):
        remote(ref, ref, sem, q_recv, vox=mate).wait_send()

    with scope("drain"):
        sent(part_out, part_send)
        sent(comb_out, comb_send)
        sent(pred_out, q_send)
        sent(v_all.at[0, :, pl.ds(0, depth)], line_send.at[0])
        for k in range(2):
            sent(v_all.at[0, :, pl.ds(0, depth)], pair_send.at[k])

        @pl.when(is_mid)
        def _():
            for k in range(1, 3):
                sent(v_all.at[0, :, pl.ds(0, depth)], line_send.at[k])
            sent(v_all.at[0, :, pl.ds(0, depth)], pair_send.at[2])

            @pl.when(core == 0)
            def _():
                sent(v_all.at[0, pl.ds(0, direct_rows), pl.ds(0, depth)], line_send.at[3])
                sent(v_all.at[0, pl.ds(0, rows_v - direct_rows), pl.ds(0, depth)], pair_send.at[3])

            @pl.when(core == 1)
            def _():
                sent(v_all.at[0, :, pl.ds(0, depth)], pair_send.at[3])

            sent(filt.at[0], ag_send)
            sent(filt.at[0, pl.ds(0, 2 * share)], hand_send)
            sent(far_filt.at[pl.ds(0, 2 * share)], plane_send)
            sent(far_out, help_send)

        @pl.when(is_end)
        def _():
            sent(filt.at[0, pl.ds(0, 2 * share)], ag_send)
            sent(filt.at[0, pl.ds(0, share)], hand_send)
            sent(filt.at[0, pl.ds(0, share)], plane_send)
            sent(filt.at[0, pl.ds(0, 2 * share)], help_send)


def put_out(w_in, pred_in, w_ref, pred_ref, sem):
    copies = [
        pltpu.make_async_copy(w_in, w_ref, sem.at[0]),
        pltpu.make_async_copy(pred_in, pred_ref, sem.at[1]),
    ]
    for copy in copies:
        copy.start()
    for copy in copies:
        copy.wait()


def plane_body(u_train, y_train, sing, lambdas, lam_index, live, v_basis, x_test):
    time_rows, features = u_train.shape
    columns = y_train.shape[1]
    blocks = lam_index.shape[0]
    cap = blocks - blocks // 3
    used = cap * BLK
    rows_v, depth = v_basis.shape
    tests = x_test.shape[0]
    share = depth
    count = len(FAR_PARTS)
    low, full = jnp.bfloat16, jnp.float32
    vmem = pl.BlockSpec(memory_space=pltpu.VMEM)
    anywhere = pl.BlockSpec(memory_space=pl.ANY)
    dma = pltpu.SemaphoreType.DMA
    weights, predicted = pl.pallas_call(
        functools.partial(plane_kernel, cap),
        out_shape=(pltpu.VMEM((rows_v, columns), low), pltpu.VMEM((tests // 4, columns), low)),
        in_specs=[anywhere] * 8,
        out_specs=(vmem, vmem),
        scratch_shapes=[
            pltpu.SMEM(live.shape, live.dtype),
            pltpu.SMEM(lam_index.shape, lam_index.dtype),
            pltpu.SMEM(lambdas.shape, lambdas.dtype),
            pltpu.VMEM((1, features), full),
            pltpu.VMEM((time_rows, columns), low),
            pltpu.VMEM((time_rows, features), low),
            pltpu.VMEM((tests, rows_v), low),
            pltpu.VMEM((2, rows_v, 4 * depth), low),
            pltpu.VMEM((2, 2, 2, BLK, share), low),
            pltpu.VMEM((2, 2, 2, BLK, share), low),
            pltpu.VMEM((2, 2, 2, BLK, share), full),
            pltpu.VMEM((2, 2, BLK, share), low),
            pltpu.VMEM((2, 2, BLK, share), low),
            pltpu.VMEM((2, 4 * share, used), low),
            pltpu.VMEM((4 * share, used), low),
            pltpu.VMEM((rows_v, used), full),
            pltpu.VMEM((tests, used), full),
            pltpu.VMEM((rows_v, used), low),
            pltpu.VMEM((rows_v, used), low),
            pltpu.VMEM((3, tests // 4, used), low),
            pltpu.VMEM((2, tests // 4, used), low),
            pltpu.VMEM((tests // 4, used), low),
            pltpu.VMEM((rows_v, used), low),
            dma((6,)),
            dma((5,)),
            dma,
            dma((4,)),
            dma((len(SIDE_PARTS),)),
            dma,
            dma((count,)),
            dma((4,)),
            dma((3,)),
            dma((count,)),
            dma,
            dma((2, 2)),
            dma,
            dma((2,)),
            dma,
            dma((2,)),
            dma,
            dma((2,)),
            dma,
            dma,
            dma,
            dma((3,)),
            dma,
            dma,
            dma((2,)),
            pltpu.SemaphoreType.REGULAR,
            pltpu.SemaphoreType.REGULAR,
        ],
        compiler_params=pltpu.CompilerParams(
            collective_id=1, has_side_effects=True
        ),
    )(live, lam_index, lambdas, sing.reshape(1, features), y_train, u_train, v_basis, x_test)
    weights = pltpu.with_memory_space_constraint(weights, pltpu.VMEM)
    predicted = pltpu.with_memory_space_constraint(predicted, pltpu.VMEM)
    return pl.pallas_call(
        put_out,
        out_shape=(
            jax.ShapeDtypeStruct((rows_v, columns), low),
            jax.ShapeDtypeStruct((tests // 4, columns), low),
        ),
        in_specs=[anywhere, anywhere],
        out_specs=(anywhere, anywhere),
        scratch_shapes=[dma((2,))],
    )(weights, predicted)


def routed(n_t, n_v, *args):
    if (n_t, n_v, args[4].shape[0]) == (4, 8, 3):
        return plane_body(*args)
    return body(n_t, n_v, *args)


def solution(mesh):
    placed = (
        P("tm", None),
        P("tm", "vox"),
        P(),
        P(),
        P("vox"),
        P("vox"),
        P("tm", "vox"),
        P(None, "tm"),
    )
    return jax.shard_map(
        functools.partial(routed, mesh.shape["tm"], mesh.shape["vox"]),
        mesh=mesh,
        in_specs=placed,
        out_specs=(P("tm", "vox"), P("tm", "vox")),
        check_vma=False,
    )
```

```python
import functools

import jax
import jax.numpy as jnp
from jax import lax
from jax.experimental import pallas as pl
from jax.experimental.pallas import tpu as pltpu
from jax.sharding import PartitionSpec as P

BLK = 128
CHUNKS = 4
TILE = 256
MESH = pl.DeviceIdType.MESH


def one_hot(live_ref, cap):
    blocks = live_ref.shape[0]
    live = [live_ref[i] for i in range(blocks)]
    before = [sum(live[:i], jnp.int32(0)) for i in range(blocks)]
    return [
        [jnp.where(before[i] == j, live[i], 0).astype(jnp.float32) for i in range(blocks)]
        for j in range(cap)
    ]


def expand(cap, live_ref, w_in, pred_in, w_ref, pred_ref):
    pick = one_hot(live_ref, cap)
    for source, target in ((w_in, w_ref), (pred_in, pred_ref)):
        values = [source[:, j * BLK : (j + 1) * BLK].astype(jnp.float32) for j in range(cap)]
        for i in range(live_ref.shape[0]):
            block = sum(pick[j][i] * values[j] for j in range(cap))
            target[:, i * BLK : (i + 1) * BLK] = block.astype(target.dtype)


def kernel(
    n_t,
    n_v,
    cap,
    live_ref,
    index_ref,
    lambda_ref,
    sing_ref,
    y_ref,
    u_ref,
    v_ref,
    x_ref,
    w_ref,
    pred_ref,
    u_buf,
    x_buf,
    v_all,
    part_out,
    part_in,
    part_own,
    filt,
    acc,
    pred_acc,
    pred_out,
    pred_in,
    u_sem,
    x_sem,
    own_sem,
    right_sem,
    left_sem,
    line_sem,
    pair_send,
    pair_recv,
    rs_send,
    rs_recv,
    ag_send,
    ag_recv,
    q_send,
    q_recv,
    far_filt,
    far_out,
    far_in,
    far_filt_send,
    far_filt_recv,
    far_send,
    far_recv,
    hand_send,
    hand_recv,
):
    t = lax.axis_index("tm")
    v = lax.axis_index("vox")
    n_z = n_v // 2
    z, core = v // 2, v % 2
    mate = z * 2 + 1 - core
    rows_v, depth = v_ref.shape
    blocks = live_ref.shape[0]
    share = part_own.shape[2]
    half = n_z // 2
    span = n_t * share
    first_round = jnp.where(z < half, 1, 0)
    at_low, at_high = z == 0, z == n_z - 1
    is_end = at_low | at_high
    is_helper = (z == 1) | (z == n_z - 2)

    def holds(zz, src):
        return jnp.logical_not(
            ((zz == 0) & (src >= half)) | ((zz == n_z - 1) & (src < half))
        )
    test_rows = pred_out.shape[1]
    rc = rows_v // CHUNKS

    def u_copy(r, owner):
        cols = pl.ds(pl.multiple_of(r * span + owner * share, share), share)
        return pltpu.make_async_copy(u_ref.at[:, cols], u_buf.at[:, cols], u_sem.at[r, owner])

    def own_copy(ch):
        rows = pl.ds(ch * rc, rc)
        return pltpu.make_async_copy(v_ref.at[rows], v_all.at[v, rows], own_sem.at[ch])

    def line_copy(src, ch, step, first=False):
        rows = pl.ds(ch * rc, rc)
        slot = src * 2 + core
        return pltpu.make_async_remote_copy(
            src_ref=v_ref.at[rows] if first else v_all.at[slot, rows],
            dst_ref=v_all.at[slot, rows],
            send_sem=(right_sem if step > 0 else left_sem).at[src, ch],
            recv_sem=line_sem.at[src, ch],
            device_id={"vox": v + 2 * step},
            device_id_type=MESH,
        )

    def pair_copy(src, ch, first=False):
        rows = pl.ds(ch * rc, rc)
        slot = src * 2 + core
        return pltpu.make_async_remote_copy(
            src_ref=v_ref.at[rows] if first else v_all.at[slot, rows],
            dst_ref=v_all.at[slot, rows],
            send_sem=pair_send.at[src, ch],
            recv_sem=pair_recv.at[src, ch],
            device_id={"vox": mate},
            device_id_type=MESH,
        )

    def pair_arrival(src, ch):
        rows = pl.ds(ch * rc, rc)
        slot = src * 2 + 1 - core
        return pltpu.make_async_remote_copy(
            src_ref=v_all.at[slot, rows],
            dst_ref=v_all.at[slot, rows],
            send_sem=pair_send.at[src, ch],
            recv_sem=pair_recv.at[src, ch],
            device_id={"vox": mate},
            device_id_type=MESH,
        )

    def peer(d):
        return lax.rem(t + d, n_t)

    def part_copy(r, to, owner):
        return pltpu.make_async_remote_copy(
            src_ref=part_out.at[r, to],
            dst_ref=part_in.at[r, owner],
            send_sem=rs_send.at[r, to],
            recv_sem=rs_recv.at[r, owner],
            device_id={"tm": to},
            device_id_type=MESH,
        )

    def filt_copy(r, to, owner):
        return pltpu.make_async_remote_copy(
            src_ref=filt.at[r, owner],
            dst_ref=filt.at[r, owner],
            send_sem=ag_send.at[r, to],
            recv_sem=ag_recv.at[r, owner],
            device_id={"tm": to},
            device_id_type=MESH,
        )

    relayed = n_t == 4
    near = [t + 1 - 2 * lax.rem(t, 2), lax.rem(t + 2, n_t)] if relayed else [peer(d) for d in range(1, n_t)]

    def relay_copy(r, k, to, owner):
        rows = pl.ds(k * (filt.shape[2] // 2), filt.shape[2] // 2)
        return pltpu.make_async_remote_copy(
            src_ref=filt.at[r, owner, rows],
            dst_ref=filt.at[r, owner, rows],
            send_sem=hand_send.at[r, k],
            recv_sem=hand_recv.at[r, k],
            device_id={"tm": to},
            device_id_type=MESH,
        )

    def pred_copy(to, owner):
        return pltpu.make_async_remote_copy(
            src_ref=pred_out.at[to],
            dst_ref=pred_in.at[owner],
            send_sem=q_send.at[to],
            recv_sem=q_recv.at[owner],
            device_id={"tm": to},
            device_id_type=MESH,
        )

    inward = jnp.where(z < half, 1, -1)

    def far_filt_copy(j, step):
        rows = pl.ds(j * BLK, BLK)
        return pltpu.make_async_remote_copy(
            src_ref=filt.at[first_round, :, rows, :],
            dst_ref=far_filt.at[:, rows, :],
            send_sem=far_filt_send.at[j],
            recv_sem=far_filt_recv.at[j],
            device_id={"vox": v + 2 * step},
            device_id_type=MESH,
        )

    def far_copy(j, ch, step):
        rows = pl.ds(ch * rc, rc)
        return pltpu.make_async_remote_copy(
            src_ref=far_out.at[j, rows],
            dst_ref=far_in.at[j, rows],
            send_sem=far_send.at[j, ch],
            recv_sem=far_recv.at[j, ch],
            device_id={"vox": v + 2 * step},
            device_id_type=MESH,
        )

    rounds = (first_round, 1 - first_round)
    for r in rounds:
        for d in range(n_t):
            u_copy(r, peer((d + 1) % n_t)).start()

    barrier = pltpu.get_barrier_semaphore()
    for d in range(1, n_t):
        pl.semaphore_signal(barrier, inc=1, device_id={"tm": peer(d)}, device_id_type=MESH)
    pl.semaphore_signal(barrier, inc=1, device_id={"vox": mate}, device_id_type=MESH)

    @pl.when(z > 0)
    def _():
        pl.semaphore_signal(barrier, inc=1, device_id={"vox": v - 2}, device_id_type=MESH)

    @pl.when(z < n_z - 1)
    def _():
        pl.semaphore_signal(barrier, inc=1, device_id={"vox": v + 2}, device_id_type=MESH)

    neighbours = jnp.where(z > 0, 1, 0) + jnp.where(z < n_z - 1, 1, 0)
    pl.semaphore_wait(barrier, n_t + neighbours)

    for ch in range(CHUNKS):

        @pl.when(z > 0)
        def _():
            line_copy(z, ch, -1, True).start()

        @pl.when(z < n_z - 1)
        def _():
            line_copy(z, ch, 1, True).start()

    pick = one_hot(live_ref, cap)
    lam = [lambda_ref[index_ref[i]] for i in range(blocks)]
    slot_lam = [sum(pick[j][i] * lam[i] for i in range(blocks)) for j in range(cap)]
    slot_live = [sum(pick[j][i] for i in range(blocks)) for j in range(cap)]

    y_cols = [y_ref[:, i * BLK : (i + 1) * BLK].astype(jnp.float32) for i in range(blocks)]
    y_t = jnp.concatenate(
        [sum(pick[j][i] * y_cols[i] for i in range(blocks)).T for j in range(cap)], axis=0
    ).astype(jnp.bfloat16)

    def make_parts(r, send):
        for d in range(1, n_t + 1):
            to = peer(d % n_t)
            u_copy(r, to).wait()

            def tile(i, _, to=to, d=d):
                off = pl.multiple_of(i * TILE, TILE)
                cols = pl.ds(pl.multiple_of(r * span + to * share + i * TILE, TILE), TILE)
                value = jnp.dot(y_t, u_buf[:, cols], preferred_element_type=jnp.float32)
                if d < n_t:
                    part_out[r, to, :, pl.ds(off, TILE)] = value.astype(jnp.bfloat16)
                else:
                    part_own[r, :, pl.ds(off, TILE)] = value
                return 0

            lax.fori_loop(0, share // TILE, tile, 0)
            if send and d < n_t:
                part_copy(r, to, t).start()

    def send_parts(r):
        for d in range(1, n_t):
            part_copy(r, peer(d), t).start()

    def filter_parts(r):
        for d in range(1, n_t):
            part_copy(r, peer(d), peer(d)).wait_recv()
        for i in range(share // TILE):
            cols = slice(i * TILE, (i + 1) * TILE)
            place = pl.multiple_of(r * span + t * share + i * TILE, TILE)
            sing = sing_ref[:, pl.ds(place, TILE)]
            for j in range(cap):
                rows = slice(j * BLK, (j + 1) * BLK)
                total = part_own[r, rows, cols]
                for d in range(1, n_t):
                    total = total + part_in[r, peer(d), rows, cols].astype(jnp.float32)
                factor = sing / (sing * sing + slot_lam[j]) * slot_live[j]
                filt[r, t, rows, cols] = (total * factor).astype(jnp.bfloat16)
        for to in near:
            filt_copy(r, to, t).start()

    def forward_filt(r):
        for to in near:
            filt_copy(r, to, to).wait_recv()
        if relayed:
            for k in range(2):
                relay_copy(r, k, near[k], near[1 - k]).start()

    def await_filt(r):
        if relayed:
            for k in range(2):
                relay_copy(r, k, near[k], n_t - 1 - t).wait_recv()

    make_parts(rounds[0], True)

    for ch in range(CHUNKS):
        pair_copy(z, ch, True).start()
        own_copy(ch).start()
    x_copy = pltpu.make_async_copy(x_ref, x_buf, x_sem)
    x_copy.start()

    make_parts(rounds[1], False)

    def relay(s, ch):
        low, high = z - 1 - s, z + 1 + s

        @pl.when((low >= 0) & holds(z, low))
        def _():
            line_copy(low, ch, -1).wait_recv()

            @pl.when((z < n_z - 1) & holds(z + 1, low))
            def _():
                line_copy(low, ch, 1).start()

            pair_copy(low, ch).start()

        @pl.when((high < n_z) & holds(z, high))
        def _():
            line_copy(high, ch, 1).wait_recv()

            @pl.when((z > 0) & holds(z - 1, high))
            def _():
                line_copy(high, ch, -1).start()

            pair_copy(high, ch).start()

    def product(values, slot, rows, factors):
        return lax.dot_general(
            values[slot, rows, :], factors, (((1,), (1,)), ((), ())),
            preferred_element_type=jnp.float32,
        )

    def place_of(slot):
        start = lax.rem(slot * depth, span)
        owner = start // share
        return owner, pl.ds(pl.multiple_of(start - owner * share, depth), depth)

    base = jnp.where(z == 1, half, 0) * 2

    def settle(ch):
        own_copy(ch).wait()

        def step(src, _):
            @pl.when(holds(z, src))
            def _():
                pair_arrival(src, ch).wait_recv()

            return 0

        lax.fori_loop(0, n_z, step, 0)

    def add_round(r, ch):
        rows = pl.ds(ch * rc, rc)

        def step(i, value):
            slot = r * half * 2 + i
            owner, inner = place_of(slot)
            return value + product(v_all, slot, rows, filt[r, owner, :, inner])

        value = jnp.zeros((rc, acc.shape[1]), jnp.float32)
        for i in range(2 * half):
            value = step(i, value)
        return value

    def far_half(ch):
        rows = pl.ds(ch * rc, rc)

        @pl.when(jnp.logical_not(is_end))
        def _():
            acc[rows, :] = add_round(rounds[0], ch)

        @pl.when(is_end)
        def _():
            acc[rows, :] = jnp.zeros((rc, acc.shape[1]), jnp.float32)

    def help_end(j, chunks):
        cols = slice(j * BLK, (j + 1) * BLK)

        @pl.when(is_helper)
        def _():
            if chunks[0] == 0:
                far_filt_copy(j, -inward).wait_recv()
            for ch in chunks:
                rows = pl.ds(ch * rc, rc)
                value = jnp.zeros((rc, BLK), jnp.float32)
                for i in range(2 * half):
                    owner, inner = place_of(base + i)
                    value += product(v_all, base + i, rows, far_filt[owner, cols, inner])
                far_out[j, rows, :] = value.astype(jnp.bfloat16)
                far_copy(j, ch, -inward).start()

    early, last = CHUNKS // 2, CHUNKS - 1
    for ch in range(early):
        relay(0, ch)
    filter_parts(rounds[0])
    for ch in range(early, last):
        relay(0, ch)
    forward_filt(rounds[0])
    send_parts(rounds[1])
    relay(0, last)
    await_filt(rounds[0])

    @pl.when(is_end)
    def _():
        for j in range(cap):
            far_filt_copy(j, inward).start()

    def relay_step(s, _):
        for ch in range(CHUNKS):
            relay(s, ch)
        return 0

    lax.fori_loop(1, n_z - 3, relay_step, 0)
    for ch in range(early):
        relay(n_z - 3, ch)
    filter_parts(rounds[1])
    for ch in range(early, last):
        relay(n_z - 3, ch)
    for ch in range(early):
        settle(ch)
        far_half(ch)
    forward_filt(rounds[1])
    for ch in range(early, last):
        settle(ch)
        far_half(ch)
    help_end(0, list(range(last)))
    relay(n_z - 3, last)
    settle(last)
    help_end(0, [last])
    far_half(last)
    help_end(1, list(range(CHUNKS)))
    for j in range(2, cap):
        help_end(j, list(range(CHUNKS)))
    await_filt(rounds[1])
    x_copy.wait()

    def finish(ch):
        rows = slice(ch * rc, (ch + 1) * rc)
        acc[rows, :] += add_round(rounds[1], ch)

        @pl.when(is_end)
        def _():
            for j in range(cap):
                cols = slice(j * BLK, (j + 1) * BLK)
                far_copy(j, ch, inward).wait_recv()
                acc[rows, cols] += far_in[j, rows, :].astype(jnp.float32)

        weights = acc[rows, :].astype(jnp.bfloat16)
        w_ref[rows, :] = weights
        value = jnp.dot(x_buf[:, rows], weights, preferred_element_type=jnp.float32)
        if ch == 0:
            pred_acc[...] = value
        else:
            pred_acc[...] += value

    for ch in range(CHUNKS):
        finish(ch)

    for d in range(1, n_t):
        to = peer(d)
        mine = pl.ds(pl.multiple_of(to * test_rows, test_rows), test_rows)
        pred_out[to] = pred_acc[mine, :].astype(jnp.bfloat16)
        pred_copy(to, t).start()
    for d in range(1, n_t):
        pred_copy(peer(d), peer(d)).wait_recv()
    total = pred_acc[pl.ds(pl.multiple_of(t * test_rows, test_rows), test_rows), :]
    for d in range(1, n_t):
        total = total + pred_in[peer(d)].astype(jnp.float32)
    pred_ref[...] = total.astype(jnp.bfloat16)

    for d in range(1, n_t):
        for r in rounds:
            part_copy(r, peer(d), t).wait_send()
        pred_copy(peer(d), t).wait_send()
    for r in rounds:
        for to in near:
            filt_copy(r, to, t).wait_send()
        if relayed:
            for k in range(2):
                relay_copy(r, k, near[k], near[1 - k]).wait_send()

    @pl.when(is_end)
    def _():
        for j in range(cap):
            far_filt_copy(j, inward).wait_send()

    @pl.when(is_helper)
    def _():
        for j in range(cap):
            for ch in range(CHUNKS):
                far_copy(j, ch, -inward).wait_send()

    def drain(src, _):
        for ch in range(CHUNKS):

            @pl.when(holds(z, src))
            def _():
                pair_copy(src, ch).wait_send()

            @pl.when((src <= z) & (z < n_z - 1) & holds(z, src) & holds(z + 1, src))
            def _():
                line_copy(src, ch, 1).wait_send()

            @pl.when((src >= z) & (z > 0) & holds(z, src) & holds(z - 1, src))
            def _():
                line_copy(src, ch, -1).wait_send()

        return 0

    lax.fori_loop(0, n_z, drain, 0)


def body(n_t, n_v, u_train, y_train, sing, lambdas, lam_index, live, v_basis, x_test):
    time_rows, features = u_train.shape
    columns = y_train.shape[1]
    blocks = lam_index.shape[0]
    cap = blocks - blocks // 3
    used = cap * BLK
    rows_v, depth = v_basis.shape
    tests = x_test.shape[0]
    share = features // n_t // 2
    n_z = n_v // 2
    low, full = jnp.bfloat16, jnp.float32
    smem = pl.BlockSpec(memory_space=pltpu.SMEM)
    vmem = pl.BlockSpec(memory_space=pltpu.VMEM)
    anywhere = pl.BlockSpec(memory_space=pl.ANY)
    dma = pltpu.SemaphoreType.DMA
    weights, predicted = pl.pallas_call(
        functools.partial(kernel, n_t, n_v, cap),
        out_shape=(
            jax.ShapeDtypeStruct((rows_v, used), low),
            jax.ShapeDtypeStruct((tests // n_t, used), low),
        ),
        in_specs=[smem, smem, smem, vmem, vmem, anywhere, anywhere, anywhere],
        out_specs=(vmem, vmem),
        scratch_shapes=[
            pltpu.VMEM((time_rows, features), low),
            pltpu.VMEM((tests, rows_v), low),
            pltpu.VMEM((n_v, rows_v, depth), low),
            pltpu.VMEM((2, n_t, used, share), low),
            pltpu.VMEM((2, n_t, used, share), low),
            pltpu.VMEM((2, used, share), full),
            pltpu.VMEM((2, n_t, used, share), low),
            pltpu.VMEM((rows_v, used), full),
            pltpu.VMEM((tests, used), full),
            pltpu.VMEM((n_t, tests // n_t, used), low),
            pltpu.VMEM((n_t, tests // n_t, used), low),
            dma((2, n_t)),
            dma,
            dma((CHUNKS,)),
            dma((n_z, CHUNKS)),
            dma((n_z, CHUNKS)),
            dma((n_z, CHUNKS)),
            dma((n_z, CHUNKS)),
            dma((n_z, CHUNKS)),
            dma((2, n_t)),
            dma((2, n_t)),
            dma((2, n_t)),
            dma((2, n_t)),
            dma((n_t,)),
            dma((n_t,)),
            pltpu.VMEM((n_t, used, share), low),
            pltpu.VMEM((cap, rows_v, BLK), low),
            pltpu.VMEM((cap, rows_v, BLK), low),
            dma((cap,)),
            dma((cap,)),
            dma((cap, CHUNKS)),
            dma((cap, CHUNKS)),
            dma((2, 2)),
            dma((2, 2)),
        ],
        compiler_params=pltpu.CompilerParams(collective_id=0, has_side_effects=True),
    )(live, lam_index, lambdas, sing.reshape(1, features), y_train, u_train, v_basis, x_test)
    return pl.pallas_call(
        functools.partial(expand, cap),
        out_shape=(
            jax.ShapeDtypeStruct((rows_v, columns), low),
            jax.ShapeDtypeStruct((tests // n_t, columns), low),
        ),
        in_specs=[smem, vmem, vmem],
        out_specs=(vmem, vmem),
    )(live, weights, predicted)


FAR_PARTS = (4, 4, 4, 8, 16, 32, 32)
SIDE_PARTS = (2, 4, 4)


def row_pieces(rows, parts):
    pieces, start = [], 0
    for part in parts:
        pieces.append((start, rows // part))
        start += rows // part
    return pieces


def widen(pick, values):
    wide = [values[:, j * BLK : (j + 1) * BLK] for j in range(len(pick))]
    return [sum(pick[j][i] * wide[j] for j in range(len(pick))) for i in range(len(pick[0]))]


def plane_kernel(
    cap,
    live_hbm,
    index_hbm,
    lambda_hbm,
    sing_hbm,
    y_hbm,
    u_hbm,
    v_hbm,
    x_hbm,
    w_ref,
    pred_ref,
    live_ref,
    index_ref,
    lambda_ref,
    sing_buf,
    y_buf,
    u_buf,
    x_buf,
    v_all,
    part_out,
    part_in,
    own,
    comb_out,
    comb_in,
    filt,
    far_filt,
    acc,
    pred_acc,
    far_out,
    far_in,
    pred_out,
    pred_in,
    lent,
    w_buf,
    in_sem,
    u_sem,
    own_sem,
    line_send,
    side_recv,
    across_recv,
    rows_recv,
    pair_send,
    pair_recv,
    pair_far_recv,
    part_send,
    part_recv,
    comb_send,
    comb_recv,
    ag_send,
    ag_recv,
    hand_send,
    hand_recv,
    plane_send,
    plane_recv,
    help_send,
    help_recv,
    q_send,
    q_recv,
    lend_recv,
    ready,
    reached,
):
    t = lax.axis_index("tm")
    v = lax.axis_index("vox")
    z, core = v // 2, v % 2
    mate = z * 2 + 1 - core
    rows_v, depth = v_hbm.shape
    blocks = live_ref.shape[0]
    share = depth
    span = 4 * share
    far_pieces = row_pieces(rows_v, FAR_PARTS)
    side_pieces = row_pieces(rows_v, SIDE_PARTS)
    whole = (0, rows_v)
    count = len(far_pieces)
    low_side = z < 2
    inward = jnp.where(low_side, 1, -1)
    is_end = (z == 0) | (z == 3)
    is_mid = jnp.logical_not(is_end)
    partner_z = jnp.where(is_end, z + inward, z - inward)
    partner = partner_z * 2 + core
    near_round = z // 2
    rounds = (1 - z % 2, z % 2)
    near = [t + 1 - 2 * lax.rem(t, 2), lax.rem(t + 2, 4)]
    diag = 3 - t
    scope = jax.named_scope

    def remote(src, dst, send, recv, **place):
        return pltpu.make_async_remote_copy(
            src_ref=src, dst_ref=dst, send_sem=send, recv_sem=recv, device_id=place, device_id_type=MESH
        )

    def slot_of(zz, cc):
        return zz * 2 + cc

    def block_of(slot, piece):
        cols = pl.ds(pl.multiple_of((slot % 4) * depth, depth), depth)
        return v_all.at[slot // 4, pl.ds(*piece), cols]

    far_mid, far_end = 3 - z, 3 - partner_z
    across_mate = (z + inward) * 2 + 1 - core

    def side_copy(piece, recv):
        return remote(v_hbm.at[pl.ds(*piece)], block_of(v, piece), line_send.at[0], recv, vox=partner)

    def side_wait(piece, recv):
        at = block_of(partner, piece)
        remote(at, at, line_send.at[0], recv, vox=partner).wait_recv()

    def across_copy():
        return remote(v_hbm, block_of(v, whole), line_send.at[1], across_recv, vox=v + 2 * inward)

    def across_wait():
        at = block_of(slot_of(far_mid, core), whole)
        remote(at, at, line_send.at[1], across_recv, vox=v + 2 * inward).wait_recv()

    def line_relay(i):
        at = block_of(partner, far_pieces[i])
        return remote(at, at, line_send.at[2], rows_recv.at[i], vox=v + 2 * inward)

    direct = (count - 2, count - 1)
    direct_rows = rows_v - far_pieces[direct[0]][0]

    def line_relay_other(i):
        at = block_of(partner, far_pieces[i])
        return remote(at, at, line_send.at[3], pair_far_recv.at[i], vox=across_mate)

    def line_relay_wait(i):
        at = block_of(slot_of(far_end, core), far_pieces[i])
        remote(at, at, line_send.at[2], rows_recv.at[i], vox=v + 2 * inward).wait_recv()

    def pair_copy(k):
        src = v_hbm if k == 0 else block_of(pair_slot(k, core), whole)
        return remote(src, block_of(pair_slot(k, core), whole), pair_send.at[k], pair_recv.at[k], vox=mate)

    def pair_slot(k, cc):
        return slot_of((z, partner_z, far_mid)[k], cc)

    def pair_wait(k):
        at = block_of(pair_slot(k, 1 - core), whole)
        remote(at, at, pair_send.at[k], pair_recv.at[k], vox=mate).wait_recv()

    def pair_far_copy(i):
        at = block_of(slot_of(far_end, core), far_pieces[i])
        return remote(at, at, pair_send.at[3], pair_far_recv.at[i], vox=mate)

    def pair_far_wait(i):
        at = block_of(slot_of(far_end, 1 - core), far_pieces[i])
        remote(at, at, pair_send.at[3], pair_far_recv.at[i], vox=mate).wait_recv()

    def own_copy():
        return pltpu.make_async_copy(v_hbm, block_of(v, whole), own_sem)

    def rows_of(i):
        return pl.ds(*far_pieces[i])

    def u_copy(i):
        first, width = (owners[i] * share, share) if i < 4 else (0, span)
        cols = pl.ds(pl.multiple_of(rounds[i // 4] * span + first, share), width)
        return pltpu.make_async_copy(u_hbm.at[:, cols], u_buf.at[:, cols], u_sem.at[i])

    def half(i):
        return pl.ds(i * BLK, BLK)

    def rank(owner):
        return pl.ds(pl.multiple_of(owner * share, share), share)

    def part_copy(o, j, s):
        return remote(part_out.at[o, j, s], part_in.at[o, j, s], part_send, part_recv.at[o, s], tm=near[j])

    def comb_copy(o, j):
        return remote(comb_out.at[o, j], comb_in.at[o, j], comb_send, comb_recv.at[o], tm=near[1 - j])

    def ag_copy(o, i, owner):
        at = filt.at[o, rank(owner)]
        return remote(at, at, ag_send, ag_recv.at[o], tm=near[i])

    def hand_copy(o, i, owner):
        at = filt.at[o, rank(owner), half(i)]
        return remote(at, at, hand_send, hand_recv.at[o], tm=near[i])

    def half_copy(i, owner):
        at = filt.at[0, rank(owner), half(i)]
        return remote(at, at, plane_send, plane_recv, tm=near[i])

    def far_filt_copy(k):
        if k == 0:
            src, dst = filt.at[0, rank(t)], far_filt.at[rank(t)]
        else:
            src, dst = filt.at[0, rank(near[k - 1]), half(k - 1)], far_filt.at[rank(near[k - 1]), half(k - 1)]
        return remote(src, dst, help_send, help_recv.at[k], vox=partner)

    def far_filt_wait(k):
        at = far_filt.at[rank(t)] if k == 0 else far_filt.at[rank(near[k - 1]), half(k - 1)]
        remote(at, at, help_send, help_recv.at[k], vox=partner).wait_recv()

    def cross_copy(s, i, owner):
        at = far_filt.at[rank(owner), half(1 - i)]
        return remote(at, at, plane_send, plane_recv, tm=near[i])

    def far_copy(ch):
        return remote(
            far_out.at[rows_of(ch)], far_in.at[rows_of(ch)], help_send, rows_recv.at[ch], vox=partner
        )

    test_rows = pred_out.shape[1]
    strip = test_rows // 2

    def lend_copy(j, k):
        at = (pl.ds(k * strip, strip), half(j))
        return remote(pred_out.at[(2, *at)], lent.at[at], q_send, lend_recv.at[k], tm=near[j])

    def pred_copy(i, j, rows):
        at = (i, rows, half(j))
        return remote(pred_out.at[at], pred_in.at[at], q_send, q_recv, tm=near[i])

    barrier = pltpu.get_barrier_semaphore()

    bits = (lax.rem(t, 2), t // 2, core)
    pairs = ({"tm": near[0]}, {"tm": near[1]}, {"vox": mate})

    def signal(sem, place):
        pl.semaphore_signal(sem, inc=1, device_id=place, device_id_type=MESH)

    for bit, place in zip(bits, pairs):

        @pl.when(bit == 0)
        def _():
            signal(barrier, place)

    @pl.when(z < 3)
    def _():
        signal(barrier, {"vox": v + 2})

    @pl.when(z == 2)
    def _():
        signal(barrier, {"vox": v - 2})

    y_copy = pltpu.make_async_copy(y_hbm, y_buf, in_sem.at[0])
    sing_copy = pltpu.make_async_copy(sing_hbm, sing_buf, in_sem.at[1])
    x_copy = pltpu.make_async_copy(x_hbm, x_buf, in_sem.at[2])
    owners = (diag, near[0], near[1], t)
    y_copy.start()
    for i in range(4):
        u_copy(i).start()
    sing_copy.start()
    scalars = [
        pltpu.make_async_copy(live_hbm, live_ref, in_sem.at[3]),
        pltpu.make_async_copy(index_hbm, index_ref, in_sem.at[4]),
        pltpu.make_async_copy(lambda_hbm, lambda_ref, in_sem.at[5]),
    ]
    for copy in scalars:
        copy.start()

    with scope("bar"):
        callers = sum(bits) + jnp.where(z == 0, 0, jnp.where(z == 1, 2, 1))

        @pl.when(callers > 0)
        def _():
            pl.semaphore_wait(barrier, callers)


    @pl.when(is_mid)
    def _():
        across_copy().start()

    for bit, place in zip(bits, pairs):

        @pl.when(bit == 1)
        def _():
            signal(ready, place)

    @pl.when((z == 1) | (z == 3))
    def _():
        signal(ready, {"vox": v - 2})

    u_copy(4).start()

    for copy in scalars:
        copy.wait()
    pick = one_hot(live_ref, cap)
    lam = [lambda_ref[index_ref[i]] for i in range(blocks)]
    slot_lam = [sum(pick[j][i] * lam[i] for i in range(blocks)) for j in range(cap)]
    slot_live = [sum(pick[j][i] for i in range(blocks)) for j in range(cap)]

    with scope("ycp"):
        y_copy.wait()
    y_cols = [y_buf[:, i * BLK : (i + 1) * BLK].astype(jnp.float32) for i in range(blocks)]
    y_t = jnp.concatenate(
        [sum(pick[j][i] * y_cols[i] for i in range(blocks)).T for j in range(cap)], axis=0
    ).astype(jnp.bfloat16)

    def greet():
        with scope("ready"):
            answers = 3 - sum(bits) + jnp.where((z == 0) | (z == 2), 1, 0)

            @pl.when(answers > 0)
            def _():
                pl.semaphore_wait(ready, answers)


        @pl.when(is_mid)
        def _():
            side_copy(whole, side_recv.at[0]).start()

        @pl.when(is_end)
        def _():
            side_copy(side_pieces[0], side_recv.at[0]).start()

    def make_parts(o):
        if o == 1:
            u_copy(4).wait()
        for i in range(4):
            if o == 0:
                u_copy(i).wait()
            for tile in range(share // TILE):
                into = slice(tile * TILE, (tile + 1) * TILE)
                start = rounds[o] * span + owners[i] * share + tile * TILE
                cols = pl.ds(pl.multiple_of(start, TILE), TILE)
                value = jnp.dot(y_t, u_buf[:, cols], preferred_element_type=jnp.float32)
                first, second = value[:BLK], value[BLK:]
                if i == 0:
                    part_out[o, 0, 1, :, into] = first.astype(jnp.bfloat16)
                    part_out[o, 1, 1, :, into] = second.astype(jnp.bfloat16)
                elif i == 1:
                    part_out[o, 0, 0, :, into] = first.astype(jnp.bfloat16)
                    own[o, 1, 1, :, into] = second
                elif i == 2:
                    own[o, 0, 1, :, into] = first
                    part_out[o, 1, 0, :, into] = second.astype(jnp.bfloat16)
                else:
                    own[o, 0, 0, :, into] = first
                    own[o, 1, 0, :, into] = second
            if o == 0 and i == 0:
                greet()
                for j in range(2):
                    part_copy(o, j, 1).start()
            if o == 0 and i in (1, 2):
                part_copy(o, i - 1, 0).start()

    def received(ref, sem):
        remote(ref, ref, q_send, sem, vox=mate).wait_recv()

    def combine(o):
        received(part_in.at[o, :, 1], part_recv.at[o, 1])
        for j in range(2):
            comb_out[o, j] = (own[o, j, 1] + part_in[o, j, 1].astype(jnp.float32)).astype(jnp.bfloat16)
            comb_copy(o, j).start()

    def filter_parts(o):
        place = pl.multiple_of(rounds[o] * span + t * share, share)
        sing = sing_buf[:, pl.ds(place, share)]
        received(part_in.at[o, :, 0], part_recv.at[o, 0])
        received(comb_in.at[o], comb_recv.at[o])
        for j in range(cap):
            total = own[o, j, 0] + part_in[o, j, 0].astype(jnp.float32) + comb_in[o, j].astype(jnp.float32)
            factor = sing / (sing * sing + slot_lam[j]) * slot_live[j]
            filt[o, rank(t), half(j)] = (total * factor).T.astype(jnp.bfloat16)

    def send_filt(o):
        for i in range(2):
            ag_copy(o, i, t).start()

    def forward_filt(o):
        received(filt.at[o, pl.ds(0, 2 * share)], ag_recv.at[o])
        for i in range(2):
            hand_copy(o, i, near[1 - i]).start()

    def await_filt(o):
        received(filt.at[o, pl.ds(0, share)], hand_recv.at[o])

    with scope("mp0"):
        make_parts(0)
    with scope("mp1"):
        make_parts(1)
    pair_copy(0).start()
    own_copy().start()
    x_copy.start()
    sing_copy.wait()

    def near_product(o, rows):
        return jnp.dot(v_all[near_round, rows, :], filt[o], preferred_element_type=jnp.float32)

    def far_product(rows, factors):
        return jnp.dot(v_all[1 - near_round, rows, :], factors, preferred_element_type=jnp.float32)

    def near_rows(o):
        own_copy().wait()
        pair_wait(0)
        pair_wait(1)
        for i in range(4):
            rows = pl.ds(i * (rows_v // 4), rows_v // 4)
            acc[rows, :] = near_product(o, rows)

    def predict(piece):
        rows = pl.ds(*piece)
        part = jnp.dot(x_buf[:, rows], w_buf[rows, :], preferred_element_type=jnp.float32)
        if piece[0] == 0:
            pred_acc[...] = part
        else:
            pred_acc[...] += part

    def predict_last(piece):
        rows = pl.ds(*piece)
        for k in range(2):
            here = pl.ds(k * strip, strip)
            mine = pl.ds(pl.multiple_of(diag * test_rows + k * strip, strip), strip)
            value = pred_acc[mine, :] + jnp.dot(x_buf[mine, rows], w_buf[rows, :], preferred_element_type=jnp.float32)
            pred_out[2, here, :] = value.astype(jnp.bfloat16)
            for j in range(2):
                lend_copy(j, k).start()
        for i, to in ((3, t), (0, near[0]), (1, near[1])):
            mine = pl.ds(pl.multiple_of(to * test_rows, test_rows), test_rows)
            value = pred_acc[mine, :] + jnp.dot(x_buf[mine, rows], w_buf[rows, :], preferred_element_type=jnp.float32)
            pred_acc[mine, :] = value
            if i < 2:
                pred_out[i, :, i * BLK : (i + 1) * BLK] = value[:, i * BLK : (i + 1) * BLK].astype(jnp.bfloat16)

                @pl.when(core == 0)
                def _():
                    pred_copy(i, i, pl.ds(0, test_rows)).start()

    def direct_lead():
        @pl.when(core == 1)
        def _():
            for i in range(2):
                pred_copy(i, i, pl.ds(0, test_rows)).start()

    def hand_on():
        for k in range(2):
            if k == 1:
                direct_lead()
            received(lent.at[pl.ds(k * strip, strip)], lend_recv.at[k])
            for j in range(2):
                to = near[1 - j]
                mine = pl.ds(pl.multiple_of(to * test_rows + k * strip, strip), strip)
                here = pl.ds(k * strip, strip)
                value = pred_acc[mine, half(j)] + lent[here, half(j)].astype(jnp.float32)
                pred_out[1 - j, here, half(j)] = value.astype(jnp.bfloat16)
                pred_copy(1 - j, j, here).start()

    def put_rows(piece):
        rows = pl.ds(*piece)
        for i, block in enumerate(widen(pick, w_buf[rows, :].astype(jnp.float32))):
            w_ref[rows, i * BLK : (i + 1) * BLK] = block.astype(jnp.bfloat16)

    head = (0, far_pieces[3][0])
    rest = (head[1], rows_v - head[1])
    last_rows = (far_pieces[4][0], rows_v - far_pieces[4][0])

    @pl.when(is_mid)
    def _():
        def arrive(i, lead=False):
            line_relay_wait(i)
            if lead or i not in direct:
                pair_far_copy(i).start()

        def help_end(*which):
            for i in which:
                pair_far_wait(i)
            first = far_pieces[which[0]][0]
            rows = pl.ds(first, sum(far_pieces[i][1] for i in which))
            far_out[rows, :] = far_product(rows, far_filt[...]).astype(jnp.bfloat16)
            for i in which:
                far_copy(i).start()

        def own_rows(piece):
            rows = pl.ds(*piece)
            w_buf[rows, :] = (acc[rows, :] + far_product(rows, filt[1])).astype(jnp.bfloat16)

        with scope("m_comb0"):
            combine(0)
            for s in (1, 0):
                for j in range(2):
                    part_copy(1, j, s).start()
        with scope("m_filt0"):
            filter_parts(0)
            send_filt(0)
        with scope("m_side0"):
            side_wait(side_pieces[0], side_recv.at[0])
            for i in range(2):
                line_relay(i).start()
        with scope("m_comb1"):
            combine(1)
        with scope("m_ff0"):
            far_filt_wait(0)
            for i in range(2):
                cross_copy(0, i, t).start()
        with scope("m_fw0"):
            forward_filt(0)
        with scope("m_across"):
            across_wait()
            pair_copy(2).start()
        with scope("m_ff1"):
            for k in (1, 2):
                far_filt_wait(k)
            for i in range(2):
                cross_copy(1, i, near[1 - i]).start()
        with scope("m_filt1"):
            filter_parts(1)
            send_filt(1)
        def tail_lead():
            with scope("m_far0"):
                arrive(0, True)
            side_last(1)
            with scope("m_cross"):
                await_cross()
            with scope("m_help0"):
                help_end(0)
            side_last(2)
            with scope("m_far1"):
                arrive(1, True)
            with scope("m_fw1"):
                forward_filt(1)
            with scope("m_help1"):
                help_end(1)
            with scope("m_aw0"):
                await_filt(0)
            with scope("m_near"):
                near_rows(0)
            for i in (2, 3):
                with scope(f"m_far{i}"):
                    arrive(i, True)
            with scope("m_aw1"):
                await_filt(1)
            with scope("m_own0"):
                for i in range(2):
                    own_rows(far_pieces[i])
            with scope("m_help2"):
                help_end(2)
            with scope("m_far4"):
                arrive(4, True)
            with scope("m_own1"):
                own_rows(far_pieces[2])
            for i in (5, 6):
                with scope(f"m_far{i}"):
                    arrive(i, True)
            with scope("m_help3"):
                help_end(3)
            with scope("m_help4"):
                help_end(4, 5, 6)
            x_copy.wait()
            with scope("m_pred0"):
                predict(head)

        def tail_late():
            with scope("m_far0"):
                arrive(0)
            side_last(1)
            with scope("m_cross"):
                await_cross()
            with scope("m_help0"):
                help_end(0)
            side_last(2)
            with scope("m_far1"):
                arrive(1)
            with scope("m_help1"):
                help_end(1)
            with scope("m_fw1"):
                forward_filt(1)
            with scope("m_aw0"):
                await_filt(0)
            with scope("m_near"):
                near_rows(0)
            with scope("m_far2"):
                arrive(2)
            with scope("m_help2"):
                help_end(2)
            with scope("m_aw1"):
                await_filt(1)
            x_copy.wait()
            with scope("m_own0"):
                own_rows(far_pieces[0])
            with scope("m_far3"):
                arrive(3)
            with scope("m_help3"):
                help_end(3)
            with scope("m_own1"):
                for i in (1, 2):
                    own_rows(far_pieces[i])
            with scope("m_far4"):
                arrive(4)
            with scope("m_help4"):
                help_end(4)
            with scope("m_far6"):
                arrive(5)
                arrive(6)
            with scope("m_help5"):
                help_end(5, 6)
            with scope("m_pred0"):
                predict(head)

        def side_last(k):
            with scope(f"m_side{k}"):
                side_wait(side_pieces[k], side_recv.at[k])
                if k == 1:
                    line_relay(2).start()
                    return
                for i in range(3, count):
                    line_relay(i).start()
                pair_copy(1).start()

            @pl.when(core == 0)
            def _():
                pl.semaphore_wait(reached, 1)
                for i in direct:
                    line_relay_other(i).start()

        def await_cross():
            received(far_filt.at[pl.ds(0, 2 * share)], plane_recv)
            pair_wait(2)

            @pl.when(core == 1)
            def _():
                signal(reached, {"vox": across_mate})


        pl.when(core == 1)(tail_lead)
        pl.when(core == 0)(tail_late)
        with scope("m_last"):
            own_rows(rest)
            predict_last(rest)
        put_rows(whole)

    @pl.when(is_end)
    def _():
        with scope("e_comb0"):
            combine(0)
            for j in range(2):
                part_copy(1, j, 1).start()
        with scope("e_filt0"):
            filter_parts(0)
            far_filt_copy(0).start()
            for i in range(2):
                half_copy(i, t).start()
            for j in range(2):
                part_copy(1, j, 0).start()
        with scope("e_half"):
            received(filt.at[0, pl.ds(0, share)], plane_recv)
            for i in range(2):
                far_filt_copy(1 + i).start()
            for i in range(1, len(side_pieces)):
                side_copy(side_pieces[i], side_recv.at[i]).start()
        with scope("e_comb1"):
            combine(1)
        with scope("e_filt1"):
            filter_parts(1)
            send_filt(1)
        with scope("e_side"):
            side_wait(whole, side_recv.at[0])
            pair_copy(1).start()
        with scope("e_fw1"):
            forward_filt(1)
        x_copy.wait()
        with scope("e_aw1"):
            await_filt(1)
        with scope("e_near"):
            near_rows(1)

        def add_far(piece):
            rows = pl.ds(*piece)
            w_buf[rows, :] = (acc[rows, :] + far_in[rows, :].astype(jnp.float32)).astype(jnp.bfloat16)

        for i in range(3):
            with scope(f"e_far{i}"):
                far_copy(i).wait_recv()
            add_far(far_pieces[i])
            predict(far_pieces[i])
            put_rows(far_pieces[i])
        with scope("e_far3"):
            far_copy(3).wait_recv()
        add_far(far_pieces[3])
        predict(far_pieces[3])
        with scope("e_far4"):
            for i in range(4, count):
                far_copy(i).wait_recv()
        with scope("e_last"):
            add_far(last_rows)
            predict_last(last_rows)
        put_rows(rest)

    with scope("hand"):
        hand_on()
    with scope("pwait"):
        remote(pred_in, pred_in, q_send, q_recv, vox=mate).wait_recv()
    total = pred_acc[pl.ds(pl.multiple_of(t * test_rows, test_rows), test_rows), :]
    for i in range(2):
        total = total + pred_in[i].astype(jnp.float32)
    total = total.astype(jnp.bfloat16).astype(jnp.float32)
    for i, block in enumerate(widen(pick, total)):
        pred_ref[:, i * BLK : (i + 1) * BLK] = block.astype(jnp.bfloat16)

    def sent(ref, sem):
        remote(ref, ref, sem, q_recv, vox=mate).wait_send()

    with scope("drain"):
        sent(part_out, part_send)
        sent(comb_out, comb_send)
        sent(pred_out, q_send)
        sent(v_all.at[0, :, pl.ds(0, depth)], line_send.at[0])
        for k in range(2):
            sent(v_all.at[0, :, pl.ds(0, depth)], pair_send.at[k])

        @pl.when(is_mid)
        def _():
            for k in range(1, 3):
                sent(v_all.at[0, :, pl.ds(0, depth)], line_send.at[k])
            sent(v_all.at[0, :, pl.ds(0, depth)], pair_send.at[2])

            @pl.when(core == 0)
            def _():
                sent(v_all.at[0, pl.ds(0, direct_rows), pl.ds(0, depth)], line_send.at[3])
                sent(v_all.at[0, pl.ds(0, rows_v - direct_rows), pl.ds(0, depth)], pair_send.at[3])

            @pl.when(core == 1)
            def _():
                sent(v_all.at[0, :, pl.ds(0, depth)], pair_send.at[3])

            sent(filt.at[0], ag_send)
            sent(filt.at[0, pl.ds(0, 2 * share)], hand_send)
            sent(far_filt.at[pl.ds(0, 2 * share)], plane_send)
            sent(far_out, help_send)

        @pl.when(is_end)
        def _():
            sent(filt.at[0, pl.ds(0, 2 * share)], ag_send)
            sent(filt.at[0, pl.ds(0, share)], hand_send)
            sent(filt.at[0, pl.ds(0, share)], plane_send)
            sent(filt.at[0, pl.ds(0, 2 * share)], help_send)


def put_out(w_in, pred_in, w_ref, pred_ref, sem):
    copies = [
        pltpu.make_async_copy(w_in, w_ref, sem.at[0]),
        pltpu.make_async_copy(pred_in, pred_ref, sem.at[1]),
    ]
    for copy in copies:
        copy.start()
    for copy in copies:
        copy.wait()


def plane_body(u_train, y_train, sing, lambdas, lam_index, live, v_basis, x_test):
    time_rows, features = u_train.shape
    columns = y_train.shape[1]
    blocks = lam_index.shape[0]
    cap = blocks - blocks // 3
    used = cap * BLK
    rows_v, depth = v_basis.shape
    tests = x_test.shape[0]
    share = depth
    count = len(FAR_PARTS)
    low, full = jnp.bfloat16, jnp.float32
    vmem = pl.BlockSpec(memory_space=pltpu.VMEM)
    anywhere = pl.BlockSpec(memory_space=pl.ANY)
    dma = pltpu.SemaphoreType.DMA
    weights, predicted = pl.pallas_call(
        functools.partial(plane_kernel, cap),
        out_shape=(pltpu.VMEM((rows_v, columns), low), pltpu.VMEM((tests // 4, columns), low)),
        in_specs=[anywhere] * 8,
        out_specs=(vmem, vmem),
        scratch_shapes=[
            pltpu.SMEM(live.shape, live.dtype),
            pltpu.SMEM(lam_index.shape, lam_index.dtype),
            pltpu.SMEM(lambdas.shape, lambdas.dtype),
            pltpu.VMEM((1, features), full),
            pltpu.VMEM((time_rows, columns), low),
            pltpu.VMEM((time_rows, features), low),
            pltpu.VMEM((tests, rows_v), low),
            pltpu.VMEM((2, rows_v, 4 * depth), low),
            pltpu.VMEM((2, 2, 2, BLK, share), low),
            pltpu.VMEM((2, 2, 2, BLK, share), low),
            pltpu.VMEM((2, 2, 2, BLK, share), full),
            pltpu.VMEM((2, 2, BLK, share), low),
            pltpu.VMEM((2, 2, BLK, share), low),
            pltpu.VMEM((2, 4 * share, used), low),
            pltpu.VMEM((4 * share, used), low),
            pltpu.VMEM((rows_v, used), full),
            pltpu.VMEM((tests, used), full),
            pltpu.VMEM((rows_v, used), low),
            pltpu.VMEM((rows_v, used), low),
            pltpu.VMEM((3, tests // 4, used), low),
            pltpu.VMEM((2, tests // 4, used), low),
            pltpu.VMEM((tests // 4, used), low),
            pltpu.VMEM((rows_v, used), low),
            dma((6,)),
            dma((5,)),
            dma,
            dma((4,)),
            dma((len(SIDE_PARTS),)),
            dma,
            dma((count,)),
            dma((4,)),
            dma((3,)),
            dma((count,)),
            dma,
            dma((2, 2)),
            dma,
            dma((2,)),
            dma,
            dma((2,)),
            dma,
            dma((2,)),
            dma,
            dma,
            dma,
            dma((3,)),
            dma,
            dma,
            dma((2,)),
            pltpu.SemaphoreType.REGULAR,
            pltpu.SemaphoreType.REGULAR,
        ],
        compiler_params=pltpu.CompilerParams(
            collective_id=1, has_side_effects=True
        ),
    )(live, lam_index, lambdas, sing.reshape(1, features), y_train, u_train, v_basis, x_test)
    weights = pltpu.with_memory_space_constraint(weights, pltpu.VMEM)
    predicted = pltpu.with_memory_space_constraint(predicted, pltpu.VMEM)
    return pl.pallas_call(
        put_out,
        out_shape=(
            jax.ShapeDtypeStruct((rows_v, columns), low),
            jax.ShapeDtypeStruct((tests // 4, columns), low),
        ),
        in_specs=[anywhere, anywhere],
        out_specs=(anywhere, anywhere),
        scratch_shapes=[dma((2,))],
    )(weights, predicted)


def routed(n_t, n_v, *args):
    if (n_t, n_v, args[4].shape[0]) == (4, 8, 3):
        return plane_body(*args)
    return body(n_t, n_v, *args)


def solution(mesh):
    placed = (
        P("tm", None),
        P("tm", "vox"),
        P(),
        P(),
        P("vox"),
        P("vox"),
        P("tm", "vox"),
        P(None, "tm"),
    )
    return jax.shard_map(
        functools.partial(routed, mesh.shape["tm"], mesh.shape["vox"]),
        mesh=mesh,
        in_specs=placed,
        out_specs=(P("tm", "vox"), P("tm", "vox")),
        check_vma=False,
    )
```

```python
import functools

import jax
import jax.numpy as jnp
from jax import lax
from jax.experimental import pallas as pl
from jax.experimental.pallas import tpu as pltpu
from jax.sharding import PartitionSpec as P

BLK = 128
CHUNKS = 4
TILE = 256
MESH = pl.DeviceIdType.MESH


def one_hot(live_ref, cap):
    blocks = live_ref.shape[0]
    live = [live_ref[i] for i in range(blocks)]
    before = [sum(live[:i], jnp.int32(0)) for i in range(blocks)]
    return [
        [jnp.where(before[i] == j, live[i], 0).astype(jnp.float32) for i in range(blocks)]
        for j in range(cap)
    ]


def expand(cap, live_ref, w_in, pred_in, w_ref, pred_ref):
    pick = one_hot(live_ref, cap)
    for source, target in ((w_in, w_ref), (pred_in, pred_ref)):
        values = [source[:, j * BLK : (j + 1) * BLK].astype(jnp.float32) for j in range(cap)]
        for i in range(live_ref.shape[0]):
            block = sum(pick[j][i] * values[j] for j in range(cap))
            target[:, i * BLK : (i + 1) * BLK] = block.astype(target.dtype)


def kernel(
    n_t,
    n_v,
    cap,
    live_ref,
    index_ref,
    lambda_ref,
    sing_ref,
    y_ref,
    u_ref,
    v_ref,
    x_ref,
    w_ref,
    pred_ref,
    u_buf,
    x_buf,
    v_all,
    part_out,
    part_in,
    part_own,
    filt,
    acc,
    pred_acc,
    pred_out,
    pred_in,
    u_sem,
    x_sem,
    own_sem,
    right_sem,
    left_sem,
    line_sem,
    pair_send,
    pair_recv,
    rs_send,
    rs_recv,
    ag_send,
    ag_recv,
    q_send,
    q_recv,
    far_filt,
    far_out,
    far_in,
    far_filt_send,
    far_filt_recv,
    far_send,
    far_recv,
    hand_send,
    hand_recv,
):
    t = lax.axis_index("tm")
    v = lax.axis_index("vox")
    n_z = n_v // 2
    z, core = v // 2, v % 2
    mate = z * 2 + 1 - core
    rows_v, depth = v_ref.shape
    blocks = live_ref.shape[0]
    share = part_own.shape[2]
    half = n_z // 2
    span = n_t * share
    first_round = jnp.where(z < half, 1, 0)
    at_low, at_high = z == 0, z == n_z - 1
    is_end = at_low | at_high
    is_helper = (z == 1) | (z == n_z - 2)

    def holds(zz, src):
        return jnp.logical_not(
            ((zz == 0) & (src >= half)) | ((zz == n_z - 1) & (src < half))
        )
    test_rows = pred_out.shape[1]
    rc = rows_v // CHUNKS

    def u_copy(r, owner):
        cols = pl.ds(pl.multiple_of(r * span + owner * share, share), share)
        return pltpu.make_async_copy(u_ref.at[:, cols], u_buf.at[:, cols], u_sem.at[r, owner])

    def own_copy(ch):
        rows = pl.ds(ch * rc, rc)
        return pltpu.make_async_copy(v_ref.at[rows], v_all.at[v, rows], own_sem.at[ch])

    def line_copy(src, ch, step, first=False):
        rows = pl.ds(ch * rc, rc)
        slot = src * 2 + core
        return pltpu.make_async_remote_copy(
            src_ref=v_ref.at[rows] if first else v_all.at[slot, rows],
            dst_ref=v_all.at[slot, rows],
            send_sem=(right_sem if step > 0 else left_sem).at[src, ch],
            recv_sem=line_sem.at[src, ch],
            device_id={"vox": v + 2 * step},
            device_id_type=MESH,
        )

    def pair_copy(src, ch, first=False):
        rows = pl.ds(ch * rc, rc)
        slot = src * 2 + core
        return pltpu.make_async_remote_copy(
            src_ref=v_ref.at[rows] if first else v_all.at[slot, rows],
            dst_ref=v_all.at[slot, rows],
            send_sem=pair_send.at[src, ch],
            recv_sem=pair_recv.at[src, ch],
            device_id={"vox": mate},
            device_id_type=MESH,
        )

    def pair_arrival(src, ch):
        rows = pl.ds(ch * rc, rc)
        slot = src * 2 + 1 - core
        return pltpu.make_async_remote_copy(
            src_ref=v_all.at[slot, rows],
            dst_ref=v_all.at[slot, rows],
            send_sem=pair_send.at[src, ch],
            recv_sem=pair_recv.at[src, ch],
            device_id={"vox": mate},
            device_id_type=MESH,
        )

    def peer(d):
        return lax.rem(t + d, n_t)

    def part_copy(r, to, owner):
        return pltpu.make_async_remote_copy(
            src_ref=part_out.at[r, to],
            dst_ref=part_in.at[r, owner],
            send_sem=rs_send.at[r, to],
            recv_sem=rs_recv.at[r, owner],
            device_id={"tm": to},
            device_id_type=MESH,
        )

    def filt_copy(r, to, owner):
        return pltpu.make_async_remote_copy(
            src_ref=filt.at[r, owner],
            dst_ref=filt.at[r, owner],
            send_sem=ag_send.at[r, to],
            recv_sem=ag_recv.at[r, owner],
            device_id={"tm": to},
            device_id_type=MESH,
        )

    relayed = n_t == 4
    near = [t + 1 - 2 * lax.rem(t, 2), lax.rem(t + 2, n_t)] if relayed else [peer(d) for d in range(1, n_t)]

    def relay_copy(r, k, to, owner):
        rows = pl.ds(k * (filt.shape[2] // 2), filt.shape[2] // 2)
        return pltpu.make_async_remote_copy(
            src_ref=filt.at[r, owner, rows],
            dst_ref=filt.at[r, owner, rows],
            send_sem=hand_send.at[r, k],
            recv_sem=hand_recv.at[r, k],
            device_id={"tm": to},
            device_id_type=MESH,
        )

    def pred_copy(to, owner):
        return pltpu.make_async_remote_copy(
            src_ref=pred_out.at[to],
            dst_ref=pred_in.at[owner],
            send_sem=q_send.at[to],
            recv_sem=q_recv.at[owner],
            device_id={"tm": to},
            device_id_type=MESH,
        )

    inward = jnp.where(z < half, 1, -1)

    def far_filt_copy(j, step):
        rows = pl.ds(j * BLK, BLK)
        return pltpu.make_async_remote_copy(
            src_ref=filt.at[first_round, :, rows, :],
            dst_ref=far_filt.at[:, rows, :],
            send_sem=far_filt_send.at[j],
            recv_sem=far_filt_recv.at[j],
            device_id={"vox": v + 2 * step},
            device_id_type=MESH,
        )

    def far_copy(j, ch, step):
        rows = pl.ds(ch * rc, rc)
        return pltpu.make_async_remote_copy(
            src_ref=far_out.at[j, rows],
            dst_ref=far_in.at[j, rows],
            send_sem=far_send.at[j, ch],
            recv_sem=far_recv.at[j, ch],
            device_id={"vox": v + 2 * step},
            device_id_type=MESH,
        )

    rounds = (first_round, 1 - first_round)
    for r in rounds:
        for d in range(n_t):
            u_copy(r, peer((d + 1) % n_t)).start()

    barrier = pltpu.get_barrier_semaphore()
    for d in range(1, n_t):
        pl.semaphore_signal(barrier, inc=1, device_id={"tm": peer(d)}, device_id_type=MESH)
    pl.semaphore_signal(barrier, inc=1, device_id={"vox": mate}, device_id_type=MESH)

    @pl.when(z > 0)
    def _():
        pl.semaphore_signal(barrier, inc=1, device_id={"vox": v - 2}, device_id_type=MESH)

    @pl.when(z < n_z - 1)
    def _():
        pl.semaphore_signal(barrier, inc=1, device_id={"vox": v + 2}, device_id_type=MESH)

    neighbours = jnp.where(z > 0, 1, 0) + jnp.where(z < n_z - 1, 1, 0)
    pl.semaphore_wait(barrier, n_t + neighbours)

    for ch in range(CHUNKS):

        @pl.when(z > 0)
        def _():
            line_copy(z, ch, -1, True).start()

        @pl.when(z < n_z - 1)
        def _():
            line_copy(z, ch, 1, True).start()

    pick = one_hot(live_ref, cap)
    lam = [lambda_ref[index_ref[i]] for i in range(blocks)]
    slot_lam = [sum(pick[j][i] * lam[i] for i in range(blocks)) for j in range(cap)]
    slot_live = [sum(pick[j][i] for i in range(blocks)) for j in range(cap)]

    y_cols = [y_ref[:, i * BLK : (i + 1) * BLK].astype(jnp.float32) for i in range(blocks)]
    y_t = jnp.concatenate(
        [sum(pick[j][i] * y_cols[i] for i in range(blocks)).T for j in range(cap)], axis=0
    ).astype(jnp.bfloat16)

    def make_parts(r, send):
        for d in range(1, n_t + 1):
            to = peer(d % n_t)
            u_copy(r, to).wait()

            def tile(i, _, to=to, d=d):
                off = pl.multiple_of(i * TILE, TILE)
                cols = pl.ds(pl.multiple_of(r * span + to * share + i * TILE, TILE), TILE)
                value = jnp.dot(y_t, u_buf[:, cols], preferred_element_type=jnp.float32)
                if d < n_t:
                    part_out[r, to, :, pl.ds(off, TILE)] = value.astype(jnp.bfloat16)
                else:
                    part_own[r, :, pl.ds(off, TILE)] = value
                return 0

            lax.fori_loop(0, share // TILE, tile, 0)
            if send and d < n_t:
                part_copy(r, to, t).start()

    def send_parts(r):
        for d in range(1, n_t):
            part_copy(r, peer(d), t).start()

    def filter_parts(r):
        for d in range(1, n_t):
            part_copy(r, peer(d), peer(d)).wait_recv()
        for i in range(share // TILE):
            cols = slice(i * TILE, (i + 1) * TILE)
            place = pl.multiple_of(r * span + t * share + i * TILE, TILE)
            sing = sing_ref[:, pl.ds(place, TILE)]
            for j in range(cap):
                rows = slice(j * BLK, (j + 1) * BLK)
                total = part_own[r, rows, cols]
                for d in range(1, n_t):
                    total = total + part_in[r, peer(d), rows, cols].astype(jnp.float32)
                factor = sing / (sing * sing + slot_lam[j]) * slot_live[j]
                filt[r, t, rows, cols] = (total * factor).astype(jnp.bfloat16)
        for to in near:
            filt_copy(r, to, t).start()

    def forward_filt(r):
        for to in near:
            filt_copy(r, to, to).wait_recv()
        if relayed:
            for k in range(2):
                relay_copy(r, k, near[k], near[1 - k]).start()

    def await_filt(r):
        if relayed:
            for k in range(2):
                relay_copy(r, k, near[k], n_t - 1 - t).wait_recv()

    make_parts(rounds[0], True)

    for ch in range(CHUNKS):
        pair_copy(z, ch, True).start()
        own_copy(ch).start()
    x_copy = pltpu.make_async_copy(x_ref, x_buf, x_sem)
    x_copy.start()

    make_parts(rounds[1], False)

    def relay(s, ch):
        low, high = z - 1 - s, z + 1 + s

        @pl.when((low >= 0) & holds(z, low))
        def _():
            line_copy(low, ch, -1).wait_recv()

            @pl.when((z < n_z - 1) & holds(z + 1, low))
            def _():
                line_copy(low, ch, 1).start()

            pair_copy(low, ch).start()

        @pl.when((high < n_z) & holds(z, high))
        def _():
            line_copy(high, ch, 1).wait_recv()

            @pl.when((z > 0) & holds(z - 1, high))
            def _():
                line_copy(high, ch, -1).start()

            pair_copy(high, ch).start()

    def product(values, slot, rows, factors):
        return lax.dot_general(
            values[slot, rows, :], factors, (((1,), (1,)), ((), ())),
            preferred_element_type=jnp.float32,
        )

    def place_of(slot):
        start = lax.rem(slot * depth, span)
        owner = start // share
        return owner, pl.ds(pl.multiple_of(start - owner * share, depth), depth)

    base = jnp.where(z == 1, half, 0) * 2

    def settle(ch):
        own_copy(ch).wait()

        def step(src, _):
            @pl.when(holds(z, src))
            def _():
                pair_arrival(src, ch).wait_recv()

            return 0

        lax.fori_loop(0, n_z, step, 0)

    def add_round(r, ch):
        rows = pl.ds(ch * rc, rc)

        def step(i, value):
            slot = r * half * 2 + i
            owner, inner = place_of(slot)
            return value + product(v_all, slot, rows, filt[r, owner, :, inner])

        value = jnp.zeros((rc, acc.shape[1]), jnp.float32)
        for i in range(2 * half):
            value = step(i, value)
        return value

    def far_half(ch):
        rows = pl.ds(ch * rc, rc)

        @pl.when(jnp.logical_not(is_end))
        def _():
            acc[rows, :] = add_round(rounds[0], ch)

        @pl.when(is_end)
        def _():
            acc[rows, :] = jnp.zeros((rc, acc.shape[1]), jnp.float32)

    def help_end(j, chunks):
        cols = slice(j * BLK, (j + 1) * BLK)

        @pl.when(is_helper)
        def _():
            if chunks[0] == 0:
                far_filt_copy(j, -inward).wait_recv()
            for ch in chunks:
                rows = pl.ds(ch * rc, rc)
                value = jnp.zeros((rc, BLK), jnp.float32)
                for i in range(2 * half):
                    owner, inner = place_of(base + i)
                    value += product(v_all, base + i, rows, far_filt[owner, cols, inner])
                far_out[j, rows, :] = value.astype(jnp.bfloat16)
                far_copy(j, ch, -inward).start()

    early, last = CHUNKS // 2, CHUNKS - 1
    for ch in range(early):
        relay(0, ch)
    filter_parts(rounds[0])
    for ch in range(early, last):
        relay(0, ch)
    forward_filt(rounds[0])
    send_parts(rounds[1])
    relay(0, last)
    await_filt(rounds[0])

    @pl.when(is_end)
    def _():
        for j in range(cap):
            far_filt_copy(j, inward).start()

    def relay_step(s, _):
        for ch in range(CHUNKS):
            relay(s, ch)
        return 0

    lax.fori_loop(1, n_z - 3, relay_step, 0)
    for ch in range(early):
        relay(n_z - 3, ch)
    filter_parts(rounds[1])
    for ch in range(early, last):
        relay(n_z - 3, ch)
    for ch in range(early):
        settle(ch)
        far_half(ch)
    forward_filt(rounds[1])
    for ch in range(early, last):
        settle(ch)
        far_half(ch)
    help_end(0, list(range(last)))
    relay(n_z - 3, last)
    settle(last)
    help_end(0, [last])
    far_half(last)
    help_end(1, list(range(CHUNKS)))
    for j in range(2, cap):
        help_end(j, list(range(CHUNKS)))
    await_filt(rounds[1])
    x_copy.wait()

    def finish(ch):
        rows = slice(ch * rc, (ch + 1) * rc)
        acc[rows, :] += add_round(rounds[1], ch)

        @pl.when(is_end)
        def _():
            for j in range(cap):
                cols = slice(j * BLK, (j + 1) * BLK)
                far_copy(j, ch, inward).wait_recv()
                acc[rows, cols] += far_in[j, rows, :].astype(jnp.float32)

        weights = acc[rows, :].astype(jnp.bfloat16)
        w_ref[rows, :] = weights
        value = jnp.dot(x_buf[:, rows], weights, preferred_element_type=jnp.float32)
        if ch == 0:
            pred_acc[...] = value
        else:
            pred_acc[...] += value

    for ch in range(CHUNKS):
        finish(ch)

    for d in range(1, n_t):
        to = peer(d)
        mine = pl.ds(pl.multiple_of(to * test_rows, test_rows), test_rows)
        pred_out[to] = pred_acc[mine, :].astype(jnp.bfloat16)
        pred_copy(to, t).start()
    for d in range(1, n_t):
        pred_copy(peer(d), peer(d)).wait_recv()
    total = pred_acc[pl.ds(pl.multiple_of(t * test_rows, test_rows), test_rows), :]
    for d in range(1, n_t):
        total = total + pred_in[peer(d)].astype(jnp.float32)
    pred_ref[...] = total.astype(jnp.bfloat16)

    for d in range(1, n_t):
        for r in rounds:
            part_copy(r, peer(d), t).wait_send()
        pred_copy(peer(d), t).wait_send()
    for r in rounds:
        for to in near:
            filt_copy(r, to, t).wait_send()
        if relayed:
            for k in range(2):
                relay_copy(r, k, near[k], near[1 - k]).wait_send()

    @pl.when(is_end)
    def _():
        for j in range(cap):
            far_filt_copy(j, inward).wait_send()

    @pl.when(is_helper)
    def _():
        for j in range(cap):
            for ch in range(CHUNKS):
                far_copy(j, ch, -inward).wait_send()

    def drain(src, _):
        for ch in range(CHUNKS):

            @pl.when(holds(z, src))
            def _():
                pair_copy(src, ch).wait_send()

            @pl.when((src <= z) & (z < n_z - 1) & holds(z, src) & holds(z + 1, src))
            def _():
                line_copy(src, ch, 1).wait_send()

            @pl.when((src >= z) & (z > 0) & holds(z, src) & holds(z - 1, src))
            def _():
                line_copy(src, ch, -1).wait_send()

        return 0

    lax.fori_loop(0, n_z, drain, 0)


def body(n_t, n_v, u_train, y_train, sing, lambdas, lam_index, live, v_basis, x_test):
    time_rows, features = u_train.shape
    columns = y_train.shape[1]
    blocks = lam_index.shape[0]
    cap = blocks - blocks // 3
    used = cap * BLK
    rows_v, depth = v_basis.shape
    tests = x_test.shape[0]
    share = features // n_t // 2
    n_z = n_v // 2
    low, full = jnp.bfloat16, jnp.float32
    smem = pl.BlockSpec(memory_space=pltpu.SMEM)
    vmem = pl.BlockSpec(memory_space=pltpu.VMEM)
    anywhere = pl.BlockSpec(memory_space=pl.ANY)
    dma = pltpu.SemaphoreType.DMA
    weights, predicted = pl.pallas_call(
        functools.partial(kernel, n_t, n_v, cap),
        out_shape=(
            jax.ShapeDtypeStruct((rows_v, used), low),
            jax.ShapeDtypeStruct((tests // n_t, used), low),
        ),
        in_specs=[smem, smem, smem, vmem, vmem, anywhere, anywhere, anywhere],
        out_specs=(vmem, vmem),
        scratch_shapes=[
            pltpu.VMEM((time_rows, features), low),
            pltpu.VMEM((tests, rows_v), low),
            pltpu.VMEM((n_v, rows_v, depth), low),
            pltpu.VMEM((2, n_t, used, share), low),
            pltpu.VMEM((2, n_t, used, share), low),
            pltpu.VMEM((2, used, share), full),
            pltpu.VMEM((2, n_t, used, share), low),
            pltpu.VMEM((rows_v, used), full),
            pltpu.VMEM((tests, used), full),
            pltpu.VMEM((n_t, tests // n_t, used), low),
            pltpu.VMEM((n_t, tests // n_t, used), low),
            dma((2, n_t)),
            dma,
            dma((CHUNKS,)),
            dma((n_z, CHUNKS)),
            dma((n_z, CHUNKS)),
            dma((n_z, CHUNKS)),
            dma((n_z, CHUNKS)),
            dma((n_z, CHUNKS)),
            dma((2, n_t)),
            dma((2, n_t)),
            dma((2, n_t)),
            dma((2, n_t)),
            dma((n_t,)),
            dma((n_t,)),
            pltpu.VMEM((n_t, used, share), low),
            pltpu.VMEM((cap, rows_v, BLK), low),
            pltpu.VMEM((cap, rows_v, BLK), low),
            dma((cap,)),
            dma((cap,)),
            dma((cap, CHUNKS)),
            dma((cap, CHUNKS)),
            dma((2, 2)),
            dma((2, 2)),
        ],
        compiler_params=pltpu.CompilerParams(collective_id=0, has_side_effects=True),
    )(live, lam_index, lambdas, sing.reshape(1, features), y_train, u_train, v_basis, x_test)
    return pl.pallas_call(
        functools.partial(expand, cap),
        out_shape=(
            jax.ShapeDtypeStruct((rows_v, columns), low),
            jax.ShapeDtypeStruct((tests // n_t, columns), low),
        ),
        in_specs=[smem, vmem, vmem],
        out_specs=(vmem, vmem),
    )(live, weights, predicted)


FAR_PARTS = (4, 4, 4, 8, 16, 32, 32)
SIDE_PARTS = (2, 4, 4)


def row_pieces(rows, parts):
    pieces, start = [], 0
    for part in parts:
        pieces.append((start, rows // part))
        start += rows // part
    return pieces


def widen(pick, values):
    wide = [values[:, j * BLK : (j + 1) * BLK] for j in range(len(pick))]
    return [sum(pick[j][i] * wide[j] for j in range(len(pick))) for i in range(len(pick[0]))]


def plane_kernel(
    cap,
    live_hbm,
    index_hbm,
    lambda_hbm,
    sing_hbm,
    y_hbm,
    u_hbm,
    v_hbm,
    x_hbm,
    w_ref,
    pred_ref,
    live_ref,
    index_ref,
    lambda_ref,
    sing_buf,
    y_buf,
    u_buf,
    x_buf,
    v_all,
    part_out,
    part_in,
    own,
    comb_out,
    comb_in,
    filt,
    far_filt,
    acc,
    pred_acc,
    far_out,
    far_in,
    pred_out,
    pred_in,
    lent,
    w_buf,
    in_sem,
    u_sem,
    own_sem,
    line_send,
    side_recv,
    across_recv,
    rows_recv,
    pair_send,
    pair_recv,
    pair_far_recv,
    part_send,
    part_recv,
    comb_send,
    comb_recv,
    ag_send,
    ag_recv,
    hand_send,
    hand_recv,
    plane_send,
    plane_recv,
    help_send,
    help_recv,
    q_send,
    q_recv,
    lend_recv,
    ready,
    reached,
):
    t = lax.axis_index("tm")
    v = lax.axis_index("vox")
    z, core = v // 2, v % 2
    mate = z * 2 + 1 - core
    rows_v, depth = v_hbm.shape
    blocks = live_ref.shape[0]
    share = depth
    span = 4 * share
    far_pieces = row_pieces(rows_v, FAR_PARTS)
    side_pieces = row_pieces(rows_v, SIDE_PARTS)
    whole = (0, rows_v)
    count = len(far_pieces)
    low_side = z < 2
    inward = jnp.where(low_side, 1, -1)
    is_end = (z == 0) | (z == 3)
    is_mid = jnp.logical_not(is_end)
    partner_z = jnp.where(is_end, z + inward, z - inward)
    partner = partner_z * 2 + core
    near_round = z // 2
    rounds = (1 - z % 2, z % 2)
    near = [t + 1 - 2 * lax.rem(t, 2), lax.rem(t + 2, 4)]
    diag = 3 - t
    scope = jax.named_scope

    def remote(src, dst, send, recv, **place):
        return pltpu.make_async_remote_copy(
            src_ref=src, dst_ref=dst, send_sem=send, recv_sem=recv, device_id=place, device_id_type=MESH
        )

    def slot_of(zz, cc):
        return zz * 2 + cc

    def block_of(slot, piece):
        cols = pl.ds(pl.multiple_of((slot % 4) * depth, depth), depth)
        return v_all.at[slot // 4, pl.ds(*piece), cols]

    far_mid, far_end = 3 - z, 3 - partner_z
    across_mate = (z + inward) * 2 + 1 - core

    def side_copy(piece, recv):
        return remote(v_hbm.at[pl.ds(*piece)], block_of(v, piece), line_send.at[0], recv, vox=partner)

    def side_wait(piece, recv):
        at = block_of(partner, piece)
        remote(at, at, line_send.at[0], recv, vox=partner).wait_recv()

    def across_copy():
        return remote(v_hbm, block_of(v, whole), line_send.at[1], across_recv, vox=v + 2 * inward)

    def across_wait():
        at = block_of(slot_of(far_mid, core), whole)
        remote(at, at, line_send.at[1], across_recv, vox=v + 2 * inward).wait_recv()

    def line_relay(i):
        at = block_of(partner, far_pieces[i])
        return remote(at, at, line_send.at[2], rows_recv.at[i], vox=v + 2 * inward)

    direct = (count - 2, count - 1)
    direct_rows = rows_v - far_pieces[direct[0]][0]

    def line_relay_other(i):
        at = block_of(partner, far_pieces[i])
        return remote(at, at, line_send.at[3], pair_far_recv.at[i], vox=across_mate)

    def line_relay_wait(i):
        at = block_of(slot_of(far_end, core), far_pieces[i])
        remote(at, at, line_send.at[2], rows_recv.at[i], vox=v + 2 * inward).wait_recv()

    def pair_copy(k):
        src = v_hbm if k == 0 else block_of(pair_slot(k, core), whole)
        return remote(src, block_of(pair_slot(k, core), whole), pair_send.at[k], pair_recv.at[k], vox=mate)

    def pair_slot(k, cc):
        return slot_of((z, partner_z, far_mid)[k], cc)

    def pair_wait(k):
        at = block_of(pair_slot(k, 1 - core), whole)
        remote(at, at, pair_send.at[k], pair_recv.at[k], vox=mate).wait_recv()

    def pair_far_copy(i):
        at = block_of(slot_of(far_end, core), far_pieces[i])
        return remote(at, at, pair_send.at[3], pair_far_recv.at[i], vox=mate)

    def pair_far_wait(i):
        at = block_of(slot_of(far_end, 1 - core), far_pieces[i])
        remote(at, at, pair_send.at[3], pair_far_recv.at[i], vox=mate).wait_recv()

    def own_copy():
        return pltpu.make_async_copy(v_hbm, block_of(v, whole), own_sem)

    def rows_of(i):
        return pl.ds(*far_pieces[i])

    def u_copy(i):
        first, width = (owners[i] * share, share) if i < 4 else (0, span)
        cols = pl.ds(pl.multiple_of(rounds[i // 4] * span + first, share), width)
        return pltpu.make_async_copy(u_hbm.at[:, cols], u_buf.at[:, cols], u_sem.at[i])

    def half(i):
        return pl.ds(i * BLK, BLK)

    def rank(owner):
        return pl.ds(pl.multiple_of(owner * share, share), share)

    def part_copy(o, j, s):
        return remote(part_out.at[o, j, s], part_in.at[o, j, s], part_send, part_recv.at[o, s], tm=near[j])

    def comb_copy(o, j):
        return remote(comb_out.at[o, j], comb_in.at[o, j], comb_send, comb_recv.at[o], tm=near[1 - j])

    def ag_copy(o, i, owner):
        at = filt.at[o, rank(owner)]
        return remote(at, at, ag_send, ag_recv.at[o], tm=near[i])

    def hand_copy(o, i, owner):
        at = filt.at[o, rank(owner), half(i)]
        return remote(at, at, hand_send, hand_recv.at[o], tm=near[i])

    def half_copy(i, owner):
        at = filt.at[0, rank(owner), half(i)]
        return remote(at, at, plane_send, plane_recv, tm=near[i])

    def far_filt_copy(k):
        if k == 0:
            src, dst = filt.at[0, rank(t)], far_filt.at[rank(t)]
        else:
            src, dst = filt.at[0, rank(near[k - 1]), half(k - 1)], far_filt.at[rank(near[k - 1]), half(k - 1)]
        return remote(src, dst, help_send, help_recv.at[k], vox=partner)

    def far_filt_wait(k):
        at = far_filt.at[rank(t)] if k == 0 else far_filt.at[rank(near[k - 1]), half(k - 1)]
        remote(at, at, help_send, help_recv.at[k], vox=partner).wait_recv()

    def cross_copy(s, i, owner):
        at = far_filt.at[rank(owner), half(1 - i)]
        return remote(at, at, plane_send, plane_recv, tm=near[i])

    def far_copy(ch):
        return remote(
            far_out.at[rows_of(ch)], far_in.at[rows_of(ch)], help_send, rows_recv.at[ch], vox=partner
        )

    test_rows = pred_out.shape[1]
    strip = test_rows // 2

    def lend_copy(j, k):
        at = (pl.ds(k * strip, strip), half(j))
        return remote(pred_out.at[(2, *at)], lent.at[at], q_send, lend_recv.at[k], tm=near[j])

    def pred_copy(i, j, rows):
        at = (i, rows, half(j))
        return remote(pred_out.at[at], pred_in.at[at], q_send, q_recv, tm=near[i])

    barrier = pltpu.get_barrier_semaphore()

    bits = (lax.rem(t, 2), t // 2, core)
    pairs = ({"tm": near[0]}, {"tm": near[1]}, {"vox": mate})

    def signal(sem, place):
        pl.semaphore_signal(sem, inc=1, device_id=place, device_id_type=MESH)

    for bit, place in zip(bits, pairs):

        @pl.when(bit == 0)
        def _():
            signal(barrier, place)

    @pl.when(z < 3)
    def _():
        signal(barrier, {"vox": v + 2})

    @pl.when(z == 2)
    def _():
        signal(barrier, {"vox": v - 2})

    y_copy = pltpu.make_async_copy(y_hbm, y_buf, in_sem.at[0])
    sing_copy = pltpu.make_async_copy(sing_hbm, sing_buf, in_sem.at[1])
    x_copy = pltpu.make_async_copy(x_hbm, x_buf, in_sem.at[2])
    owners = (diag, near[0], near[1], t)
    y_copy.start()
    for i in range(4):
        u_copy(i).start()
    sing_copy.start()
    scalars = [
        pltpu.make_async_copy(live_hbm, live_ref, in_sem.at[3]),
        pltpu.make_async_copy(index_hbm, index_ref, in_sem.at[4]),
        pltpu.make_async_copy(lambda_hbm, lambda_ref, in_sem.at[5]),
    ]
    for copy in scalars:
        copy.start()

    with scope("bar"):
        callers = sum(bits) + jnp.where(z == 0, 0, jnp.where(z == 1, 2, 1))

        @pl.when(callers > 0)
        def _():
            pl.semaphore_wait(barrier, callers)


    @pl.when(is_mid)
    def _():
        across_copy().start()

    for bit, place in zip(bits, pairs):

        @pl.when(bit == 1)
        def _():
            signal(ready, place)

    @pl.when((z == 1) | (z == 3))
    def _():
        signal(ready, {"vox": v - 2})

    u_copy(4).start()

    for copy in scalars:
        copy.wait()
    pick = one_hot(live_ref, cap)
    lam = [lambda_ref[index_ref[i]] for i in range(blocks)]
    slot_lam = [sum(pick[j][i] * lam[i] for i in range(blocks)) for j in range(cap)]
    slot_live = [sum(pick[j][i] for i in range(blocks)) for j in range(cap)]

    with scope("ycp"):
        y_copy.wait()
    y_cols = [y_buf[:, i * BLK : (i + 1) * BLK].astype(jnp.float32) for i in range(blocks)]
    y_t = jnp.concatenate(
        [sum(pick[j][i] * y_cols[i] for i in range(blocks)).T for j in range(cap)], axis=0
    ).astype(jnp.bfloat16)

    def greet():
        with scope("ready"):
            answers = 3 - sum(bits) + jnp.where((z == 0) | (z == 2), 1, 0)

            @pl.when(answers > 0)
            def _():
                pl.semaphore_wait(ready, answers)


        @pl.when(is_mid)
        def _():
            side_copy(whole, side_recv.at[0]).start()

        @pl.when(is_end)
        def _():
            side_copy(side_pieces[0], side_recv.at[0]).start()

    def make_parts(o):
        if o == 1:
            u_copy(4).wait()
        for i in range(4):
            if o == 0:
                u_copy(i).wait()
            for tile in range(share // TILE):
                into = slice(tile * TILE, (tile + 1) * TILE)
                start = rounds[o] * span + owners[i] * share + tile * TILE
                cols = pl.ds(pl.multiple_of(start, TILE), TILE)
                value = jnp.dot(y_t, u_buf[:, cols], preferred_element_type=jnp.float32)
                first, second = value[:BLK], value[BLK:]
                if i == 0:
                    part_out[o, 0, 1, :, into] = first.astype(jnp.bfloat16)
                    part_out[o, 1, 1, :, into] = second.astype(jnp.bfloat16)
                elif i == 1:
                    part_out[o, 0, 0, :, into] = first.astype(jnp.bfloat16)
                    own[o, 1, 1, :, into] = second
                elif i == 2:
                    own[o, 0, 1, :, into] = first
                    part_out[o, 1, 0, :, into] = second.astype(jnp.bfloat16)
                else:
                    own[o, 0, 0, :, into] = first
                    own[o, 1, 0, :, into] = second
            if o == 0 and i == 0:
                greet()
                for j in range(2):
                    part_copy(o, j, 1).start()
            if o == 0 and i in (1, 2):
                part_copy(o, i - 1, 0).start()

    def received(ref, sem):
        remote(ref, ref, q_send, sem, vox=mate).wait_recv()

    def combine(o):
        received(part_in.at[o, :, 1], part_recv.at[o, 1])
        for j in range(2):
            comb_out[o, j] = (own[o, j, 1] + part_in[o, j, 1].astype(jnp.float32)).astype(jnp.bfloat16)
            comb_copy(o, j).start()

    def filter_parts(o):
        place = pl.multiple_of(rounds[o] * span + t * share, share)
        sing = sing_buf[:, pl.ds(place, share)]
        received(part_in.at[o, :, 0], part_recv.at[o, 0])
        received(comb_in.at[o], comb_recv.at[o])
        for j in range(cap):
            total = own[o, j, 0] + part_in[o, j, 0].astype(jnp.float32) + comb_in[o, j].astype(jnp.float32)
            factor = sing / (sing * sing + slot_lam[j]) * slot_live[j]
            filt[o, rank(t), half(j)] = (total * factor).T.astype(jnp.bfloat16)

    def send_filt(o):
        for i in range(2):
            ag_copy(o, i, t).start()

    def forward_filt(o):
        received(filt.at[o, pl.ds(0, 2 * share)], ag_recv.at[o])
        for i in range(2):
            hand_copy(o, i, near[1 - i]).start()

    def await_filt(o):
        received(filt.at[o, pl.ds(0, share)], hand_recv.at[o])

    with scope("mp0"):
        make_parts(0)
    with scope("mp1"):
        make_parts(1)
    pair_copy(0).start()
    own_copy().start()
    x_copy.start()
    sing_copy.wait()

    def near_product(o, rows):
        return jnp.dot(v_all[near_round, rows, :], filt[o], preferred_element_type=jnp.float32)

    def far_product(rows, factors):
        return jnp.dot(v_all[1 - near_round, rows, :], factors, preferred_element_type=jnp.float32)

    def near_rows(o):
        own_copy().wait()
        pair_wait(0)
        pair_wait(1)
        for i in range(4):
            rows = pl.ds(i * (rows_v // 4), rows_v // 4)
            acc[rows, :] = near_product(o, rows)

    def predict(piece):
        rows = pl.ds(*piece)
        part = jnp.dot(x_buf[:, rows], w_buf[rows, :], preferred_element_type=jnp.float32)
        if piece[0] == 0:
            pred_acc[...] = part
        else:
            pred_acc[...] += part

    def predict_last(piece):
        rows = pl.ds(*piece)
        for k in range(2):
            here = pl.ds(k * strip, strip)
            mine = pl.ds(pl.multiple_of(diag * test_rows + k * strip, strip), strip)
            value = pred_acc[mine, :] + jnp.dot(x_buf[mine, rows], w_buf[rows, :], preferred_element_type=jnp.float32)
            pred_out[2, here, :] = value.astype(jnp.bfloat16)
            for j in range(2):
                lend_copy(j, k).start()
        for i, to in ((3, t), (0, near[0]), (1, near[1])):
            mine = pl.ds(pl.multiple_of(to * test_rows, test_rows), test_rows)
            value = pred_acc[mine, :] + jnp.dot(x_buf[mine, rows], w_buf[rows, :], preferred_element_type=jnp.float32)
            pred_acc[mine, :] = value
            if i < 2:
                pred_out[i, :, i * BLK : (i + 1) * BLK] = value[:, i * BLK : (i + 1) * BLK].astype(jnp.bfloat16)

                @pl.when(core == 0)
                def _():
                    pred_copy(i, i, pl.ds(0, test_rows)).start()

    def direct_lead():
        @pl.when(core == 1)
        def _():
            for i in range(2):
                pred_copy(i, i, pl.ds(0, test_rows)).start()

    def hand_on():
        for k in range(2):
            if k == 1:
                direct_lead()
            received(lent.at[pl.ds(k * strip, strip)], lend_recv.at[k])
            for j in range(2):
                to = near[1 - j]
                mine = pl.ds(pl.multiple_of(to * test_rows + k * strip, strip), strip)
                here = pl.ds(k * strip, strip)
                value = pred_acc[mine, half(j)] + lent[here, half(j)].astype(jnp.float32)
                pred_out[1 - j, here, half(j)] = value.astype(jnp.bfloat16)
                pred_copy(1 - j, j, here).start()

    def put_rows(piece):
        rows = pl.ds(*piece)
        for i, block in enumerate(widen(pick, w_buf[rows, :].astype(jnp.float32))):
            w_ref[rows, i * BLK : (i + 1) * BLK] = block.astype(jnp.bfloat16)

    head = (0, far_pieces[3][0])
    rest = (head[1], rows_v - head[1])
    last_rows = (far_pieces[4][0], rows_v - far_pieces[4][0])

    @pl.when(is_mid)
    def _():
        def arrive(i, lead=False):
            line_relay_wait(i)
            if lead or i not in direct:
                pair_far_copy(i).start()

        def help_end(*which):
            for i in which:
                pair_far_wait(i)
            first = far_pieces[which[0]][0]
            rows = pl.ds(first, sum(far_pieces[i][1] for i in which))
            far_out[rows, :] = far_product(rows, far_filt[...]).astype(jnp.bfloat16)
            for i in which:
                far_copy(i).start()

        def own_rows(piece):
            rows = pl.ds(*piece)
            w_buf[rows, :] = (acc[rows, :] + far_product(rows, filt[1])).astype(jnp.bfloat16)

        with scope("m_comb0"):
            combine(0)
            for s in (1, 0):
                for j in range(2):
                    part_copy(1, j, s).start()
        with scope("m_filt0"):
            filter_parts(0)
            send_filt(0)
        with scope("m_side0"):
            side_wait(side_pieces[0], side_recv.at[0])
            for i in range(2):
                line_relay(i).start()
        with scope("m_comb1"):
            combine(1)
        with scope("m_ff0"):
            far_filt_wait(0)
            for i in range(2):
                cross_copy(0, i, t).start()
        with scope("m_fw0"):
            forward_filt(0)
        with scope("m_across"):
            across_wait()
            pair_copy(2).start()
        with scope("m_ff1"):
            for k in (1, 2):
                far_filt_wait(k)
            for i in range(2):
                cross_copy(1, i, near[1 - i]).start()
        with scope("m_filt1"):
            filter_parts(1)
            send_filt(1)
        def tail_lead():
            with scope("m_far0"):
                arrive(0, True)
            side_last(1)
            with scope("m_cross"):
                await_cross()
            with scope("m_help0"):
                help_end(0)
            side_last(2)
            with scope("m_far1"):
                arrive(1, True)
            with scope("m_fw1"):
                forward_filt(1)
            with scope("m_help1"):
                help_end(1)
            with scope("m_aw0"):
                await_filt(0)
            with scope("m_near"):
                near_rows(0)
            for i in (2, 3):
                with scope(f"m_far{i}"):
                    arrive(i, True)
            with scope("m_aw1"):
                await_filt(1)
            with scope("m_own0"):
                for i in range(2):
                    own_rows(far_pieces[i])
            with scope("m_help2"):
                help_end(2)
            with scope("m_far4"):
                arrive(4, True)
            with scope("m_own1"):
                own_rows(far_pieces[2])
            for i in (5, 6):
                with scope(f"m_far{i}"):
                    arrive(i, True)
            with scope("m_help3"):
                help_end(3)
            with scope("m_help4"):
                help_end(5, 6)
                help_end(4)
            x_copy.wait()
            with scope("m_pred0"):
                predict(head)

        def tail_late():
            with scope("m_far0"):
                arrive(0)
            side_last(1)
            with scope("m_cross"):
                await_cross()
            with scope("m_help0"):
                help_end(0)
            side_last(2)
            with scope("m_far1"):
                arrive(1)
            with scope("m_help1"):
                help_end(1)
            with scope("m_fw1"):
                forward_filt(1)
            with scope("m_aw0"):
                await_filt(0)
            with scope("m_near"):
                near_rows(0)
            with scope("m_far2"):
                arrive(2)
            with scope("m_help2"):
                help_end(2)
            with scope("m_aw1"):
                await_filt(1)
            x_copy.wait()
            with scope("m_own0"):
                own_rows(far_pieces[0])
            with scope("m_far3"):
                arrive(3)
            with scope("m_help3"):
                help_end(3)
            with scope("m_own1"):
                for i in (1, 2):
                    own_rows(far_pieces[i])
            with scope("m_far4"):
                arrive(4)
            with scope("m_help4"):
                help_end(4)
            with scope("m_far6"):
                arrive(5)
                arrive(6)
            with scope("m_help5"):
                help_end(5, 6)
            with scope("m_pred0"):
                predict(head)

        def side_last(k):
            with scope(f"m_side{k}"):
                side_wait(side_pieces[k], side_recv.at[k])
                if k == 1:
                    line_relay(2).start()
                    return
                for i in range(3, count):
                    line_relay(i).start()
                pair_copy(1).start()

            @pl.when(core == 0)
            def _():
                pl.semaphore_wait(reached, 1)
                for i in direct:
                    line_relay_other(i).start()

        def await_cross():
            received(far_filt.at[pl.ds(0, 2 * share)], plane_recv)
            pair_wait(2)

            @pl.when(core == 1)
            def _():
                signal(reached, {"vox": across_mate})


        pl.when(core == 1)(tail_lead)
        pl.when(core == 0)(tail_late)
        with scope("m_last"):
            own_rows(rest)
            predict_last(rest)
        put_rows(whole)

    @pl.when(is_end)
    def _():
        with scope("e_comb0"):
            combine(0)
            for j in range(2):
                part_copy(1, j, 1).start()
        with scope("e_filt0"):
            filter_parts(0)
            far_filt_copy(0).start()
            for i in range(2):
                half_copy(i, t).start()
            for j in range(2):
                part_copy(1, j, 0).start()
        with scope("e_half"):
            received(filt.at[0, pl.ds(0, share)], plane_recv)
            for i in range(2):
                far_filt_copy(1 + i).start()
            for i in range(1, len(side_pieces)):
                side_copy(side_pieces[i], side_recv.at[i]).start()
        with scope("e_comb1"):
            combine(1)
        with scope("e_filt1"):
            filter_parts(1)
            send_filt(1)
        with scope("e_side"):
            side_wait(whole, side_recv.at[0])
            pair_copy(1).start()
        with scope("e_fw1"):
            forward_filt(1)
        x_copy.wait()
        with scope("e_aw1"):
            await_filt(1)
        with scope("e_near"):
            near_rows(1)

        def add_far(piece):
            rows = pl.ds(*piece)
            w_buf[rows, :] = (acc[rows, :] + far_in[rows, :].astype(jnp.float32)).astype(jnp.bfloat16)

        for i in range(3):
            with scope(f"e_far{i}"):
                far_copy(i).wait_recv()
            add_far(far_pieces[i])
            predict(far_pieces[i])
            put_rows(far_pieces[i])
        with scope("e_far3"):
            far_copy(3).wait_recv()
        add_far(far_pieces[3])
        predict(far_pieces[3])
        with scope("e_far4"):
            for i in range(4, count):
                far_copy(i).wait_recv()
        with scope("e_last"):
            add_far(last_rows)
            predict_last(last_rows)
        put_rows(rest)

    with scope("hand"):
        hand_on()
    with scope("pwait"):
        remote(pred_in, pred_in, q_send, q_recv, vox=mate).wait_recv()
    total = pred_acc[pl.ds(pl.multiple_of(t * test_rows, test_rows), test_rows), :]
    for i in range(2):
        total = total + pred_in[i].astype(jnp.float32)
    total = total.astype(jnp.bfloat16).astype(jnp.float32)
    for i, block in enumerate(widen(pick, total)):
        pred_ref[:, i * BLK : (i + 1) * BLK] = block.astype(jnp.bfloat16)

    def sent(ref, sem):
        remote(ref, ref, sem, q_recv, vox=mate).wait_send()

    with scope("drain"):
        sent(part_out, part_send)
        sent(comb_out, comb_send)
        sent(pred_out, q_send)
        sent(v_all.at[0, :, pl.ds(0, depth)], line_send.at[0])
        for k in range(2):
            sent(v_all.at[0, :, pl.ds(0, depth)], pair_send.at[k])

        @pl.when(is_mid)
        def _():
            for k in range(1, 3):
                sent(v_all.at[0, :, pl.ds(0, depth)], line_send.at[k])
            sent(v_all.at[0, :, pl.ds(0, depth)], pair_send.at[2])

            @pl.when(core == 0)
            def _():
                sent(v_all.at[0, pl.ds(0, direct_rows), pl.ds(0, depth)], line_send.at[3])
                sent(v_all.at[0, pl.ds(0, rows_v - direct_rows), pl.ds(0, depth)], pair_send.at[3])

            @pl.when(core == 1)
            def _():
                sent(v_all.at[0, :, pl.ds(0, depth)], pair_send.at[3])

            sent(filt.at[0], ag_send)
            sent(filt.at[0, pl.ds(0, 2 * share)], hand_send)
            sent(far_filt.at[pl.ds(0, 2 * share)], plane_send)
            sent(far_out, help_send)

        @pl.when(is_end)
        def _():
            sent(filt.at[0, pl.ds(0, 2 * share)], ag_send)
            sent(filt.at[0, pl.ds(0, share)], hand_send)
            sent(filt.at[0, pl.ds(0, share)], plane_send)
            sent(filt.at[0, pl.ds(0, 2 * share)], help_send)


def put_out(w_in, pred_in, w_ref, pred_ref, sem):
    copies = [
        pltpu.make_async_copy(w_in, w_ref, sem.at[0]),
        pltpu.make_async_copy(pred_in, pred_ref, sem.at[1]),
    ]
    for copy in copies:
        copy.start()
    for copy in copies:
        copy.wait()


def plane_body(u_train, y_train, sing, lambdas, lam_index, live, v_basis, x_test):
    time_rows, features = u_train.shape
    columns = y_train.shape[1]
    blocks = lam_index.shape[0]
    cap = blocks - blocks // 3
    used = cap * BLK
    rows_v, depth = v_basis.shape
    tests = x_test.shape[0]
    share = depth
    count = len(FAR_PARTS)
    low, full = jnp.bfloat16, jnp.float32
    vmem = pl.BlockSpec(memory_space=pltpu.VMEM)
    anywhere = pl.BlockSpec(memory_space=pl.ANY)
    dma = pltpu.SemaphoreType.DMA
    weights, predicted = pl.pallas_call(
        functools.partial(plane_kernel, cap),
        out_shape=(pltpu.VMEM((rows_v, columns), low), pltpu.VMEM((tests // 4, columns), low)),
        in_specs=[anywhere] * 8,
        out_specs=(vmem, vmem),
        scratch_shapes=[
            pltpu.SMEM(live.shape, live.dtype),
            pltpu.SMEM(lam_index.shape, lam_index.dtype),
            pltpu.SMEM(lambdas.shape, lambdas.dtype),
            pltpu.VMEM((1, features), full),
            pltpu.VMEM((time_rows, columns), low),
            pltpu.VMEM((time_rows, features), low),
            pltpu.VMEM((tests, rows_v), low),
            pltpu.VMEM((2, rows_v, 4 * depth), low),
            pltpu.VMEM((2, 2, 2, BLK, share), low),
            pltpu.VMEM((2, 2, 2, BLK, share), low),
            pltpu.VMEM((2, 2, 2, BLK, share), full),
            pltpu.VMEM((2, 2, BLK, share), low),
            pltpu.VMEM((2, 2, BLK, share), low),
            pltpu.VMEM((2, 4 * share, used), low),
            pltpu.VMEM((4 * share, used), low),
            pltpu.VMEM((rows_v, used), full),
            pltpu.VMEM((tests, used), full),
            pltpu.VMEM((rows_v, used), low),
            pltpu.VMEM((rows_v, used), low),
            pltpu.VMEM((3, tests // 4, used), low),
            pltpu.VMEM((2, tests // 4, used), low),
            pltpu.VMEM((tests // 4, used), low),
            pltpu.VMEM((rows_v, used), low),
            dma((6,)),
            dma((5,)),
            dma,
            dma((4,)),
            dma((len(SIDE_PARTS),)),
            dma,
            dma((count,)),
            dma((4,)),
            dma((3,)),
            dma((count,)),
            dma,
            dma((2, 2)),
            dma,
            dma((2,)),
            dma,
            dma((2,)),
            dma,
            dma((2,)),
            dma,
            dma,
            dma,
            dma((3,)),
            dma,
            dma,
            dma((2,)),
            pltpu.SemaphoreType.REGULAR,
            pltpu.SemaphoreType.REGULAR,
        ],
        compiler_params=pltpu.CompilerParams(
            collective_id=1, has_side_effects=True
        ),
    )(live, lam_index, lambdas, sing.reshape(1, features), y_train, u_train, v_basis, x_test)
    weights = pltpu.with_memory_space_constraint(weights, pltpu.VMEM)
    predicted = pltpu.with_memory_space_constraint(predicted, pltpu.VMEM)
    return pl.pallas_call(
        put_out,
        out_shape=(
            jax.ShapeDtypeStruct((rows_v, columns), low),
            jax.ShapeDtypeStruct((tests // 4, columns), low),
        ),
        in_specs=[anywhere, anywhere],
        out_specs=(anywhere, anywhere),
        scratch_shapes=[dma((2,))],
    )(weights, predicted)


def routed(n_t, n_v, *args):
    if (n_t, n_v, args[4].shape[0]) == (4, 8, 3):
        return plane_body(*args)
    return body(n_t, n_v, *args)


def solution(mesh):
    placed = (
        P("tm", None),
        P("tm", "vox"),
        P(),
        P(),
        P("vox"),
        P("vox"),
        P("tm", "vox"),
        P(None, "tm"),
    )
    return jax.shard_map(
        functools.partial(routed, mesh.shape["tm"], mesh.shape["vox"]),
        mesh=mesh,
        in_specs=placed,
        out_specs=(P("tm", "vox"), P("tm", "vox")),
        check_vma=False,
    )
```
